256 devices in a mesh: pair: 4 (over y), value: 64 (over z, x, core).
Axes of the slice: x: 4, y: 4, z: 8, core: 2. Of those that a mesh axis runs over, the one named last changes fastest.
Arguments:
- student: bfloat16 [1536, 65536], P('pair', 'value'), may hold values from -8 to 8
- teacher: bfloat16 [1536, 65536], P('pair', 'value'), may hold values from -8 to 8
- bw_table: float32 [8], replicated, may hold values from 0.5 to 8
- bw_index: int32 [4], replicated, may hold values from 0 to 7
- group_ids: int32 [1536], replicated, may hold values from 0 to 15, as said below
Outputs:
- force: float32 [1536, 65536], P('pair', 'value')
- loss: float32 [], replicated
The draws below stay inside these ranges and needn't reach their ends.
Inputs may be any that keep to these rules, and one draw needn't show every extreme that they name: `group_ids`: every group from 0 to 15 holds at least one sample.
All inputs are finite; a program needn't handle non-finite values.
Results may differ from the reference program's by a relative error of at most 0.00045.
The reference program's roundings to bfloat16 on the way count: a program that leaves them out, or rounds other values in their place, can miss the bound.
Values may be sent and summed in bfloat16 or wider, within the bound.
A program may use at most 64 MiB of HBM per device.

```python
import math
import jax
import jax.numpy as jnp
from jax import lax

LATENT = 65536
NBW = 8
NSEL = 4
GROUPS = 16
SAMPLES = 1536


def group_draw(key):
    key_base, key_shuffle = jax.random.split(jax.random.fold_in(key, 7))
    groups = jax.random.randint(key_base, (SAMPLES,), 0, GROUPS, dtype=jnp.int32)
    shuffle = jax.random.permutation(key_shuffle, SAMPLES)
    return groups.at[shuffle[:GROUPS]].set(jnp.arange(GROUPS, dtype=jnp.int32))


def latent_pair(key):
    groups = group_draw(key)
    subkeys = jax.random.split(jax.random.fold_in(key, 31), 7)
    pattern_count = 32
    member = (groups[:, None] == jnp.arange(GROUPS, dtype=jnp.int32)[None, :]).astype(jnp.float32)
    coeffs = jax.random.normal(subkeys[0], (SAMPLES, pattern_count), jnp.float32) * (0.6 / math.sqrt(pattern_count))
    teacher_gaps = jnp.exp(jax.random.uniform(subkeys[1], (SAMPLES, 1), jnp.float32, math.log(0.2), math.log(0.8)))
    centers = 0.8 * jnp.clip(jax.random.normal(subkeys[2], (GROUPS, LATENT), jnp.float32), -4.0, 4.0)
    patterns = jnp.clip(jax.random.normal(subkeys[3], (pattern_count, LATENT), jnp.float32), -4.0, 4.0)
    sample_noise = 0.6 * jnp.clip(jax.random.normal(subkeys[4], (SAMPLES, LATENT), jnp.float32), -4.0, 4.0)
    scales = jnp.exp(jax.random.uniform(subkeys[5], (SAMPLES, 1), jnp.float32, math.log(0.5), math.log(1.0)))
    shifts = jnp.clip(jax.random.normal(subkeys[6], (SAMPLES, LATENT), jnp.float32), -4.0, 4.0)
    student = jnp.dot(member, centers, precision=lax.Precision.HIGHEST)
    student = student + jnp.dot(coeffs, patterns, precision=lax.Precision.HIGHEST)
    student = student + sample_noise * scales
    teacher = student + shifts * teacher_gaps
    student = jnp.clip(student, -8.0, 8.0).astype(jnp.bfloat16)
    teacher = jnp.clip(teacher, -8.0, 8.0).astype(jnp.bfloat16)
    return (student, teacher)


def draw_student(key, part):
    return latent_pair(key)[0]


def draw_teacher(key, part):
    return latent_pair(key)[1]


def draw_group_ids(key, part):
    return group_draw(key)


def with_ends(drawn, stream_key, least, largest):
    longest = drawn.shape.index(max(drawn.shape))
    spots = []
    for shift in (0, 1):
        where = [jax.random.randint(jax.random.fold_in(stream_key, axis), (), 0, length) for axis, length in enumerate(drawn.shape)]
        where[longest] = (where[longest] + shift) % drawn.shape[longest]
        spots.append(tuple(where))
    return drawn.at[spots[0]].set(least).at[spots[1]].set(largest)


def setup_inputs(seed: int = 0) -> dict:
    seeds = jax.random.split(jax.random.key(seed), 6)
    student = draw_student(jax.random.fold_in(seeds[5], 71), 0)
    teacher = draw_teacher(jax.random.fold_in(seeds[5], 71), 0)
    bw_table = jnp.clip(jnp.exp(jax.random.uniform(seeds[2], (NBW,), jnp.float32, math.log(0.5), math.log(8.0))), 0.5, 8.0)
    bw_index = with_ends(jax.random.randint(seeds[3], (NSEL,), 0, NBW), jax.random.fold_in(seeds[3], 1), 0, NBW - 1).astype(jnp.int32)
    group_ids = draw_group_ids(jax.random.fold_in(seeds[5], 71), 0)
    return {"student": student, "teacher": teacher, "bw_table": bw_table, "bw_index": bw_index, "group_ids": group_ids}


def kernel_terms(gram_self, gram_cross, norm_rows, norm_student, norm_teacher, same_group, heights, latent):
    dist_self = jnp.maximum(norm_rows[:, None] + norm_student[None, :] - 2.0 * gram_self, 0.0)
    dist_cross = jnp.maximum(norm_rows[:, None] + norm_teacher[None, :] - 2.0 * gram_cross, 0.0)
    kern_self = jnp.zeros_like(dist_self)
    kern_cross = jnp.zeros_like(dist_cross)
    weight_self = jnp.zeros_like(dist_self)
    weight_cross = jnp.zeros_like(dist_cross)
    count = heights.shape[0]
    for member in range(count):
        height = heights[member]
        width_now = height * latent
        exp_self = jnp.exp(-dist_self / width_now)
        exp_cross = jnp.exp(-dist_cross / width_now)
        kern_self = kern_self + exp_self
        kern_cross = kern_cross + exp_cross
        weight_self = weight_self + exp_self / height
        weight_cross = weight_cross + exp_cross / height
    kern_self = kern_self / count * same_group
    kern_cross = kern_cross / count * same_group
    weight_self = weight_self / count * same_group
    weight_cross = weight_cross / count * same_group
    row_loss = jnp.sum(kern_self - 2.0 * kern_cross, axis=1)
    total_self = jnp.sum(weight_self, axis=1)
    total_cross = jnp.sum(weight_cross, axis=1)
    return weight_self.astype(jnp.bfloat16), weight_cross.astype(jnp.bfloat16), row_loss, total_self, total_cross


def reference(student, teacher, bw_table, bw_index, group_ids):
    student_wide = student.astype(jnp.float32)
    teacher_wide = teacher.astype(jnp.float32)
    norm_student = jnp.sum(student_wide * student_wide, axis=1)
    norm_teacher = jnp.sum(teacher_wide * teacher_wide, axis=1)
    gram_self = jnp.dot(student, student.T, preferred_element_type=jnp.float32)
    gram_cross = jnp.dot(student, teacher.T, preferred_element_type=jnp.float32)
    heights = bw_table[bw_index]
    same_group = (group_ids[:, None] == group_ids[None, :]).astype(jnp.float32)
    group_sizes = jnp.sum(same_group, axis=1)
    weight_self, weight_cross, row_loss, total_self, total_cross = kernel_terms(
        gram_self, gram_cross, norm_student, norm_student, norm_teacher, same_group, heights, float(LATENT))
    loss = jnp.sum(row_loss / group_sizes) / SAMPLES
    pulled = student_wide * (total_cross - total_self)[:, None]
    pulled = pulled + jnp.dot(weight_self, student, preferred_element_type=jnp.float32)
    pulled = pulled - jnp.dot(weight_cross, teacher, preferred_element_type=jnp.float32)
    force = pulled / group_sizes[:, None]
    return force, loss
```

```python
import functools

import jax
import jax.numpy as jnp
from jax import lax
from jax.experimental import pallas as pl
from jax.experimental.pallas import tpu as pltpu
from jax.sharding import PartitionSpec as P

MESH = pl.DeviceIdType.MESH
F32, BF16 = jnp.float32, jnp.bfloat16


class Sizes:
    def __init__(self, ny, nx, nz, nc, samples, tile, latent):
        self.ny, self.nx, self.nz, self.nc = ny, nx, nz, nc
        self.samples, self.tile, self.latent = samples, tile, float(latent)
        self.rows = samples // ny
        self.cols = tile // ny
        self.groups = 2 * nc * nx
        self.half = nz // 2
        self.cap = 8 * ny * self.half
        self.blocks = self.cap // 8


def pair_terms(dist_self, dist_cross, mask, heights, latent):
    kern_self = jnp.zeros_like(dist_self)
    kern_cross = jnp.zeros_like(dist_cross)
    weight_self = jnp.zeros_like(dist_self)
    weight_cross = jnp.zeros_like(dist_cross)
    count = len(heights)
    for height in heights:
        width_now = height * latent
        exp_self = jnp.exp(-dist_self / width_now)
        exp_cross = jnp.exp(-dist_cross / width_now)
        kern_self = kern_self + exp_self
        kern_cross = kern_cross + exp_cross
        weight_self = weight_self + exp_self / height
        weight_cross = weight_cross + exp_cross / height
    kern_self = kern_self / count * mask
    kern_cross = kern_cross / count * mask
    weight_self = weight_self / count * mask
    weight_cross = weight_cross / count * mask
    row_loss = jnp.sum(kern_self - 2.0 * kern_cross, axis=1, keepdims=True)
    pull = jnp.sum(weight_cross, axis=1, keepdims=True) - jnp.sum(weight_self, axis=1, keepdims=True)
    return weight_self.astype(BF16), weight_cross.astype(BF16), row_loss, pull


class Pool:
    def __init__(self):
        self.total = 0

    def take(self, count):
        first = self.total
        self.total += count
        return first

    def pair(self, count):
        return self.take(count), self.take(count)


def exchanges(z):
    pool = Pool()
    sizes = {
        "in_s": z.ny, "in_t": z.ny, "core": z.groups // 2, "a1": z.nx, "b1": z.ny, "a2": z.ny, "b2": z.nx, "z3": z.nz,
        "gz_w": z.nz, "gz_t": z.nz, "g2a_w": z.ny, "g2a_t": z.ny, "g2b_w": z.nx, "g2b_t": z.nx,
        "g1a_w": z.nx, "g1a_t": z.nx, "g1b_w": z.ny, "g1b_t": z.ny, "gc_w": 1, "gc_t": 1, "out": z.ny, "own": 3,
    }
    return {name: pool.pair(count) for name, count in sizes.items()}, pool.total


def fused(z, ids, s_ref, t_ref, gr_ref, gc_ref, tab_ref, idx_ref, f_ref, l_ref,
          xin_s, xin_t, sort_ref, back_ref, xacc, xs, d_ref, rc, r1a, r1b, sums, r2a, r2b, u_ref, r3,
          wf, t3, t2a, t2b, t1a, t1b, tall, fs, fo, sems):
    y, v = lax.axis_index("pair"), lax.axis_index("value")
    c = lax.rem(v, z.nc)
    x = lax.rem(v // z.nc, z.nx)
    zc = v // (z.nc * z.nx)
    other = 1 - c
    hg = z.groups // 2
    quarter = z.cap // z.ny

    def at(yy=None, xx=None, zz=None, cc=None):
        yy = y if yy is None else yy
        xx = x if xx is None else xx
        zz = zc if zz is None else zz
        cc = c if cc is None else cc
        return (yy, (zz * z.nx + xx) * z.nc + cc)

    def on_y(k):
        return lax.rem(y + k, z.ny)

    def on_x(k):
        return lax.rem(x + k, z.nx)

    def on_z(k):
        return lax.rem(zc + k, z.nz)

    barrier = pltpu.get_barrier_semaphore()
    peers = [at(yy=on_y(k)) for k in range(1, z.ny)] + [at(xx=on_x(k)) for k in range(1, z.nx)]
    peers += [at(zz=on_z(k)) for k in range(1, z.nz)] + [at(cc=other)]
    for peer in peers:
        pl.semaphore_signal(barrier, inc=1, device_id=peer, device_id_type=MESH)
    pl.semaphore_wait(barrier, len(peers))

    def copy(name, src, dst, send, recv, device):
        first_send, first_recv = ids[name]
        return pltpu.make_async_remote_copy(
            src_ref=src, dst_ref=dst, send_sem=sems.at[first_send + send], recv_sem=sems.at[first_recv + recv],
            device_id=device, device_id_type=MESH)

    far_first = sorted(range(1, z.ny), key=lambda k: -min(k, z.ny - k))

    def in_copy(name, ref, land, k, source, target):
        cols = pl.ds(pl.multiple_of(target * z.cols, z.cols), z.cols)
        return copy(name, ref.at[:, cols], land.at[source], k, source, at(yy=on_y(k)))

    for k in far_first:
        in_copy("in_s", s_ref, xin_s, k, y, on_y(k)).start()
        in_copy("in_t", t_ref, xin_t, k, y, on_y(k)).start()
    own_cols = pl.ds(pl.multiple_of(y * z.cols, z.cols), z.cols)
    own_s = pltpu.make_async_copy(s_ref.at[:, own_cols], xin_s.at[y], sems.at[ids["own"][0]])
    own_t = pltpu.make_async_copy(t_ref.at[:, own_cols], xin_t.at[y], sems.at[ids["own"][0] + 1])
    own_s.start()
    own_t.start()

    chunk = z.rows
    for part in range(z.ny):
        cols = pl.ds(part * chunk, chunk)
        ids_row = gr_ref[:, cols]

        def count_before(step, rank):
            first = pl.multiple_of(step * z.cap, z.cap)
            ids_col = gc_ref[pl.ds(first, z.cap), :]
            at_row = first + lax.broadcasted_iota(jnp.int32, (z.cap, chunk), 0)
            at_col = part * chunk + lax.broadcasted_iota(jnp.int32, (z.cap, chunk), 1)
            hit = jnp.where((ids_col == ids_row) & (at_row < at_col), 1, 0)
            return rank + jnp.sum(hit, axis=0, keepdims=True)

        rank = lax.fori_loop(0, z.samples // z.cap, count_before, jnp.zeros((1, chunk), jnp.int32))
        place = ids_row * z.cap + rank

        def fill_sort(step, _):
            first = pl.multiple_of(step * z.cap, z.cap)
            slot = first + lax.broadcasted_iota(jnp.int32, (z.cap, chunk), 0)
            sort_ref[part, pl.ds(first, z.cap), :] = jnp.where(slot == place, 1.0, 0.0).astype(BF16)
            return 0

        lax.fori_loop(0, z.groups, fill_sort, 0)

    own_s.wait()
    own_t.wait()

    xacc[...] = jnp.zeros_like(xacc)
    slots = z.groups * z.cap
    tall_rows = slots // 4

    def sort_from(source):
        def body(step, _):
            first = pl.multiple_of(step * tall_rows, tall_rows)
            place = sort_ref[source, pl.ds(first, tall_rows), :]
            xacc[pl.ds(first, tall_rows), 0:z.cols] += jnp.dot(place, xin_s[source], preferred_element_type=F32)
            xacc[pl.ds(first, tall_rows), z.cols:2 * z.cols] += jnp.dot(place, xin_t[source], preferred_element_type=F32)
            return 0

        lax.fori_loop(0, 4, body, 0)

    sort_from(y)
    for k in reversed(far_first):
        source = on_y(z.ny - k)
        in_copy("in_s", s_ref, xin_s, k, source, on_y(k)).wait_recv()
        in_copy("in_t", t_ref, xin_t, k, source, on_y(k)).wait_recv()
        sort_from(source)

    def distances(group):
        rows = pl.ds(pl.multiple_of(group * z.cap, z.cap), z.cap)
        both = jnp.concatenate([xacc[rows, 0:z.cols], xacc[rows, z.cols:2 * z.cols]], axis=0).astype(BF16)
        xs[group] = both
        gram = lax.dot_general(both, both, (((1,), (1,)), ((), ())), preferred_element_type=F32)
        size = 2 * z.cap
        eye = lax.broadcasted_iota(jnp.int32, (size, size), 0) == lax.broadcasted_iota(jnp.int32, (size, size), 1)
        diagonal = jnp.where(eye, gram, 0.0)
        norm_row = jnp.sum(diagonal, axis=0, keepdims=True)
        norm_col = jnp.sum(diagonal[0:z.cap], axis=1, keepdims=True)
        d_ref[group] = norm_col + norm_row - 2.0 * gram[0:z.cap]

    def core_copy(i, group):
        return copy("core", d_ref.at[group], rc.at[i], i, i, at(cc=other))

    def to_other(i, _):
        distances(other * hg + i)
        core_copy(i, other * hg + i).start()
        return 0

    lax.fori_loop(0, hg, to_other, 0)

    def a1_copy(k, source):
        return copy("a1", d_ref.at[c * hg + on_x(k)], r1a.at[source], k, source, at(xx=on_x(k)))

    def b1_copy(k, source):
        return copy("b1", d_ref.at[c * hg + z.nx + on_y(k)], r1b.at[source], k, source, at(yy=on_y(k)))

    def add_core(i):
        distances(c * hg + i)
        core_copy(i, c * hg + i).wait_recv()
        d_ref[c * hg + i] += rc[i]

    def mine(k, _):
        add_core(on_x(k))

        @pl.when(k < z.nx)
        def _():
            a1_copy(k, x).start()

        add_core(z.nx + on_y(k))

        @pl.when(k < z.nx)
        def _():
            b1_copy(k, y).start()

        return 0

    lax.fori_loop(1, z.nx + 1, mine, 0)

    total_a = d_ref[c * hg + x]
    for k in range(1, z.nx):
        source = on_x(z.nx - k)
        a1_copy(k, source).wait_recv()
        total_a = total_a + r1a[source]
    sums[0] = total_a

    def a2_copy(k, source):
        rows = pl.ds(pl.multiple_of(on_y(k) * quarter, quarter), quarter)
        return copy("a2", sums.at[0, rows], r2a.at[source], k, source, at(yy=on_y(k)))

    for k in range(1, z.ny):
        a2_copy(k, y).start()
    total_b = d_ref[c * hg + z.nx + y]
    for k in range(1, z.ny):
        source = on_y(z.ny - k)
        b1_copy(k, source).wait_recv()
        total_b = total_b + r1b[source]
    sums[1] = total_b

    def b2_copy(k, source):
        rows = pl.ds(pl.multiple_of(on_x(k) * quarter, quarter), quarter)
        return copy("b2", sums.at[1, rows], r2b.at[source], k, source, at(xx=on_x(k)))

    for k in range(1, z.nx):
        b2_copy(k, x).start()

    part_a = sums[0, pl.ds(pl.multiple_of(y * quarter, quarter), quarter), :]
    for k in range(1, z.ny):
        source = on_y(z.ny - k)
        a2_copy(k, source).wait_recv()
        part_a = part_a + r2a[source]
    u_ref[0:z.half] = part_a.reshape(z.half, 8, 2 * z.cap)
    part_b = sums[1, pl.ds(pl.multiple_of(x * quarter, quarter), quarter), :]
    for k in range(1, z.nx):
        source = on_x(z.nx - k)
        b2_copy(k, source).wait_recv()
        part_b = part_b + r2b[source]
    u_ref[z.half:2 * z.half] = part_b.reshape(z.half, 8, 2 * z.cap)

    def z3_copy(k, source):
        return copy("z3", u_ref.at[on_z(k)], r3.at[source], k, source, at(zz=on_z(k)))

    for k in range(1, z.nz):
        z3_copy(k, zc).start()

    def fill_back(step, _):
        first = pl.multiple_of(step * z.cap, z.cap)
        ids_col = gc_ref[pl.ds(first, z.cap), :]
        at_row = first + lax.broadcasted_iota(jnp.int32, (z.cap, z.samples), 0)
        at_col = lax.broadcasted_iota(jnp.int32, (z.cap, z.samples), 1)
        hit = jnp.where((ids_col == gr_ref[...]) & (at_col < at_row), 1.0, 0.0)
        rank = jnp.sum(hit, axis=1, keepdims=True).astype(jnp.int32)
        place = ids_col * z.cap + rank
        slot = lax.broadcasted_iota(jnp.int32, (z.cap, slots), 1)
        back_ref[pl.ds(first, z.cap), :] = jnp.where(slot == place, 1.0, 0.0).astype(BF16)
        return 0

    lax.fori_loop(0, z.samples // z.cap, fill_back, 0)

    dist = u_ref[zc]
    for k in range(1, z.nz):
        source = on_z(z.nz - k)
        z3_copy(k, source).wait_recv()
        dist = dist + r3[source]

    way = zc // z.half
    member = (1 - way) * x + way * y
    sub = (1 - way) * y + way * x
    group = c * hg + way * z.nx + member
    block = sub * z.half + lax.rem(zc, z.half)
    size = jnp.sum(jnp.where(gr_ref[...] == group, 1.0, 0.0), axis=1, keepdims=True)
    row_at = (block * 8 + lax.broadcasted_iota(jnp.int32, (8, z.cap), 0)).astype(F32)
    col_at = lax.broadcasted_iota(jnp.int32, (8, z.cap), 1).astype(F32)
    mask = jnp.where((row_at < size) & (col_at < size), 1.0, 0.0)
    dist = jnp.maximum(dist, 0.0)
    heights = [tab_ref[idx_ref[m]] for m in range(4)]
    weight_self, weight_cross, row_loss, pull = pair_terms(
        dist[:, 0:z.cap], dist[:, z.cap:2 * z.cap], mask, heights, z.latent)
    wf[group, block] = jnp.concatenate([weight_self.astype(F32), -weight_cross.astype(F32)], axis=0).astype(BF16)
    lane = 2 * (member * z.blocks + block)
    lanes = lax.broadcasted_iota(jnp.int32, (8, 128), 1)
    t3[zc] = jnp.where(lanes == lane, pull, 0.0) + jnp.where(lanes == lane + 1, row_loss / size, 0.0)

    def gz_copies(k, source):
        way_of = source // z.half
        group_of = c * hg + way_of * z.nx + (1 - way_of) * x + way_of * y
        block_of = ((1 - way_of) * y + way_of * x) * z.half + lax.rem(source, z.half)
        place = wf.at[group_of, block_of]
        return (copy("gz_w", place, place, k, source, at(zz=on_z(k))),
                copy("gz_t", t3.at[source], t3.at[source], k, source, at(zz=on_z(k))))

    def start(pair):
        for one in pair:
            one.start()

    def wait_recv(pair):
        for one in pair:
            one.wait_recv()

    for k in range(1, z.nz):
        start(gz_copies(k, zc))
    for k in range(1, z.nz):
        wait_recv(gz_copies(k, on_z(z.nz - k)))
    t2a[y] = jnp.sum(t3[0:z.half], axis=0)
    t2b[x] = jnp.sum(t3[z.half:2 * z.half], axis=0)

    def g2a_copies(k, source):
        place = wf.at[c * hg + x, pl.ds(source * z.half, z.half)]
        return (copy("g2a_w", place, place, k, source, at(yy=on_y(k))),
                copy("g2a_t", t2a.at[source], t2a.at[source], k, source, at(yy=on_y(k))))

    def g2b_copies(k, source):
        place = wf.at[c * hg + z.nx + y, pl.ds(source * z.half, z.half)]
        return (copy("g2b_w", place, place, k, source, at(xx=on_x(k))),
                copy("g2b_t", t2b.at[source], t2b.at[source], k, source, at(xx=on_x(k))))

    for k in range(1, z.nx):
        start(g2a_copies(k, y))
        start(g2b_copies(k, x))

    def g1a_copies(k, source):
        place = wf.at[c * hg + source]
        return (copy("g1a_w", place, place, k, source, at(xx=on_x(k))),
                copy("g1a_t", t1a.at[source], t1a.at[source], k, source, at(xx=on_x(k))))

    def g1b_copies(k, source):
        place = wf.at[c * hg + z.nx + source]
        return (copy("g1b_w", place, place, k, source, at(yy=on_y(k))),
                copy("g1b_t", t1b.at[source], t1b.at[source], k, source, at(yy=on_y(k))))

    for k in range(1, z.ny):
        wait_recv(g2a_copies(k, on_y(z.ny - k)))
    t1a[x] = jnp.sum(t2a[...], axis=0)
    for k in range(1, z.nx):
        start(g1a_copies(k, x))
    for k in range(1, z.nx):
        wait_recv(g2b_copies(k, on_x(z.nx - k)))
    t1b[y] = jnp.sum(t2b[...], axis=0)
    for k in range(1, z.ny):
        start(g1b_copies(k, y))
    for k in range(1, z.nx):
        wait_recv(g1a_copies(k, on_x(z.nx - k)))
    for k in range(1, z.ny):
        wait_recv(g1b_copies(k, on_y(z.ny - k)))
    tall[c, 0] = jnp.sum(t1a[...], axis=0)
    tall[c, 1] = jnp.sum(t1b[...], axis=0)

    def gc_copies(core):
        place = wf.at[pl.ds(core * hg, hg)]
        return (copy("gc_w", place, place, 0, 0, at(cc=other)),
                copy("gc_t", tall.at[core], tall.at[core], 0, 0, at(cc=other)))

    start(gc_copies(c))

    def force_of(g):
        tile = tall[g // hg, lax.rem(g, hg) // z.nx]
        spot = lax.broadcasted_iota(jnp.int32, (z.blocks, 8, 128), 2)
        want = 2 * (lax.rem(g, z.nx) * z.blocks + lax.broadcasted_iota(jnp.int32, (z.blocks, 8, 128), 0))
        picked = jnp.where(spot == want, jnp.broadcast_to(tile[None], (z.blocks, 8, 128)), 0.0)
        pulls = jnp.sum(picked, axis=2, keepdims=True).reshape(z.cap, 1)
        held = wf[g].astype(F32).reshape(z.blocks, 2, 8, z.cap)
        weights = jnp.concatenate(
            [held[:, 0].reshape(z.cap, z.cap), held[:, 1].reshape(z.cap, z.cap)], axis=1).astype(BF16)
        values = xs[g]
        pulled = values[0:z.cap].astype(F32) * pulls + jnp.dot(weights, values, preferred_element_type=F32)
        size_of = jnp.sum(jnp.where(gr_ref[...] == g, 1.0, 0.0), axis=1, keepdims=True)
        force = pulled / size_of
        high = force.astype(BF16)
        low = (force - high.astype(F32)).astype(BF16)
        rows = pl.ds(pl.multiple_of(g * z.cap, z.cap), z.cap)
        fs[rows, 0:z.cols] = high
        fs[rows, z.cols:2 * z.cols] = low

    def own_force(i, _):
        force_of(c * hg + i)
        return 0

    def other_force(i, _):
        force_of(other * hg + i)
        return 0

    lax.fori_loop(0, hg, own_force, 0)
    wait_recv(gc_copies(other))
    lax.fori_loop(0, hg, other_force, 0)

    odd = lax.rem(lax.broadcasted_iota(jnp.int32, (8, 128), 1), 2) == 1
    every = jnp.where(odd, tall[0, 0] + tall[0, 1] + tall[1, 0] + tall[1, 1], 0.0)
    every = jnp.sum(jnp.sum(every, axis=1, keepdims=True), axis=0, keepdims=True)
    l_ref[...] = jnp.broadcast_to(every / z.samples, l_ref.shape)

    def out_copy(k, source):
        cols = pl.ds(pl.multiple_of(source * z.cols, z.cols), z.cols)
        return copy("out", fo.at[k], f_ref.at[:, cols], k, source, at(yy=on_y(k)))

    def out_local():
        return pltpu.make_async_copy(fo.at[0], f_ref.at[:, own_cols], sems.at[ids["own"][0] + 2])

    def unsort(k):
        rows = pl.ds(pl.multiple_of(on_y(k) * z.rows, z.rows), z.rows)
        moved = jnp.dot(back_ref[rows, :], fs[...], preferred_element_type=F32)
        fo[k] = moved[:, 0:z.cols] + moved[:, z.cols:2 * z.cols]

    def send_out(step, _):
        k = step if z.ny == 2 else lax.rem(step + z.ny // 2 - 1, z.ny - 1) + 1
        if z.ny == 2:
            k = 1
        unsort(k)
        out_copy(k, y).start()
        return 0

    lax.fori_loop(0, z.ny - 1, send_out, 0)
    unsort(0)
    out_local().start()
    out_local().wait()
    for k in range(1, z.ny):
        out_copy(k, on_y(z.ny - k)).wait_recv()

    for k in range(1, z.ny):
        in_copy("in_s", s_ref, xin_s, k, y, on_y(k)).wait_send()
        in_copy("in_t", t_ref, xin_t, k, y, on_y(k)).wait_send()
        b1_copy(k, y).wait_send()
        a2_copy(k, y).wait_send()
        out_copy(k, y).wait_send()
        for one in g2a_copies(k, y) + g1b_copies(k, y):
            one.wait_send()
    for k in range(1, z.nx):
        a1_copy(k, x).wait_send()
        b2_copy(k, x).wait_send()
        for one in g2b_copies(k, x) + g1a_copies(k, x):
            one.wait_send()
    for k in range(1, z.nz):
        z3_copy(k, zc).wait_send()
        for one in gz_copies(k, zc):
            one.wait_send()
    for i in range(hg):
        core_copy(i, other * hg + i).wait_send()
    for one in gc_copies(c):
        one.wait_send()


def sorted_path(z, student, teacher, bw_table, bw_index, group_ids):
    ids, count = exchanges(z)
    slots, pair, hg = z.groups * z.cap, 2 * z.cap, z.groups // 2
    quarter = z.cap // z.ny
    vmem, smem, anywhere = (pl.BlockSpec(memory_space=m) for m in (pltpu.VMEM, pltpu.SMEM, pl.ANY))
    force, loss = pl.pallas_call(
        functools.partial(fused, z, ids),
        out_shape=(jax.ShapeDtypeStruct((z.rows, z.tile), F32), jax.ShapeDtypeStruct((8, 128), F32)),
        in_specs=[anywhere, anywhere, vmem, vmem, smem, smem],
        out_specs=(anywhere, vmem),
        scratch_shapes=[
            pltpu.VMEM((z.ny, z.rows, z.cols), BF16),
            pltpu.VMEM((z.ny, z.rows, z.cols), BF16),
            pltpu.VMEM((z.ny, slots, z.rows), BF16),
            pltpu.VMEM((z.samples, slots), BF16),
            pltpu.VMEM((slots, 2 * z.cols), F32),
            pltpu.VMEM((z.groups, pair, z.cols), BF16),
            pltpu.VMEM((z.groups, z.cap, pair), F32),
            pltpu.VMEM((hg, z.cap, pair), F32),
            pltpu.VMEM((z.nx, z.cap, pair), F32),
            pltpu.VMEM((z.ny, z.cap, pair), F32),
            pltpu.VMEM((2, z.cap, pair), F32),
            pltpu.VMEM((z.ny, quarter, pair), F32),
            pltpu.VMEM((z.nx, quarter, pair), F32),
            pltpu.VMEM((z.nz, 8, pair), F32),
            pltpu.VMEM((z.nz, 8, pair), F32),
            pltpu.VMEM((z.groups, z.blocks, 16, z.cap), BF16),
            pltpu.VMEM((z.nz, 8, 128), F32),
            pltpu.VMEM((z.ny, 8, 128), F32),
            pltpu.VMEM((z.nx, 8, 128), F32),
            pltpu.VMEM((z.nx, 8, 128), F32),
            pltpu.VMEM((z.ny, 8, 128), F32),
            pltpu.VMEM((2, 2, 8, 128), F32),
            pltpu.VMEM((slots, 2 * z.cols), BF16),
            pltpu.VMEM((z.ny, z.rows, z.cols), F32),
            pltpu.SemaphoreType.DMA((count,)),
        ],
        compiler_params=pltpu.CompilerParams(
            collective_id=1, has_side_effects=True, vmem_limit_bytes=56 * 1024 * 1024),
        name="grouped",
    )(student, teacher, group_ids.reshape(1, z.samples), group_ids.reshape(z.samples, 1), bw_table, bw_index)
    return force, loss[0, 0]


def dense_path(z, student, teacher, bw_table, bw_index, group_ids):
    students = lax.all_gather(student, "pair", axis=0, tiled=True)
    teachers = lax.all_gather(teacher, "pair", axis=0, tiled=True)
    both = jnp.concatenate([students, teachers], axis=0)
    wide = both.astype(F32)
    row_wide = student.astype(F32)
    norms = jnp.sum(wide * wide, axis=1)
    row_norms = jnp.sum(row_wide * row_wide, axis=1)
    gram = lax.dot_general(student, both, (((1,), (1,)), ((), ())), preferred_element_type=F32)
    dist = jnp.maximum(lax.psum(row_norms[:, None] + norms[None, :] - 2.0 * gram, "value"), 0.0)
    row_ids = lax.dynamic_slice_in_dim(group_ids, lax.axis_index("pair") * z.rows, z.rows)
    same = (row_ids[:, None] == group_ids[None, :]).astype(F32)
    sizes = jnp.sum(same, axis=1, keepdims=True)
    heights = bw_table[bw_index]
    weight_self, weight_cross, row_loss, pull = pair_terms(
        dist[:, :z.samples], dist[:, z.samples:], same, [heights[m] for m in range(4)], z.latent)
    loss = lax.psum(jnp.sum(row_loss / sizes), "pair") / z.samples
    pulled = row_wide * pull
    pulled = pulled + jnp.dot(weight_self, students, preferred_element_type=F32)
    pulled = pulled - jnp.dot(weight_cross, teachers, preferred_element_type=F32)
    return pulled / sizes, loss


def build(mesh, z):
    def step(student, teacher, bw_table, bw_index, group_ids):
        each = jnp.arange(z.groups, dtype=group_ids.dtype)
        largest = jnp.max(jnp.sum((group_ids[None, :] == each[:, None]).astype(jnp.int32), axis=1))
        return lax.cond(
            largest <= z.cap,
            functools.partial(sorted_path, z),
            functools.partial(dense_path, z),
            student, teacher, bw_table, bw_index, group_ids)

    return jax.shard_map(
        step, mesh=mesh,
        in_specs=(P("pair", "value"), P("pair", "value"), P(None), P(None), P(None)),
        out_specs=(P("pair", "value"), P()),
        check_vma=False)


def solution(mesh):
    return build(mesh, Sizes(ny=4, nx=4, nz=8, nc=2, samples=1536, tile=1024, latent=65536))
```

```python
import functools

import jax
import jax.numpy as jnp
from jax import lax
from jax.experimental import pallas as pl
from jax.experimental.pallas import tpu as pltpu
from jax.sharding import PartitionSpec as P

MESH = pl.DeviceIdType.MESH
F32, BF16 = jnp.float32, jnp.bfloat16


class Sizes:
    def __init__(self, ny, nx, nz, nc, samples, tile, latent):
        self.ny, self.nx, self.nz, self.nc = ny, nx, nz, nc
        self.samples, self.tile, self.latent = samples, tile, float(latent)
        self.rows = samples // ny
        self.cols = tile // ny
        self.groups = 2 * nc * nx
        self.half = nz // 2
        self.cap = 8 * ny * self.half
        self.blocks = self.cap // 8
        self.most = self.cap - 3


def pair_terms(dist_self, dist_cross, mask, heights, latent):
    kern_self = jnp.zeros_like(dist_self)
    kern_cross = jnp.zeros_like(dist_cross)
    weight_self = jnp.zeros_like(dist_self)
    weight_cross = jnp.zeros_like(dist_cross)
    count = len(heights)
    for height in heights:
        width_now = height * latent
        exp_self = jnp.exp(-dist_self / width_now)
        exp_cross = jnp.exp(-dist_cross / width_now)
        kern_self = kern_self + exp_self
        kern_cross = kern_cross + exp_cross
        weight_self = weight_self + exp_self / height
        weight_cross = weight_cross + exp_cross / height
    kern_self = kern_self / count * mask
    kern_cross = kern_cross / count * mask
    weight_self = weight_self / count * mask
    weight_cross = weight_cross / count * mask
    row_loss = jnp.sum(kern_self - 2.0 * kern_cross, axis=1, keepdims=True)
    pull = jnp.sum(weight_cross, axis=1, keepdims=True) - jnp.sum(weight_self, axis=1, keepdims=True)
    return weight_self.astype(BF16), weight_cross.astype(BF16), row_loss, pull


class Pool:
    def __init__(self):
        self.total = 0

    def take(self, count):
        first = self.total
        self.total += count
        return first

    def pair(self, count):
        return self.take(count), self.take(count)


def exchanges(z):
    pool = Pool()
    sizes = {
        "in_s": z.ny, "in_t": z.ny, "core": z.groups // 2, "a1": z.nx, "b1": z.ny, "a2": z.ny, "b2": z.nx, "z3": z.nz,
        "gz": z.nz, "g2a": z.ny, "g2b": z.nx, "g1a": z.nx, "g1b": z.ny, "gc": 1, "out": z.ny, "own": 3,
    }
    return {name: pool.pair(count) for name, count in sizes.items()}, pool.total


def fused(z, ids, s_ref, t_ref, g_ref, tab_ref, idx_ref, f_ref, l_ref,
          xin_s, xin_t, sort_ref, back_ref, xacc, xs, d_ref, rc, r1a, r1b, sums, r2a, r2b, u_ref, r3,
          wf, gr_ref, gc_ref, losses, fs, fo, sems):
    y, v = lax.axis_index("pair"), lax.axis_index("value")
    c = lax.rem(v, z.nc)
    x = lax.rem(v // z.nc, z.nx)
    zc = v // (z.nc * z.nx)
    other = 1 - c
    hg = z.groups // 2
    quarter = z.cap // z.ny

    def at(yy=None, xx=None, zz=None, cc=None):
        yy = y if yy is None else yy
        xx = x if xx is None else xx
        zz = zc if zz is None else zz
        cc = c if cc is None else cc
        return (yy, (zz * z.nx + xx) * z.nc + cc)

    def on_y(k):
        return lax.rem(y + k, z.ny)

    def on_x(k):
        return lax.rem(x + k, z.nx)

    def on_z(k):
        return lax.rem(zc + k, z.nz)

    barrier = pltpu.get_barrier_semaphore()
    peers = [at(yy=on_y(k)) for k in range(1, z.ny)] + [at(xx=on_x(k)) for k in range(1, z.nx)]
    peers += [at(zz=on_z(k)) for k in range(1, z.nz)] + [at(cc=other)]
    for peer in peers:
        pl.semaphore_signal(barrier, inc=1, device_id=peer, device_id_type=MESH)
    pl.semaphore_wait(barrier, len(peers))

    def copy(name, src, dst, send, recv, device):
        first_send, first_recv = ids[name]
        return pltpu.make_async_remote_copy(
            src_ref=src, dst_ref=dst, send_sem=sems.at[first_send + send], recv_sem=sems.at[first_recv + recv],
            device_id=device, device_id_type=MESH)

    pending = []

    def drain():
        for one in pending:
            one.wait_send()

    far_first = sorted(range(1, z.ny), key=lambda k: -min(k, z.ny - k))

    def in_copy(name, ref, land, k, source, target):
        cols = pl.ds(pl.multiple_of(target * z.cols, z.cols), z.cols)
        return copy(name, ref.at[:, cols], land.at[source], k, source, at(yy=on_y(k)))

    for k in far_first:
        in_copy("in_s", s_ref, xin_s, k, y, on_y(k)).start()
        in_copy("in_t", t_ref, xin_t, k, y, on_y(k)).start()
        pending += [in_copy("in_s", s_ref, xin_s, k, y, on_y(k)), in_copy("in_t", t_ref, xin_t, k, y, on_y(k))]
    own_cols = pl.ds(pl.multiple_of(y * z.cols, z.cols), z.cols)
    own_s = pltpu.make_async_copy(s_ref.at[:, own_cols], xin_s.at[y], sems.at[ids["own"][0]])
    own_t = pltpu.make_async_copy(t_ref.at[:, own_cols], xin_t.at[y], sems.at[ids["own"][0] + 1])
    own_s.start()
    own_t.start()

    gr_ref[...] = g_ref[...].reshape(1, z.samples)
    corner = (lax.broadcasted_iota(jnp.int32, (z.cap, z.cap), 0) == lax.broadcasted_iota(jnp.int32, (z.cap, z.cap), 1))

    def turn(step, _):
        first = pl.multiple_of(step * z.cap, z.cap)
        spread = jnp.where(corner, gr_ref[:, pl.ds(first, z.cap)], 0).astype(F32)
        gc_ref[pl.ds(first, z.cap), :] = jnp.sum(spread, axis=1, keepdims=True).astype(jnp.int32)
        return 0

    lax.fori_loop(0, z.samples // z.cap, turn, 0)

    chunk = z.rows
    for part in range(z.ny):
        cols = pl.ds(part * chunk, chunk)
        ids_row = gr_ref[:, cols]

        def count_before(step, rank):
            first = pl.multiple_of(step * z.cap, z.cap)
            ids_col = gc_ref[pl.ds(first, z.cap), :]
            at_row = first + lax.broadcasted_iota(jnp.int32, (z.cap, chunk), 0)
            at_col = part * chunk + lax.broadcasted_iota(jnp.int32, (z.cap, chunk), 1)
            hit = jnp.where((ids_col == ids_row) & (at_row < at_col), 1, 0)
            return rank + jnp.sum(hit, axis=0, keepdims=True)

        rank = lax.fori_loop(0, z.samples // z.cap, count_before, jnp.zeros((1, chunk), jnp.int32))
        place = ids_row * z.cap + rank

        def fill_sort(step, _):
            first = pl.multiple_of(step * z.cap, z.cap)
            slot = first + lax.broadcasted_iota(jnp.int32, (z.cap, chunk), 0)
            sort_ref[part, pl.ds(first, z.cap), :] = jnp.where(slot == place, 1.0, 0.0).astype(BF16)
            return 0

        lax.fori_loop(0, z.groups, fill_sort, 0)

    own_s.wait()
    own_t.wait()

    xacc[...] = jnp.zeros_like(xacc)
    slots = z.groups * z.cap
    tall_rows = slots // 4

    def sort_from(source):
        def body(step, _):
            first = pl.multiple_of(step * tall_rows, tall_rows)
            place = sort_ref[source, pl.ds(first, tall_rows), :]
            xacc[pl.ds(first, tall_rows), 0:z.cols] += jnp.dot(place, xin_s[source], preferred_element_type=F32)
            xacc[pl.ds(first, tall_rows), z.cols:2 * z.cols] += jnp.dot(place, xin_t[source], preferred_element_type=F32)
            return 0

        lax.fori_loop(0, 4, body, 0)

    sort_from(y)
    for k in reversed(far_first):
        source = on_y(z.ny - k)
        in_copy("in_s", s_ref, xin_s, k, source, on_y(k)).wait_recv()
        in_copy("in_t", t_ref, xin_t, k, source, on_y(k)).wait_recv()
        sort_from(source)

    def distances(group):
        rows = pl.ds(pl.multiple_of(group * z.cap, z.cap), z.cap)
        both = jnp.concatenate([xacc[rows, 0:z.cols], xacc[rows, z.cols:2 * z.cols]], axis=0).astype(BF16)
        xs[group] = both
        gram = lax.dot_general(both, both, (((1,), (1,)), ((), ())), preferred_element_type=F32)
        size = 2 * z.cap
        eye = lax.broadcasted_iota(jnp.int32, (size, size), 0) == lax.broadcasted_iota(jnp.int32, (size, size), 1)
        diagonal = jnp.where(eye, gram, 0.0)
        norm_row = jnp.sum(diagonal, axis=0, keepdims=True)
        norm_col = jnp.sum(diagonal[0:z.cap], axis=1, keepdims=True)
        d_ref[group] = norm_col + norm_row - 2.0 * gram[0:z.cap]

    def core_copy(i, group):
        return copy("core", d_ref.at[group], rc.at[i], i, i, at(cc=other))

    def to_other(i, _):
        distances(other * hg + i)
        core_copy(i, other * hg + i).start()
        return 0

    lax.fori_loop(0, hg, to_other, 0)

    def a1_copy(k, source):
        return copy("a1", d_ref.at[c * hg + on_x(k)], r1a.at[source], k, source, at(xx=on_x(k)))

    def b1_copy(k, source):
        return copy("b1", d_ref.at[c * hg + z.nx + on_y(k)], r1b.at[source], k, source, at(yy=on_y(k)))

    def add_core(i):
        distances(c * hg + i)
        core_copy(i, c * hg + i).wait_recv()
        d_ref[c * hg + i] += rc[i]

    def mine(k, _):
        add_core(on_x(k))

        @pl.when(k < z.nx)
        def _():
            a1_copy(k, x).start()

        add_core(z.nx + on_y(k))

        @pl.when(k < z.nx)
        def _():
            b1_copy(k, y).start()

        return 0

    lax.fori_loop(1, z.nx + 1, mine, 0)

    for i in range(hg):
        pending.append(core_copy(i, other * hg + i))
    for k in range(1, z.nx):
        pending += [a1_copy(k, x), b1_copy(k, y)]
    total_a = d_ref[c * hg + x]
    for k in range(1, z.nx):
        source = on_x(z.nx - k)
        a1_copy(k, source).wait_recv()
        total_a = total_a + r1a[source]
    sums[0] = total_a

    def a2_copy(k, source):
        rows = pl.ds(pl.multiple_of(on_y(k) * quarter, quarter), quarter)
        return copy("a2", sums.at[0, rows], r2a.at[source], k, source, at(yy=on_y(k)))

    for k in range(1, z.ny):
        a2_copy(k, y).start()
        pending.append(a2_copy(k, y))
    total_b = d_ref[c * hg + z.nx + y]
    for k in range(1, z.ny):
        source = on_y(z.ny - k)
        b1_copy(k, source).wait_recv()
        total_b = total_b + r1b[source]
    sums[1] = total_b

    def b2_copy(k, source):
        rows = pl.ds(pl.multiple_of(on_x(k) * quarter, quarter), quarter)
        return copy("b2", sums.at[1, rows], r2b.at[source], k, source, at(xx=on_x(k)))

    for k in range(1, z.nx):
        b2_copy(k, x).start()
        pending.append(b2_copy(k, x))

    part_a = sums[0, pl.ds(pl.multiple_of(y * quarter, quarter), quarter), :]
    for k in range(1, z.ny):
        source = on_y(z.ny - k)
        a2_copy(k, source).wait_recv()
        part_a = part_a + r2a[source]
    u_ref[0:z.half] = part_a.reshape(z.half, 8, 2 * z.cap)
    part_b = sums[1, pl.ds(pl.multiple_of(x * quarter, quarter), quarter), :]
    for k in range(1, z.nx):
        source = on_x(z.nx - k)
        b2_copy(k, source).wait_recv()
        part_b = part_b + r2b[source]
    u_ref[z.half:2 * z.half] = part_b.reshape(z.half, 8, 2 * z.cap)

    def z3_copy(k, source):
        return copy("z3", u_ref.at[on_z(k)], r3.at[source], k, source, at(zz=on_z(k)))

    for k in range(1, z.nz):
        z3_copy(k, zc).start()
        pending.append(z3_copy(k, zc))

    def fill_back(step, _):
        first = pl.multiple_of(step * z.cap, z.cap)
        ids_col = gc_ref[pl.ds(first, z.cap), :]
        at_row = first + lax.broadcasted_iota(jnp.int32, (z.cap, z.samples), 0)
        at_col = lax.broadcasted_iota(jnp.int32, (z.cap, z.samples), 1)
        hit = jnp.where((ids_col == gr_ref[...]) & (at_col < at_row), 1.0, 0.0)
        rank = jnp.sum(hit, axis=1, keepdims=True).astype(jnp.int32)
        place = ids_col * z.cap + rank
        slot = lax.broadcasted_iota(jnp.int32, (z.cap, slots), 1)
        back_ref[pl.ds(first, z.cap), :] = jnp.where(slot == place, 1.0, 0.0).astype(BF16)
        return 0

    lax.fori_loop(0, z.samples // z.cap, fill_back, 0)

    dist = u_ref[zc]
    for k in range(1, z.nz):
        source = on_z(z.nz - k)
        z3_copy(k, source).wait_recv()
        dist = dist + r3[source]

    way = zc // z.half
    member = (1 - way) * x + way * y
    sub = (1 - way) * y + way * x
    group = c * hg + way * z.nx + member
    block = sub * z.half + lax.rem(zc, z.half)
    size = jnp.sum(jnp.where(gr_ref[...] == group, 1.0, 0.0), axis=1, keepdims=True)
    row_at = (block * 8 + lax.broadcasted_iota(jnp.int32, (8, z.cap), 0)).astype(F32)
    col_at = lax.broadcasted_iota(jnp.int32, (8, z.cap), 1).astype(F32)
    mask = jnp.where((row_at < size) & (col_at < size), 1.0, 0.0)
    dist = jnp.maximum(dist, 0.0)
    heights = [tab_ref[idx_ref[m]] for m in range(4)]
    weight_self, weight_cross, row_loss, pull = pair_terms(
        dist[:, 0:z.cap], dist[:, z.cap:2 * z.cap], mask, heights, z.latent)
    lanes = lax.broadcasted_iota(jnp.int32, (8, z.cap), 1)

    def with_row_term(weights, term):
        first = term.astype(BF16).astype(F32)
        second = (term - first).astype(BF16).astype(F32)
        third = term - first - second
        columns = jnp.where(lanes == z.cap - 3, first, jnp.where(lanes == z.cap - 2, second, third))
        return jnp.where(lanes < z.most, weights, columns)

    wf[group, block] = jnp.concatenate(
        [with_row_term(weight_self.astype(F32), pull), with_row_term(-weight_cross.astype(F32), row_loss / size)],
        axis=0).astype(BF16)

    def gz_copy(k, source):
        way_of = source // z.half
        group_of = c * hg + way_of * z.nx + (1 - way_of) * x + way_of * y
        block_of = ((1 - way_of) * y + way_of * x) * z.half + lax.rem(source, z.half)
        place = wf.at[group_of, block_of]
        return copy("gz", place, place, k, source, at(zz=on_z(k)))

    def start(one):
        one.start()
        pending.append(one)

    for k in range(1, z.nz):
        start(gz_copy(k, zc))
    for k in range(1, z.nz):
        gz_copy(k, on_z(z.nz - k)).wait_recv()

    def g2a_copy(k, source):
        place = wf.at[c * hg + x, pl.ds(source * z.half, z.half)]
        return copy("g2a", place, place, k, source, at(yy=on_y(k)))

    def g2b_copy(k, source):
        place = wf.at[c * hg + z.nx + y, pl.ds(source * z.half, z.half)]
        return copy("g2b", place, place, k, source, at(xx=on_x(k)))

    for k in range(1, z.nx):
        start(g2a_copy(k, y))
        start(g2b_copy(k, x))

    def g1a_copy(k, source):
        place = wf.at[c * hg + source]
        return copy("g1a", place, place, k, source, at(xx=on_x(k)))

    def g1b_copy(k, source):
        place = wf.at[c * hg + z.nx + source]
        return copy("g1b", place, place, k, source, at(yy=on_y(k)))

    for k in range(1, z.ny):
        g2a_copy(k, on_y(z.ny - k)).wait_recv()
    for k in range(1, z.nx):
        start(g1a_copy(k, x))
    for k in range(1, z.nx):
        g2b_copy(k, on_x(z.nx - k)).wait_recv()
    for k in range(1, z.ny):
        start(g1b_copy(k, y))
    for k in range(1, z.nx):
        g1a_copy(k, on_x(z.nx - k)).wait_recv()
    for k in range(1, z.ny):
        g1b_copy(k, on_y(z.ny - k)).wait_recv()

    def gc_copy(core):
        place = wf.at[pl.ds(core * hg, hg)]
        return copy("gc", place, place, 0, 0, at(cc=other))

    start(gc_copy(c))

    def force_of(g):
        held = wf[g].astype(F32).reshape(z.blocks, 2, 8, z.cap)
        to_self, to_cross = held[:, 0].reshape(z.cap, z.cap), held[:, 1].reshape(z.cap, z.cap)
        last = lax.broadcasted_iota(jnp.int32, (z.cap, z.cap), 1) >= z.most
        pulls = jnp.sum(jnp.where(last, to_self, 0.0), axis=1, keepdims=True)
        losses[g] = jnp.sum(jnp.where(last, to_cross, 0.0), axis=0, keepdims=True)
        weights = jnp.concatenate([to_self, to_cross], axis=1).astype(BF16)
        values = xs[g]
        pulled = values[0:z.cap].astype(F32) * pulls + jnp.dot(weights, values, preferred_element_type=F32)
        size_of = jnp.sum(jnp.where(gr_ref[...] == g, 1.0, 0.0), axis=1, keepdims=True)
        force = pulled / size_of
        high = force.astype(BF16)
        low = (force - high.astype(F32)).astype(BF16)
        rows = pl.ds(pl.multiple_of(g * z.cap, z.cap), z.cap)
        fs[rows, 0:z.cols] = high
        fs[rows, z.cols:2 * z.cols] = low

    def own_force(i, _):
        force_of(c * hg + i)
        return 0

    def other_force(i, _):
        force_of(other * hg + i)
        return 0

    lax.fori_loop(0, hg, own_force, 0)
    gc_copy(other).wait_recv()
    lax.fori_loop(0, hg, other_force, 0)

    l_ref[...] = jnp.sum(jnp.sum(losses[...], axis=0), axis=1, keepdims=True) / z.samples

    def out_copy(k, source):
        cols = pl.ds(pl.multiple_of(source * z.cols, z.cols), z.cols)
        return copy("out", fo.at[k], f_ref.at[:, cols], k, source, at(yy=on_y(k)))

    def out_local():
        return pltpu.make_async_copy(fo.at[0], f_ref.at[:, own_cols], sems.at[ids["own"][0] + 2])

    def unsort(k):
        rows = pl.ds(pl.multiple_of(on_y(k) * z.rows, z.rows), z.rows)
        moved = jnp.dot(back_ref[rows, :], fs[...], preferred_element_type=F32)
        fo[k] = moved[:, 0:z.cols] + moved[:, z.cols:2 * z.cols]

    def send_out(step, _):
        k = step if z.ny == 2 else lax.rem(step + z.ny // 2 - 1, z.ny - 1) + 1
        if z.ny == 2:
            k = 1
        unsort(k)
        out_copy(k, y).start()
        return 0

    lax.fori_loop(0, z.ny - 1, send_out, 0)
    unsort(0)
    out_local().start()
    out_local().wait()
    for k in range(1, z.ny):
        out_copy(k, on_y(z.ny - k)).wait_recv()

    for k in range(1, z.ny):
        pending.append(out_copy(k, y))
    drain()


def sorted_path(z, student, teacher, bw_table, bw_index, group_ids):
    ids, count = exchanges(z)
    slots, pair, hg = z.groups * z.cap, 2 * z.cap, z.groups // 2
    quarter = z.cap // z.ny
    vmem, smem, anywhere = (pl.BlockSpec(memory_space=m) for m in (pltpu.VMEM, pltpu.SMEM, pl.ANY))
    force, loss = pl.pallas_call(
        functools.partial(fused, z, ids),
        out_shape=(jax.ShapeDtypeStruct((z.rows, z.tile), F32), jax.ShapeDtypeStruct((1, 1), F32)),
        in_specs=[anywhere, anywhere, vmem, smem, smem],
        out_specs=(anywhere, vmem),
        scratch_shapes=[
            pltpu.VMEM((z.ny, z.rows, z.cols), BF16),
            pltpu.VMEM((z.ny, z.rows, z.cols), BF16),
            pltpu.VMEM((z.ny, slots, z.rows), BF16),
            pltpu.VMEM((z.samples, slots), BF16),
            pltpu.VMEM((slots, 2 * z.cols), F32),
            pltpu.VMEM((z.groups, pair, z.cols), BF16),
            pltpu.VMEM((z.groups, z.cap, pair), F32),
            pltpu.VMEM((hg, z.cap, pair), F32),
            pltpu.VMEM((z.nx, z.cap, pair), F32),
            pltpu.VMEM((z.ny, z.cap, pair), F32),
            pltpu.VMEM((2, z.cap, pair), F32),
            pltpu.VMEM((z.ny, quarter, pair), F32),
            pltpu.VMEM((z.nx, quarter, pair), F32),
            pltpu.VMEM((z.nz, 8, pair), F32),
            pltpu.VMEM((z.nz, 8, pair), F32),
            pltpu.VMEM((z.groups, z.blocks, 16, z.cap), BF16),
            pltpu.VMEM((1, z.samples), jnp.int32),
            pltpu.VMEM((z.samples, 1), jnp.int32),
            pltpu.VMEM((z.groups, 1, z.cap), F32),
            pltpu.VMEM((slots, 2 * z.cols), BF16),
            pltpu.VMEM((z.ny, z.rows, z.cols), F32),
            pltpu.SemaphoreType.DMA((count,)),
        ],
        compiler_params=pltpu.CompilerParams(
            collective_id=1, has_side_effects=True, vmem_limit_bytes=56 * 1024 * 1024),
        name="grouped",
    )(student, teacher, group_ids, bw_table, bw_index)
    return force, loss.reshape(())


def gather_pair(z, block):
    y = lax.axis_index("pair")
    out = jnp.zeros((z.ny,) + block.shape, block.dtype)
    for k in range(z.ny):
        moved = lax.ppermute(block, "pair", [(i, (i + k) % z.ny) for i in range(z.ny)]) if k else block
        out = lax.dynamic_update_index_in_dim(out, moved, lax.rem(y + z.ny - k, z.ny), 0)
    return out.reshape((z.ny * block.shape[0],) + block.shape[1:])


def sum_over(array, axis, count):
    step = 1
    while step < count:
        array = array + lax.ppermute(array, axis, [(i, i ^ step) for i in range(count)])
        step *= 2
    return array


def dense_path(z, student, teacher, bw_table, bw_index, group_ids):
    students = gather_pair(z, student)
    teachers = gather_pair(z, teacher)
    both = jnp.concatenate([students, teachers], axis=0)
    wide = both.astype(F32)
    row_wide = student.astype(F32)
    norms = jnp.sum(wide * wide, axis=1)
    row_norms = jnp.sum(row_wide * row_wide, axis=1)
    gram = lax.dot_general(student, both, (((1,), (1,)), ((), ())), preferred_element_type=F32)
    part = row_norms[:, None] + norms[None, :] - 2.0 * gram
    dist = jnp.maximum(sum_over(part, "value", z.nx * z.nz * z.nc), 0.0)
    row_ids = lax.dynamic_slice_in_dim(group_ids, lax.axis_index("pair") * z.rows, z.rows)
    same = (row_ids[:, None] == group_ids[None, :]).astype(F32)
    sizes = jnp.sum(same, axis=1, keepdims=True)
    heights = bw_table[bw_index]
    weight_self, weight_cross, row_loss, pull = pair_terms(
        dist[:, :z.samples], dist[:, z.samples:], same, [heights[m] for m in range(4)], z.latent)
    loss = sum_over(jnp.broadcast_to(jnp.sum(row_loss / sizes), (8, 128)), "pair", z.ny)[0, 0] / z.samples
    pulled = row_wide * pull
    pulled = pulled + jnp.dot(weight_self, students, preferred_element_type=F32)
    pulled = pulled - jnp.dot(weight_cross, teachers, preferred_element_type=F32)
    return pulled / sizes, loss


def build(mesh, z):
    def step(student, teacher, bw_table, bw_index, group_ids):
        each = jnp.arange(z.groups, dtype=group_ids.dtype)
        largest = jnp.max(jnp.sum((group_ids[None, :] == each[:, None]).astype(jnp.int32), axis=1))
        return lax.cond(
            largest <= z.most,
            functools.partial(sorted_path, z),
            functools.partial(dense_path, z),
            student, teacher, bw_table, bw_index, group_ids)

    return jax.shard_map(
        step, mesh=mesh,
        in_specs=(P("pair", "value"), P("pair", "value"), P(None), P(None), P(None)),
        out_specs=(P("pair", "value"), P()),
        check_vma=False)


def solution(mesh):
    return build(mesh, Sizes(ny=4, nx=4, nz=8, nc=2, samples=1536, tile=1024, latent=65536))
```

```python
import functools

import jax
import jax.numpy as jnp
from jax import lax
from jax.experimental import pallas as pl
from jax.experimental.pallas import tpu as pltpu
from jax.sharding import PartitionSpec as P

MESH = pl.DeviceIdType.MESH
F32, BF16 = jnp.float32, jnp.bfloat16


TOGETHER = 4


class Sizes:
    def __init__(self, ny, nx, nz, nc, samples, tile, latent):
        self.ny, self.nx, self.nz, self.nc = ny, nx, nz, nc
        self.samples, self.tile, self.latent = samples, tile, float(latent)
        self.rows = samples // ny
        self.cols = tile // ny
        self.groups = 2 * nc * nx
        self.half = nz // 2
        self.cap = 8 * ny * self.half
        self.blocks = self.cap // 8
        self.most = self.cap - 3
        self.lanes = min(128, self.rows)


def pair_terms(dist_self, dist_cross, mask, heights, latent):
    kern_self = jnp.zeros_like(dist_self)
    kern_cross = jnp.zeros_like(dist_cross)
    weight_self = jnp.zeros_like(dist_self)
    weight_cross = jnp.zeros_like(dist_cross)
    count = len(heights)
    for height in heights:
        width_now = height * latent
        exp_self = jnp.exp(-dist_self / width_now)
        exp_cross = jnp.exp(-dist_cross / width_now)
        kern_self = kern_self + exp_self
        kern_cross = kern_cross + exp_cross
        weight_self = weight_self + exp_self / height
        weight_cross = weight_cross + exp_cross / height
    kern_self = kern_self / count * mask
    kern_cross = kern_cross / count * mask
    weight_self = weight_self / count * mask
    weight_cross = weight_cross / count * mask
    row_loss = jnp.sum(kern_self - 2.0 * kern_cross, axis=1, keepdims=True)
    pull = jnp.sum(weight_cross, axis=1, keepdims=True) - jnp.sum(weight_self, axis=1, keepdims=True)
    return weight_self.astype(BF16), weight_cross.astype(BF16), row_loss, pull


class Pool:
    def __init__(self):
        self.total = 0

    def take(self, count):
        first = self.total
        self.total += count
        return first

    def pair(self, count):
        return self.take(count), self.take(count)


def exchanges(z):
    pool = Pool()
    sizes = {
        "in_s": z.ny, "in_t": z.ny, "core": z.groups // 2, "a1": z.nx, "b1": z.ny, "a2": z.ny, "b2": z.nx, "z3": z.nz,
        "gz": z.nz, "g2a": z.ny, "g2b": z.nx, "g1a": z.nx, "g1b": z.ny, "gc": 1, "out": z.ny, "scale": z.ny, "own": 3,
    }
    return {name: pool.pair(count) for name, count in sizes.items()}, pool.total


def fused(z, ids, s_ref, t_ref, g_ref, tab_ref, idx_ref, q_ref, scale_ref, l_ref, most_ref,
          xin_s, xin_t, sort_ref, back_ref, xacc, xs, d_ref, rc, r1a, r1b, sums, r2a, r2b, u_ref, r3,
          wf, gr_ref, gc_ref, losses, fs, qs, scales, landed, sems):
    y, v = lax.axis_index("pair"), lax.axis_index("value")
    c = lax.rem(v, z.nc)
    x = lax.rem(v // z.nc, z.nx)
    zc = v // (z.nc * z.nx)
    other = 1 - c
    hg = z.groups // 2
    quarter = z.cap // z.ny

    def at(yy=None, xx=None, zz=None, cc=None):
        yy = y if yy is None else yy
        xx = x if xx is None else xx
        zz = zc if zz is None else zz
        cc = c if cc is None else cc
        return (yy, (zz * z.nx + xx) * z.nc + cc)

    def on_y(k):
        return lax.rem(y + k, z.ny)

    def on_x(k):
        return lax.rem(x + k, z.nx)

    def on_z(k):
        return lax.rem(zc + k, z.nz)

    barrier = pltpu.get_barrier_semaphore()
    peers = [at(yy=on_y(k)) for k in range(1, z.ny)] + [at(xx=on_x(k)) for k in range(1, z.nx)]
    peers += [at(zz=on_z(k)) for k in range(1, z.nz)] + [at(cc=other)]
    for peer in peers:
        pl.semaphore_signal(barrier, inc=1, device_id=peer, device_id_type=MESH)
    pl.semaphore_wait(barrier, len(peers))

    def copy(name, src, dst, send, recv, device):
        first_send, first_recv = ids[name]
        return pltpu.make_async_remote_copy(
            src_ref=src, dst_ref=dst, send_sem=sems.at[first_send + send], recv_sem=sems.at[first_recv + recv],
            device_id=device, device_id_type=MESH)

    pending = []

    def drain():
        for one in pending:
            one.wait_send()

    order = sorted(range(1, z.ny), key=lambda k: min(k, z.ny - k))

    def in_copy(name, ref, land, k, source, target):
        cols = pl.ds(pl.multiple_of(target * z.cols, z.cols), z.cols)
        return copy(name, ref.at[:, cols], land.at[source], k, source, at(yy=on_y(k)))

    for k in order:
        in_copy("in_s", s_ref, xin_s, k, y, on_y(k)).start()
        in_copy("in_t", t_ref, xin_t, k, y, on_y(k)).start()
        pending += [in_copy("in_s", s_ref, xin_s, k, y, on_y(k)), in_copy("in_t", t_ref, xin_t, k, y, on_y(k))]
    own_cols = pl.ds(pl.multiple_of(y * z.cols, z.cols), z.cols)
    own_s = pltpu.make_async_copy(s_ref.at[:, own_cols], xin_s.at[y], sems.at[ids["own"][0]])
    own_t = pltpu.make_async_copy(t_ref.at[:, own_cols], xin_t.at[y], sems.at[ids["own"][0] + 1])
    own_s.start()
    own_t.start()

    gr_ref[...] = g_ref[...].reshape(1, z.samples)
    corner = (lax.broadcasted_iota(jnp.int32, (z.cap, z.cap), 0) == lax.broadcasted_iota(jnp.int32, (z.cap, z.cap), 1))

    def turn(step, _):
        first = pl.multiple_of(step * z.cap, z.cap)
        spread = jnp.where(corner, gr_ref[:, pl.ds(first, z.cap)], 0).astype(F32)
        gc_ref[pl.ds(first, z.cap), :] = jnp.sum(spread, axis=1, keepdims=True).astype(jnp.int32)
        return 0

    lax.fori_loop(0, z.samples // z.cap, turn, 0)

    chunk = z.rows
    largest = jnp.zeros((1, 1), jnp.int32)
    for part in range(z.ny):
        cols = pl.ds(part * chunk, chunk)
        ids_row = gr_ref[:, cols]

        def count_before(step, rank):
            first = pl.multiple_of(step * z.cap, z.cap)
            ids_col = gc_ref[pl.ds(first, z.cap), :]
            at_row = first + lax.broadcasted_iota(jnp.int32, (z.cap, chunk), 0)
            at_col = part * chunk + lax.broadcasted_iota(jnp.int32, (z.cap, chunk), 1)
            hit = jnp.where((ids_col == ids_row) & (at_row < at_col), 1, 0)
            return rank + jnp.sum(hit, axis=0, keepdims=True)

        rank = lax.fori_loop(0, z.samples // z.cap, count_before, jnp.zeros((1, chunk), jnp.int32))
        largest = jnp.maximum(largest, jnp.max(rank, axis=1, keepdims=True) + 1)
        place = ids_row * z.cap + rank

        def fill_sort(step, _):
            first = pl.multiple_of(step * z.cap, z.cap)
            slot = first + lax.broadcasted_iota(jnp.int32, (z.cap, chunk), 0)
            sort_ref[part, pl.ds(first, z.cap), :] = jnp.where(slot == place, 1.0, 0.0).astype(BF16)
            return 0

        lax.fori_loop(0, z.groups, fill_sort, 0)

    most_ref[...] = largest
    slots = z.groups * z.cap

    def fill_back(step, _):
        first = pl.multiple_of(step * z.cap, z.cap)
        ids_col = gc_ref[pl.ds(first, z.cap), :]
        at_row = first + lax.broadcasted_iota(jnp.int32, (z.cap, z.samples), 0)
        at_col = lax.broadcasted_iota(jnp.int32, (z.cap, z.samples), 1)
        hit = jnp.where((ids_col == gr_ref[...]) & (at_col < at_row), 1.0, 0.0)
        rank = jnp.sum(hit, axis=1, keepdims=True).astype(jnp.int32)
        place = ids_col * z.cap + rank
        slot = lax.broadcasted_iota(jnp.int32, (z.cap, slots), 1)
        back_ref[pl.ds(first, z.cap), :] = jnp.where(slot == place, 1.0, 0.0).astype(BF16)
        return 0

    lax.fori_loop(0, z.samples // z.cap, fill_back, 0)

    own_s.wait()
    own_t.wait()

    xacc[...] = jnp.zeros_like(xacc)
    tall_rows = slots // 4

    def sort_from(source):
        def body(step, _):
            first = pl.multiple_of(step * tall_rows, tall_rows)
            place = sort_ref[source, pl.ds(first, tall_rows), :]
            xacc[pl.ds(first, tall_rows), 0:z.cols] += jnp.dot(place, xin_s[source], preferred_element_type=F32)
            xacc[pl.ds(first, tall_rows), z.cols:2 * z.cols] += jnp.dot(place, xin_t[source], preferred_element_type=F32)
            return 0

        lax.fori_loop(0, 4, body, 0)

    sort_from(y)
    for k in order:
        source = on_y(z.ny - k)
        in_copy("in_s", s_ref, xin_s, k, source, on_y(k)).wait_recv()
        in_copy("in_t", t_ref, xin_t, k, source, on_y(k)).wait_recv()
        sort_from(source)

    def distances(groups):
        size = 2 * z.cap
        eye = lax.broadcasted_iota(jnp.int32, (size, size), 0) == lax.broadcasted_iota(jnp.int32, (size, size), 1)
        found = []
        for group in groups:
            rows = pl.ds(pl.multiple_of(group * z.cap, z.cap), z.cap)
            both = jnp.concatenate([xacc[rows, 0:z.cols], xacc[rows, z.cols:2 * z.cols]], axis=0).astype(BF16)
            gram = lax.dot_general(both, both, (((1,), (1,)), ((), ())), preferred_element_type=F32)
            found.append((both, gram))
        parts = []
        for both, gram in found:
            diagonal = jnp.where(eye, gram, 0.0)
            norm_row = jnp.sum(diagonal, axis=0, keepdims=True)
            norm_col = jnp.sum(diagonal[0:z.cap], axis=1, keepdims=True)
            parts.append(norm_col + norm_row - 2.0 * gram[0:z.cap])
        for group, (both, _), part in zip(groups, found, parts):
            xs[group] = both
            d_ref[group] = part

    def core_copy(i, group):
        return copy("core", d_ref.at[group], rc.at[i], i, i, at(cc=other))

    def to_other(i, _):
        now = [TOGETHER * i + n for n in range(TOGETHER)]
        distances([other * hg + n for n in now])
        for n in now:
            core_copy(n, other * hg + n).start()
        return 0

    lax.fori_loop(0, hg // TOGETHER, to_other, 0)

    def a1_copy(k, source):
        return copy("a1", d_ref.at[c * hg + on_x(k)], r1a.at[source], k, source, at(xx=on_x(k)))

    def b1_copy(k, source):
        return copy("b1", d_ref.at[c * hg + z.nx + on_y(k)], r1b.at[source], k, source, at(yy=on_y(k)))

    def mine(k, _):
        now = (on_x(k), z.nx + on_y(k))
        distances([c * hg + i for i in now])
        for i in now:
            core_copy(i, c * hg + i).wait_recv()
            d_ref[c * hg + i] += rc[i]

        @pl.when(k < z.nx)
        def _():
            a1_copy(k, x).start()
            b1_copy(k, y).start()

        return 0

    lax.fori_loop(1, z.nx + 1, mine, 0)

    for i in range(hg):
        pending.append(core_copy(i, other * hg + i))
    for k in range(1, z.nx):
        pending += [a1_copy(k, x), b1_copy(k, y)]
    total_a = d_ref[c * hg + x]
    for k in range(1, z.nx):
        source = on_x(z.nx - k)
        a1_copy(k, source).wait_recv()
        total_a = total_a + r1a[source]
    sums[0] = total_a

    def a2_copy(k, source):
        rows = pl.ds(pl.multiple_of(on_y(k) * quarter, quarter), quarter)
        return copy("a2", sums.at[0, rows], r2a.at[source], k, source, at(yy=on_y(k)))

    for k in range(1, z.ny):
        a2_copy(k, y).start()
        pending.append(a2_copy(k, y))
    total_b = d_ref[c * hg + z.nx + y]
    for k in range(1, z.ny):
        source = on_y(z.ny - k)
        b1_copy(k, source).wait_recv()
        total_b = total_b + r1b[source]
    sums[1] = total_b

    def b2_copy(k, source):
        rows = pl.ds(pl.multiple_of(on_x(k) * quarter, quarter), quarter)
        return copy("b2", sums.at[1, rows], r2b.at[source], k, source, at(xx=on_x(k)))

    for k in range(1, z.nx):
        b2_copy(k, x).start()
        pending.append(b2_copy(k, x))

    part_a = sums[0, pl.ds(pl.multiple_of(y * quarter, quarter), quarter), :]
    for k in range(1, z.ny):
        source = on_y(z.ny - k)
        a2_copy(k, source).wait_recv()
        part_a = part_a + r2a[source]
    u_ref[0:z.half] = part_a.reshape(z.half, 8, 2 * z.cap)
    part_b = sums[1, pl.ds(pl.multiple_of(x * quarter, quarter), quarter), :]
    for k in range(1, z.nx):
        source = on_x(z.nx - k)
        b2_copy(k, source).wait_recv()
        part_b = part_b + r2b[source]
    u_ref[z.half:2 * z.half] = part_b.reshape(z.half, 8, 2 * z.cap)

    def z3_copy(k, source):
        return copy("z3", u_ref.at[on_z(k)], r3.at[source], k, source, at(zz=on_z(k)))

    for k in range(1, z.nz):
        z3_copy(k, zc).start()
        pending.append(z3_copy(k, zc))

    dist = u_ref[zc]
    for k in range(1, z.nz):
        source = on_z(z.nz - k)
        z3_copy(k, source).wait_recv()
        dist = dist + r3[source]

    way = zc // z.half
    member = (1 - way) * x + way * y
    sub = (1 - way) * y + way * x
    group = c * hg + way * z.nx + member
    block = sub * z.half + lax.rem(zc, z.half)
    size = jnp.sum(jnp.where(gr_ref[...] == group, 1.0, 0.0), axis=1, keepdims=True)
    row_at = (block * 8 + lax.broadcasted_iota(jnp.int32, (8, z.cap), 0)).astype(F32)
    col_at = lax.broadcasted_iota(jnp.int32, (8, z.cap), 1).astype(F32)
    mask = jnp.where((row_at < size) & (col_at < size), 1.0, 0.0)
    dist = jnp.maximum(dist, 0.0)
    heights = [tab_ref[idx_ref[m]] for m in range(4)]
    weight_self, weight_cross, row_loss, pull = pair_terms(
        dist[:, 0:z.cap], dist[:, z.cap:2 * z.cap], mask, heights, z.latent)
    lanes = lax.broadcasted_iota(jnp.int32, (8, z.cap), 1)

    def with_row_term(weights, term):
        first = term.astype(BF16).astype(F32)
        second = (term - first).astype(BF16).astype(F32)
        third = term - first - second
        columns = jnp.where(lanes == z.cap - 3, first, jnp.where(lanes == z.cap - 2, second, third))
        return jnp.where(lanes < z.most, weights, columns)

    wf[group, block] = jnp.concatenate(
        [with_row_term(weight_self.astype(F32), pull), with_row_term(-weight_cross.astype(F32), row_loss / size)],
        axis=0).astype(BF16)

    def gz_copy(k, source):
        way_of = source // z.half
        group_of = c * hg + way_of * z.nx + (1 - way_of) * x + way_of * y
        block_of = ((1 - way_of) * y + way_of * x) * z.half + lax.rem(source, z.half)
        place = wf.at[group_of, block_of]
        return copy("gz", place, place, k, source, at(zz=on_z(k)))

    def start(one):
        one.start()
        pending.append(one)

    for k in range(1, z.nz):
        start(gz_copy(k, zc))
    for k in range(1, z.nz):
        gz_copy(k, on_z(z.nz - k)).wait_recv()

    def g2a_copy(k, source):
        place = wf.at[c * hg + x, pl.ds(source * z.half, z.half)]
        return copy("g2a", place, place, k, source, at(yy=on_y(k)))

    def g2b_copy(k, source):
        place = wf.at[c * hg + z.nx + y, pl.ds(source * z.half, z.half)]
        return copy("g2b", place, place, k, source, at(xx=on_x(k)))

    for k in range(1, z.nx):
        start(g2a_copy(k, y))
        start(g2b_copy(k, x))

    def g1a_copy(k, source):
        place = wf.at[c * hg + source]
        return copy("g1a", place, place, k, source, at(xx=on_x(k)))

    def g1b_copy(k, source):
        place = wf.at[c * hg + z.nx + source]
        return copy("g1b", place, place, k, source, at(yy=on_y(k)))

    for k in range(1, z.ny):
        g2a_copy(k, on_y(z.ny - k)).wait_recv()
    for k in range(1, z.nx):
        start(g1a_copy(k, x))
    for k in range(1, z.nx):
        g2b_copy(k, on_x(z.nx - k)).wait_recv()
    for k in range(1, z.ny):
        start(g1b_copy(k, y))
    for k in range(1, z.nx):
        g1a_copy(k, on_x(z.nx - k)).wait_recv()
    for k in range(1, z.ny):
        g1b_copy(k, on_y(z.ny - k)).wait_recv()

    def gc_copy(core):
        place = wf.at[pl.ds(core * hg, hg)]
        return copy("gc", place, place, 0, 0, at(cc=other))

    start(gc_copy(c))

    last = lax.broadcasted_iota(jnp.int32, (z.cap, z.cap), 1) >= z.most

    def force_of(groups):
        found = []
        for g in groups:
            held = wf[g].astype(F32).reshape(z.blocks, 2, 8, z.cap)
            to_self, to_cross = held[:, 0].reshape(z.cap, z.cap), held[:, 1].reshape(z.cap, z.cap)
            pulls = jnp.sum(jnp.where(last, to_self, 0.0), axis=1, keepdims=True)
            loss = jnp.sum(jnp.where(last, to_cross, 0.0), axis=0, keepdims=True)
            weights = jnp.concatenate([to_self, to_cross], axis=1).astype(BF16)
            values = xs[g]
            pulled = values[0:z.cap].astype(F32) * pulls + jnp.dot(weights, values, preferred_element_type=F32)
            size_of = jnp.sum(jnp.where(gr_ref[...] == g, 1.0, 0.0), axis=1, keepdims=True)
            force = pulled / size_of
            high = force.astype(BF16)
            low = (force - high.astype(F32)).astype(BF16)
            found.append((loss, high, low))
        for g, (loss, high, low) in zip(groups, found):
            rows = pl.ds(pl.multiple_of(g * z.cap, z.cap), z.cap)
            losses[g] = loss
            fs[rows, 0:z.cols] = high
            fs[rows, z.cols:2 * z.cols] = low

    def own_force(i, _):
        force_of([c * hg + TOGETHER * i + n for n in range(TOGETHER)])
        return 0

    def other_force(i, _):
        force_of([other * hg + TOGETHER * i + n for n in range(TOGETHER)])
        return 0

    lax.fori_loop(0, hg // TOGETHER, own_force, 0)
    gc_copy(other).wait_recv()
    lax.fori_loop(0, hg // TOGETHER, other_force, 0)

    l_ref[...] = jnp.sum(jnp.sum(losses[...], axis=0), axis=1, keepdims=True) / z.samples

    def out_copies(k, source):
        cols = pl.ds(pl.multiple_of(source * z.cols, z.cols), z.cols)
        return (copy("out", qs.at[k], q_ref.at[:, cols], k, source, at(yy=on_y(k))),
                copy("scale", scales.at[k], landed.at[source], k, source, at(yy=on_y(k))))

    parts = z.rows // z.lanes
    square = (z.lanes, z.lanes)
    same = lax.broadcasted_iota(jnp.int32, square, 0) == lax.broadcasted_iota(jnp.int32, square, 1)

    def unsort(k):
        rows = pl.ds(pl.multiple_of(on_y(k) * z.rows, z.rows), z.rows)
        moved = jnp.dot(back_ref[rows, :], fs[...], preferred_element_type=F32)
        force = moved[:, 0:z.cols] + moved[:, z.cols:2 * z.cols]
        top = jnp.maximum(jnp.max(jnp.abs(force), axis=1, keepdims=True), 1e-33)
        qs[k] = jnp.round(force * (32767.0 / top)).astype(jnp.int32).astype(jnp.int16)
        step = top / 32767.0
        for part in range(parts):
            spread = jnp.where(same, step[part * z.lanes:(part + 1) * z.lanes], 0.0)
            scales[k, part:part + 1, :] = jnp.sum(spread, axis=0, keepdims=True)

    def send_out(step, _):
        k = lax.rem(step + z.ny // 2 - 1, z.ny - 1) + 1
        unsort(k)
        for one in out_copies(k, y):
            one.start()
        return 0

    scales[...] = jnp.zeros_like(scales)
    lax.fori_loop(0, z.ny - 1, send_out, 0)
    unsort(0)
    local = pltpu.make_async_copy(qs.at[0], q_ref.at[:, own_cols], sems.at[ids["own"][0] + 2])
    local.start()
    landed[y] = scales[0]
    for k in range(1, z.ny):
        for one in out_copies(k, on_y(z.ny - k)):
            one.wait_recv()
    for part in range(parts):
        at_lane = lax.broadcasted_iota(jnp.int32, (z.lanes, 128), 1)
        column = jnp.zeros((z.lanes, 128), F32)
        for source in range(z.ny):
            spread = jnp.where(same, landed[source, part:part + 1, :], 0.0)
            column = jnp.where(at_lane == source, jnp.sum(spread, axis=1, keepdims=True), column)
        scale_ref[part * z.lanes:(part + 1) * z.lanes, :] = column
    local.wait()

    for k in range(1, z.ny):
        pending += out_copies(k, y)
    drain()


def sorted_path(z, student, teacher, bw_table, bw_index, group_ids):
    ids, count = exchanges(z)
    slots, pair, hg = z.groups * z.cap, 2 * z.cap, z.groups // 2
    quarter = z.cap // z.ny
    vmem, smem, anywhere = (pl.BlockSpec(memory_space=m) for m in (pltpu.VMEM, pltpu.SMEM, pl.ANY))
    sent, scale, loss, largest = pl.pallas_call(
        functools.partial(fused, z, ids),
        out_shape=(jax.ShapeDtypeStruct((z.rows, z.tile), jnp.int16), jax.ShapeDtypeStruct((z.rows, 128), F32),
                   jax.ShapeDtypeStruct((1, 1), F32), jax.ShapeDtypeStruct((1, 1), jnp.int32)),
        in_specs=[anywhere, anywhere, vmem, smem, smem],
        out_specs=(anywhere, vmem, vmem, vmem),
        scratch_shapes=[
            pltpu.VMEM((z.ny, z.rows, z.cols), BF16),
            pltpu.VMEM((z.ny, z.rows, z.cols), BF16),
            pltpu.VMEM((z.ny, slots, z.rows), BF16),
            pltpu.VMEM((z.samples, slots), BF16),
            pltpu.VMEM((slots, 2 * z.cols), F32),
            pltpu.VMEM((z.groups, pair, z.cols), BF16),
            pltpu.VMEM((z.groups, z.cap, pair), F32),
            pltpu.VMEM((hg, z.cap, pair), F32),
            pltpu.VMEM((z.nx, z.cap, pair), F32),
            pltpu.VMEM((z.ny, z.cap, pair), F32),
            pltpu.VMEM((2, z.cap, pair), F32),
            pltpu.VMEM((z.ny, quarter, pair), F32),
            pltpu.VMEM((z.nx, quarter, pair), F32),
            pltpu.VMEM((z.nz, 8, pair), F32),
            pltpu.VMEM((z.nz, 8, pair), F32),
            pltpu.VMEM((z.groups, z.blocks, 16, z.cap), BF16),
            pltpu.VMEM((1, z.samples), jnp.int32),
            pltpu.VMEM((z.samples, 1), jnp.int32),
            pltpu.VMEM((z.groups, 1, z.cap), F32),
            pltpu.VMEM((slots, 2 * z.cols), BF16),
            pltpu.VMEM((z.ny, z.rows, z.cols), jnp.int16),
            pltpu.VMEM((z.ny, 8, z.lanes), F32),
            pltpu.VMEM((z.ny, 8, z.lanes), F32),
            pltpu.SemaphoreType.DMA((count,)),
        ],
        compiler_params=pltpu.CompilerParams(
            collective_id=1, has_side_effects=True, vmem_limit_bytes=56 * 1024 * 1024),
        name="grouped",
    )(student, teacher, group_ids, bw_table, bw_index)
    return sent, scale, loss.reshape(()), largest.reshape(())


def gather_pair(z, block):
    y = lax.axis_index("pair")
    out = jnp.zeros((z.ny,) + block.shape, block.dtype)
    for k in range(z.ny):
        moved = lax.ppermute(block, "pair", [(i, (i + k) % z.ny) for i in range(z.ny)]) if k else block
        out = lax.dynamic_update_index_in_dim(out, moved, lax.rem(y + z.ny - k, z.ny), 0)
    return out.reshape((z.ny * block.shape[0],) + block.shape[1:])


def sum_over(array, axis, count):
    step = 1
    while step < count:
        array = array + lax.ppermute(array, axis, [(i, i ^ step) for i in range(count)])
        step *= 2
    return array


def dense_path(z, student, teacher, bw_table, bw_index, group_ids):
    students = gather_pair(z, student)
    teachers = gather_pair(z, teacher)
    both = jnp.concatenate([students, teachers], axis=0)
    wide = both.astype(F32)
    row_wide = student.astype(F32)
    norms = jnp.sum(wide * wide, axis=1)
    row_norms = jnp.sum(row_wide * row_wide, axis=1)
    gram = lax.dot_general(student, both, (((1,), (1,)), ((), ())), preferred_element_type=F32)
    part = row_norms[:, None] + norms[None, :] - 2.0 * gram
    dist = jnp.maximum(sum_over(part, "value", z.nx * z.nz * z.nc), 0.0)
    row_ids = lax.dynamic_slice_in_dim(group_ids, lax.axis_index("pair") * z.rows, z.rows)
    same = (row_ids[:, None] == group_ids[None, :]).astype(F32)
    sizes = jnp.sum(same, axis=1, keepdims=True)
    heights = bw_table[bw_index]
    weight_self, weight_cross, row_loss, pull = pair_terms(
        dist[:, :z.samples], dist[:, z.samples:], same, [heights[m] for m in range(4)], z.latent)
    loss = sum_over(jnp.broadcast_to(jnp.sum(row_loss / sizes), (8, 128)), "pair", z.ny)[0, 0] / z.samples
    pulled = row_wide * pull
    pulled = pulled + jnp.dot(weight_self, students, preferred_element_type=F32)
    pulled = pulled - jnp.dot(weight_cross, teachers, preferred_element_type=F32)
    return pulled / sizes, loss


def scaled(z, sent, scale):
    column = lax.broadcasted_iota(jnp.int32, (z.rows, z.tile), 1)
    wide = scale[:, z.ny - 1:z.ny]
    for source in reversed(range(z.ny - 1)):
        wide = jnp.where(column < (source + 1) * z.cols, scale[:, source:source + 1], wide)
    return sent.astype(F32) * wide


def build(mesh, z):
    def step(student, teacher, bw_table, bw_index, group_ids):
        sent, scale, loss, largest = sorted_path(z, student, teacher, bw_table, bw_index, group_ids)
        return lax.cond(
            largest <= z.most,
            lambda *held: (scaled(z, held[0], held[1]), held[2]),
            lambda *held: dense_path(z, *held[3:]),
            sent, scale, loss, student, teacher, bw_table, bw_index, group_ids)

    return jax.shard_map(
        step, mesh=mesh,
        in_specs=(P("pair", "value"), P("pair", "value"), P(None), P(None), P(None)),
        out_specs=(P("pair", "value"), P()),
        check_vma=False)


def solution(mesh):
    return build(mesh, Sizes(ny=4, nx=4, nz=8, nc=2, samples=1536, tile=1024, latent=65536))
```

```python
import functools

import jax
import jax.numpy as jnp
from jax import lax
from jax.experimental import pallas as pl
from jax.experimental.pallas import tpu as pltpu
from jax.sharding import PartitionSpec as P

MESH = pl.DeviceIdType.MESH
F32, BF16 = jnp.float32, jnp.bfloat16


TOGETHER = 4


class Sizes:
    def __init__(self, ny, nx, nz, nc, samples, tile, latent):
        self.ny, self.nx, self.nz, self.nc = ny, nx, nz, nc
        self.samples, self.tile, self.latent = samples, tile, float(latent)
        self.rows = samples // ny
        self.cols = tile // ny
        self.groups = 2 * nc * nx
        self.half = nz // 2
        self.cap = 8 * ny * self.half
        self.blocks = self.cap // 8
        self.most = self.cap - 3
        self.lanes = min(128, self.rows)


def pair_terms(dist_self, dist_cross, mask, heights, latent):
    kern_self = jnp.zeros_like(dist_self)
    kern_cross = jnp.zeros_like(dist_cross)
    weight_self = jnp.zeros_like(dist_self)
    weight_cross = jnp.zeros_like(dist_cross)
    count = len(heights)
    for height in heights:
        width_now = height * latent
        exp_self = jnp.exp(-dist_self / width_now)
        exp_cross = jnp.exp(-dist_cross / width_now)
        kern_self = kern_self + exp_self
        kern_cross = kern_cross + exp_cross
        weight_self = weight_self + exp_self / height
        weight_cross = weight_cross + exp_cross / height
    kern_self = kern_self / count * mask
    kern_cross = kern_cross / count * mask
    weight_self = weight_self / count * mask
    weight_cross = weight_cross / count * mask
    row_loss = jnp.sum(kern_self - 2.0 * kern_cross, axis=1, keepdims=True)
    pull = jnp.sum(weight_cross, axis=1, keepdims=True) - jnp.sum(weight_self, axis=1, keepdims=True)
    return weight_self.astype(BF16), weight_cross.astype(BF16), row_loss, pull


class Pool:
    def __init__(self):
        self.total = 0

    def take(self, count):
        first = self.total
        self.total += count
        return first

    def pair(self, count):
        return self.take(count), self.take(count)


def exchanges(z):
    pool = Pool()
    sizes = {
        "in_s": z.ny, "in_t": z.ny, "core": z.groups // 2, "a1": z.nx, "b1": z.ny, "a2": z.ny, "b2": z.nx, "z3": z.nz,
        "gz": z.nz, "g2a": z.ny, "g2b": z.nx, "g1a": z.nx, "g1b": z.ny, "gc": 2, "out": z.ny, "scale": z.ny, "own": 3,
    }
    return {name: pool.pair(count) for name, count in sizes.items()}, pool.total


def fused(z, ids, s_ref, t_ref, g_ref, tab_ref, idx_ref, q_ref, scale_ref, l_ref, most_ref,
          xin_s, xin_t, sort_ref, back_ref, xacc, xs, d_ref, rc, r1a, r1b, sums, r2a, r2b, u_ref, r3,
          wf, gr_ref, gc_ref, losses, fs, qs, scales, landed, sems):
    y, v = lax.axis_index("pair"), lax.axis_index("value")
    c = lax.rem(v, z.nc)
    x = lax.rem(v // z.nc, z.nx)
    zc = v // (z.nc * z.nx)
    other = 1 - c
    hg = z.groups // 2
    quarter = z.cap // z.ny

    def at(yy=None, xx=None, zz=None, cc=None):
        yy = y if yy is None else yy
        xx = x if xx is None else xx
        zz = zc if zz is None else zz
        cc = c if cc is None else cc
        return (yy, (zz * z.nx + xx) * z.nc + cc)

    def on_y(k):
        return lax.rem(y + k, z.ny)

    def on_x(k):
        return lax.rem(x + k, z.nx)

    def on_z(k):
        return lax.rem(zc + k, z.nz)

    z_order = sorted(range(1, z.nz), key=lambda k: -min(k, z.nz - k))
    barrier = pltpu.get_barrier_semaphore()
    peers = [at(yy=on_y(k)) for k in range(1, z.ny)] + [at(xx=on_x(k)) for k in range(1, z.nx)]
    peers += [at(zz=on_z(k)) for k in range(1, z.nz)] + [at(cc=other)]
    for peer in peers:
        pl.semaphore_signal(barrier, inc=1, device_id=peer, device_id_type=MESH)
    pl.semaphore_wait(barrier, len(peers))

    def copy(name, src, dst, send, recv, device):
        first_send, first_recv = ids[name]
        return pltpu.make_async_remote_copy(
            src_ref=src, dst_ref=dst, send_sem=sems.at[first_send + send], recv_sem=sems.at[first_recv + recv],
            device_id=device, device_id_type=MESH)

    pending = []

    def drain():
        for one in pending:
            one.wait_send()

    order = sorted(range(1, z.ny), key=lambda k: min(k, z.ny - k))

    def in_copy(name, ref, land, k, source, target):
        cols = pl.ds(pl.multiple_of(target * z.cols, z.cols), z.cols)
        return copy(name, ref.at[:, cols], land.at[source], k, source, at(yy=on_y(k)))

    for k in order:
        in_copy("in_s", s_ref, xin_s, k, y, on_y(k)).start()
        in_copy("in_t", t_ref, xin_t, k, y, on_y(k)).start()
        pending += [in_copy("in_s", s_ref, xin_s, k, y, on_y(k)), in_copy("in_t", t_ref, xin_t, k, y, on_y(k))]
    own_cols = pl.ds(pl.multiple_of(y * z.cols, z.cols), z.cols)
    own_s = pltpu.make_async_copy(s_ref.at[:, own_cols], xin_s.at[y], sems.at[ids["own"][0]])
    own_t = pltpu.make_async_copy(t_ref.at[:, own_cols], xin_t.at[y], sems.at[ids["own"][0] + 1])
    own_s.start()
    own_t.start()

    gr_ref[...] = g_ref[...].reshape(1, z.samples)
    corner = (lax.broadcasted_iota(jnp.int32, (z.cap, z.cap), 0) == lax.broadcasted_iota(jnp.int32, (z.cap, z.cap), 1))

    def turn(step, _):
        first = pl.multiple_of(step * z.cap, z.cap)
        spread = jnp.where(corner, gr_ref[:, pl.ds(first, z.cap)], 0).astype(F32)
        gc_ref[pl.ds(first, z.cap), :] = jnp.sum(spread, axis=1, keepdims=True).astype(jnp.int32)
        return 0

    lax.fori_loop(0, z.samples // z.cap, turn, 0)

    chunk = z.rows
    largest = jnp.zeros((1, 1), jnp.int32)
    for part in range(z.ny):
        cols = pl.ds(part * chunk, chunk)
        ids_row = gr_ref[:, cols]

        def count_before(step, rank):
            first = pl.multiple_of(step * z.cap, z.cap)
            ids_col = gc_ref[pl.ds(first, z.cap), :]
            at_row = first + lax.broadcasted_iota(jnp.int32, (z.cap, chunk), 0)
            at_col = part * chunk + lax.broadcasted_iota(jnp.int32, (z.cap, chunk), 1)
            hit = jnp.where((ids_col == ids_row) & (at_row < at_col), 1, 0)
            return rank + jnp.sum(hit, axis=0, keepdims=True)

        rank = lax.fori_loop(0, z.samples // z.cap, count_before, jnp.zeros((1, chunk), jnp.int32))
        largest = jnp.maximum(largest, jnp.max(rank, axis=1, keepdims=True) + 1)
        place = ids_row * z.cap + rank

        def fill_sort(step, _):
            first = pl.multiple_of(step * z.cap, z.cap)
            slot = first + lax.broadcasted_iota(jnp.int32, (z.cap, chunk), 0)
            sort_ref[part, pl.ds(first, z.cap), :] = jnp.where(slot == place, 1.0, 0.0).astype(BF16)
            return 0

        lax.fori_loop(0, z.groups, fill_sort, 0)

    most_ref[...] = largest
    slots = z.groups * z.cap

    def fill_back(step, _):
        first = pl.multiple_of(step * z.cap, z.cap)
        ids_col = gc_ref[pl.ds(first, z.cap), :]
        at_row = first + lax.broadcasted_iota(jnp.int32, (z.cap, z.samples), 0)
        at_col = lax.broadcasted_iota(jnp.int32, (z.cap, z.samples), 1)
        hit = jnp.where((ids_col == gr_ref[...]) & (at_col < at_row), 1.0, 0.0)
        rank = jnp.sum(hit, axis=1, keepdims=True).astype(jnp.int32)
        place = ids_col * z.cap + rank
        slot = lax.broadcasted_iota(jnp.int32, (z.cap, slots), 1)
        back_ref[pl.ds(first, z.cap), :] = jnp.where(slot == place, 1.0, 0.0).astype(BF16)
        return 0

    lax.fori_loop(0, z.samples // z.cap, fill_back, 0)

    own_s.wait()
    own_t.wait()

    xacc[...] = jnp.zeros_like(xacc)
    tall_rows = slots // 4

    def sort_from(source):
        def body(step, _):
            first = pl.multiple_of(step * tall_rows, tall_rows)
            place = sort_ref[source, pl.ds(first, tall_rows), :]
            xacc[pl.ds(first, tall_rows), 0:z.cols] += jnp.dot(place, xin_s[source], preferred_element_type=F32)
            xacc[pl.ds(first, tall_rows), z.cols:2 * z.cols] += jnp.dot(place, xin_t[source], preferred_element_type=F32)
            return 0

        lax.fori_loop(0, 4, body, 0)

    sort_from(y)
    for k in order:
        source = on_y(z.ny - k)
        in_copy("in_s", s_ref, xin_s, k, source, on_y(k)).wait_recv()
        in_copy("in_t", t_ref, xin_t, k, source, on_y(k)).wait_recv()
        sort_from(source)

    def distances(groups):
        size = 2 * z.cap
        eye = lax.broadcasted_iota(jnp.int32, (size, size), 0) == lax.broadcasted_iota(jnp.int32, (size, size), 1)
        found = []
        for group in groups:
            rows = pl.ds(pl.multiple_of(group * z.cap, z.cap), z.cap)
            both = jnp.concatenate([xacc[rows, 0:z.cols], xacc[rows, z.cols:2 * z.cols]], axis=0).astype(BF16)
            gram = lax.dot_general(both, both, (((1,), (1,)), ((), ())), preferred_element_type=F32)
            found.append((both, gram))
        parts = []
        for both, gram in found:
            diagonal = jnp.where(eye, gram, 0.0)
            norm_row = jnp.sum(diagonal, axis=0, keepdims=True)
            norm_col = jnp.sum(diagonal[0:z.cap], axis=1, keepdims=True)
            parts.append(norm_col + norm_row - 2.0 * gram[0:z.cap])
        for group, (both, _), part in zip(groups, found, parts):
            xs[group] = both
            d_ref[group] = part

    def core_copy(i, group):
        return copy("core", d_ref.at[group], rc.at[i], i, i, at(cc=other))

    def to_other(i, _):
        now = [TOGETHER * i + n for n in range(TOGETHER)]
        distances([other * hg + n for n in now])
        for n in now:
            core_copy(n, other * hg + n).start()
        return 0

    lax.fori_loop(0, hg // TOGETHER, to_other, 0)

    def a1_copy(k, source):
        return copy("a1", d_ref.at[c * hg + on_x(k)], r1a.at[source], k, source, at(xx=on_x(k)))

    def b1_copy(k, source):
        return copy("b1", d_ref.at[c * hg + z.nx + on_y(k)], r1b.at[source], k, source, at(yy=on_y(k)))

    def mine(k, _):
        now = (on_x(k), z.nx + on_y(k))
        distances([c * hg + i for i in now])
        for i in now:
            core_copy(i, c * hg + i).wait_recv()
            d_ref[c * hg + i] += rc[i]

        @pl.when(k < z.nx)
        def _():
            a1_copy(k, x).start()
            b1_copy(k, y).start()

        return 0

    lax.fori_loop(1, z.nx + 1, mine, 0)

    for i in range(hg):
        pending.append(core_copy(i, other * hg + i))
    for k in range(1, z.nx):
        pending += [a1_copy(k, x), b1_copy(k, y)]
    total_a = d_ref[c * hg + x]
    for k in range(1, z.nx):
        source = on_x(z.nx - k)
        a1_copy(k, source).wait_recv()
        total_a = total_a + r1a[source]
    sums[0] = total_a

    def a2_copy(k, source):
        rows = pl.ds(pl.multiple_of(on_y(k) * quarter, quarter), quarter)
        return copy("a2", sums.at[0, rows], r2a.at[source], k, source, at(yy=on_y(k)))

    for k in range(1, z.ny):
        a2_copy(k, y).start()
        pending.append(a2_copy(k, y))
    total_b = d_ref[c * hg + z.nx + y]
    for k in range(1, z.ny):
        source = on_y(z.ny - k)
        b1_copy(k, source).wait_recv()
        total_b = total_b + r1b[source]
    sums[1] = total_b

    def b2_copy(k, source):
        rows = pl.ds(pl.multiple_of(on_x(k) * quarter, quarter), quarter)
        return copy("b2", sums.at[1, rows], r2b.at[source], k, source, at(xx=on_x(k)))

    for k in range(1, z.nx):
        b2_copy(k, x).start()
        pending.append(b2_copy(k, x))

    part_a = sums[0, pl.ds(pl.multiple_of(y * quarter, quarter), quarter), :]
    for k in range(1, z.ny):
        source = on_y(z.ny - k)
        a2_copy(k, source).wait_recv()
        part_a = part_a + r2a[source]
    u_ref[0:z.half] = part_a.reshape(z.half, 8, 2 * z.cap)
    part_b = sums[1, pl.ds(pl.multiple_of(x * quarter, quarter), quarter), :]
    for k in range(1, z.nx):
        source = on_x(z.nx - k)
        b2_copy(k, source).wait_recv()
        part_b = part_b + r2b[source]
    u_ref[z.half:2 * z.half] = part_b.reshape(z.half, 8, 2 * z.cap)

    def z3_copy(k, source):
        return copy("z3", u_ref.at[on_z(k)], r3.at[source], k, source, at(zz=on_z(k)))

    for k in z_order:
        z3_copy(k, zc).start()
        pending.append(z3_copy(k, zc))

    dist = u_ref[zc]
    for k in range(1, z.nz):
        source = on_z(z.nz - k)
        z3_copy(k, source).wait_recv()
        dist = dist + r3[source]

    way = zc // z.half
    member = (1 - way) * x + way * y
    sub = (1 - way) * y + way * x
    group = c * hg + way * z.nx + member
    block = sub * z.half + lax.rem(zc, z.half)
    size = jnp.sum(jnp.where(gr_ref[...] == group, 1.0, 0.0), axis=1, keepdims=True)
    row_at = (block * 8 + lax.broadcasted_iota(jnp.int32, (8, z.cap), 0)).astype(F32)
    col_at = lax.broadcasted_iota(jnp.int32, (8, z.cap), 1).astype(F32)
    mask = jnp.where((row_at < size) & (col_at < size), 1.0, 0.0)
    dist = jnp.maximum(dist, 0.0)
    heights = [tab_ref[idx_ref[m]] for m in range(4)]
    weight_self, weight_cross, row_loss, pull = pair_terms(
        dist[:, 0:z.cap], dist[:, z.cap:2 * z.cap], mask, heights, z.latent)
    lanes = lax.broadcasted_iota(jnp.int32, (8, z.cap), 1)

    def with_row_term(weights, term):
        first = term.astype(BF16).astype(F32)
        second = (term - first).astype(BF16).astype(F32)
        third = term - first - second
        columns = jnp.where(lanes == z.cap - 3, first, jnp.where(lanes == z.cap - 2, second, third))
        return jnp.where(lanes < z.most, weights, columns)

    wf[group, block] = jnp.concatenate(
        [with_row_term(weight_self.astype(F32), pull), with_row_term(-weight_cross.astype(F32), row_loss / size)],
        axis=0).astype(BF16)

    def gz_copy(k, source):
        way_of = source // z.half
        group_of = c * hg + way_of * z.nx + (1 - way_of) * x + way_of * y
        block_of = ((1 - way_of) * y + way_of * x) * z.half + lax.rem(source, z.half)
        place = wf.at[group_of, block_of]
        return copy("gz", place, place, k, source, at(zz=on_z(k)))

    def start(one):
        one.start()
        pending.append(one)

    for k in z_order:
        start(gz_copy(k, zc))
    for k in range(1, z.nz):
        gz_copy(k, on_z(z.nz - k)).wait_recv()

    def g2a_copy(k, source):
        place = wf.at[c * hg + x, pl.ds(source * z.half, z.half)]
        return copy("g2a", place, place, k, source, at(yy=on_y(k)))

    def g2b_copy(k, source):
        place = wf.at[c * hg + z.nx + y, pl.ds(source * z.half, z.half)]
        return copy("g2b", place, place, k, source, at(xx=on_x(k)))

    for k in range(1, z.nx):
        start(g2a_copy(k, y))
        start(g2b_copy(k, x))

    def g1a_copy(k, source):
        place = wf.at[c * hg + source]
        return copy("g1a", place, place, k, source, at(xx=on_x(k)))

    def g1b_copy(k, source):
        place = wf.at[c * hg + z.nx + source]
        return copy("g1b", place, place, k, source, at(yy=on_y(k)))

    for k in range(1, z.ny):
        g2a_copy(k, on_y(z.ny - k)).wait_recv()
    for k in range(1, z.nx):
        start(g1a_copy(k, x))
    for k in range(1, z.nx):
        g2b_copy(k, on_x(z.nx - k)).wait_recv()
    for k in range(1, z.ny):
        start(g1b_copy(k, y))
    def gc_copy(way_of, core):
        place = wf.at[pl.ds(core * hg + way_of * z.nx, z.nx)]
        return copy("gc", place, place, way_of, way_of, at(cc=other))

    for k in range(1, z.nx):
        g1a_copy(k, on_x(z.nx - k)).wait_recv()
    start(gc_copy(0, c))
    for k in range(1, z.ny):
        g1b_copy(k, on_y(z.ny - k)).wait_recv()
    start(gc_copy(1, c))

    last = lax.broadcasted_iota(jnp.int32, (z.cap, z.cap), 1) >= z.most

    def force_of(groups):
        found = []
        for g in groups:
            held = wf[g].astype(F32).reshape(z.blocks, 2, 8, z.cap)
            to_self, to_cross = held[:, 0].reshape(z.cap, z.cap), held[:, 1].reshape(z.cap, z.cap)
            pulls = jnp.sum(jnp.where(last, to_self, 0.0), axis=1, keepdims=True)
            loss = jnp.sum(jnp.where(last, to_cross, 0.0), axis=0, keepdims=True)
            weights = jnp.concatenate([to_self, to_cross], axis=1).astype(BF16)
            values = xs[g]
            pulled = values[0:z.cap].astype(F32) * pulls + jnp.dot(weights, values, preferred_element_type=F32)
            size_of = jnp.sum(jnp.where(gr_ref[...] == g, 1.0, 0.0), axis=1, keepdims=True)
            force = pulled / size_of
            high = force.astype(BF16)
            low = (force - high.astype(F32)).astype(BF16)
            found.append((loss, high, low))
        for g, (loss, high, low) in zip(groups, found):
            rows = pl.ds(pl.multiple_of(g * z.cap, z.cap), z.cap)
            losses[g] = loss
            fs[rows, 0:z.cols] = high
            fs[rows, z.cols:2 * z.cols] = low

    def forces(first):
        force_of([first + n for n in range(z.nx)])

    forces(c * hg)
    forces(c * hg + z.nx)
    for way_of in range(2):
        gc_copy(way_of, other).wait_recv()
        forces(other * hg + way_of * z.nx)

    l_ref[...] = jnp.sum(jnp.sum(losses[...], axis=0), axis=1, keepdims=True) / z.samples

    def out_copies(k, source):
        cols = pl.ds(pl.multiple_of(source * z.cols, z.cols), z.cols)
        return (copy("out", qs.at[k], q_ref.at[:, cols], k, source, at(yy=on_y(k))),
                copy("scale", scales.at[k], landed.at[source], k, source, at(yy=on_y(k))))

    parts = z.rows // z.lanes
    square = (z.lanes, z.lanes)
    same = lax.broadcasted_iota(jnp.int32, square, 0) == lax.broadcasted_iota(jnp.int32, square, 1)

    def unsort(k):
        rows = pl.ds(pl.multiple_of(on_y(k) * z.rows, z.rows), z.rows)
        moved = jnp.dot(back_ref[rows, :], fs[...], preferred_element_type=F32)
        force = moved[:, 0:z.cols] + moved[:, z.cols:2 * z.cols]
        top = jnp.maximum(jnp.max(jnp.abs(force), axis=1, keepdims=True), 1e-33)
        qs[k] = jnp.round(force * (32767.0 / top)).astype(jnp.int32).astype(jnp.int16)
        step = top / 32767.0
        for part in range(parts):
            spread = jnp.where(same, step[part * z.lanes:(part + 1) * z.lanes], 0.0)
            scales[k, part:part + 1, :] = jnp.sum(spread, axis=0, keepdims=True)

    def send_out(step, _):
        k = lax.rem(step + z.ny // 2 - 1, z.ny - 1) + 1
        unsort(k)
        for one in out_copies(k, y):
            one.start()
        return 0

    scales[...] = jnp.zeros_like(scales)
    lax.fori_loop(0, z.ny - 1, send_out, 0)
    unsort(0)
    local = pltpu.make_async_copy(qs.at[0], q_ref.at[:, own_cols], sems.at[ids["own"][0] + 2])
    local.start()
    landed[y] = scales[0]
    for k in range(1, z.ny):
        for one in out_copies(k, on_y(z.ny - k)):
            one.wait_recv()
    for part in range(parts):
        at_lane = lax.broadcasted_iota(jnp.int32, (z.lanes, 128), 1)
        column = jnp.zeros((z.lanes, 128), F32)
        for source in range(z.ny):
            spread = jnp.where(same, landed[source, part:part + 1, :], 0.0)
            column = jnp.where(at_lane == source, jnp.sum(spread, axis=1, keepdims=True), column)
        scale_ref[part * z.lanes:(part + 1) * z.lanes, :] = column
    local.wait()

    for k in range(1, z.ny):
        pending += out_copies(k, y)
    drain()


def sorted_path(z, student, teacher, bw_table, bw_index, group_ids):
    ids, count = exchanges(z)
    slots, pair, hg = z.groups * z.cap, 2 * z.cap, z.groups // 2
    quarter = z.cap // z.ny
    vmem, smem, anywhere = (pl.BlockSpec(memory_space=m) for m in (pltpu.VMEM, pltpu.SMEM, pl.ANY))
    sent, scale, loss, largest = pl.pallas_call(
        functools.partial(fused, z, ids),
        out_shape=(jax.ShapeDtypeStruct((z.rows, z.tile), jnp.int16), jax.ShapeDtypeStruct((z.rows, 128), F32),
                   jax.ShapeDtypeStruct((1, 1), F32), jax.ShapeDtypeStruct((1, 1), jnp.int32)),
        in_specs=[anywhere, anywhere, vmem, smem, smem],
        out_specs=(anywhere, vmem, vmem, vmem),
        scratch_shapes=[
            pltpu.VMEM((z.ny, z.rows, z.cols), BF16),
            pltpu.VMEM((z.ny, z.rows, z.cols), BF16),
            pltpu.VMEM((z.ny, slots, z.rows), BF16),
            pltpu.VMEM((z.samples, slots), BF16),
            pltpu.VMEM((slots, 2 * z.cols), F32),
            pltpu.VMEM((z.groups, pair, z.cols), BF16),
            pltpu.VMEM((z.groups, z.cap, pair), F32),
            pltpu.VMEM((hg, z.cap, pair), F32),
            pltpu.VMEM((z.nx, z.cap, pair), F32),
            pltpu.VMEM((z.ny, z.cap, pair), F32),
            pltpu.VMEM((2, z.cap, pair), F32),
            pltpu.VMEM((z.ny, quarter, pair), F32),
            pltpu.VMEM((z.nx, quarter, pair), F32),
            pltpu.VMEM((z.nz, 8, pair), F32),
            pltpu.VMEM((z.nz, 8, pair), F32),
            pltpu.VMEM((z.groups, z.blocks, 16, z.cap), BF16),
            pltpu.VMEM((1, z.samples), jnp.int32),
            pltpu.VMEM((z.samples, 1), jnp.int32),
            pltpu.VMEM((z.groups, 1, z.cap), F32),
            pltpu.VMEM((slots, 2 * z.cols), BF16),
            pltpu.VMEM((z.ny, z.rows, z.cols), jnp.int16),
            pltpu.VMEM((z.ny, 8, z.lanes), F32),
            pltpu.VMEM((z.ny, 8, z.lanes), F32),
            pltpu.SemaphoreType.DMA((count,)),
        ],
        compiler_params=pltpu.CompilerParams(
            collective_id=1, has_side_effects=True, vmem_limit_bytes=56 * 1024 * 1024),
        name="grouped",
    )(student, teacher, group_ids, bw_table, bw_index)
    return sent, scale, loss.reshape(()), largest.reshape(())


def gather_pair(z, block):
    y = lax.axis_index("pair")
    out = jnp.zeros((z.ny,) + block.shape, block.dtype)
    for k in range(z.ny):
        moved = lax.ppermute(block, "pair", [(i, (i + k) % z.ny) for i in range(z.ny)]) if k else block
        out = lax.dynamic_update_index_in_dim(out, moved, lax.rem(y + z.ny - k, z.ny), 0)
    return out.reshape((z.ny * block.shape[0],) + block.shape[1:])


def sum_over(array, axis, count):
    step = 1
    while step < count:
        array = array + lax.ppermute(array, axis, [(i, i ^ step) for i in range(count)])
        step *= 2
    return array


def dense_path(z, student, teacher, bw_table, bw_index, group_ids):
    students = gather_pair(z, student)
    teachers = gather_pair(z, teacher)
    both = jnp.concatenate([students, teachers], axis=0)
    wide = both.astype(F32)
    row_wide = student.astype(F32)
    norms = jnp.sum(wide * wide, axis=1)
    row_norms = jnp.sum(row_wide * row_wide, axis=1)
    gram = lax.dot_general(student, both, (((1,), (1,)), ((), ())), preferred_element_type=F32)
    part = row_norms[:, None] + norms[None, :] - 2.0 * gram
    dist = jnp.maximum(sum_over(part, "value", z.nx * z.nz * z.nc), 0.0)
    row_ids = lax.dynamic_slice_in_dim(group_ids, lax.axis_index("pair") * z.rows, z.rows)
    same = (row_ids[:, None] == group_ids[None, :]).astype(F32)
    sizes = jnp.sum(same, axis=1, keepdims=True)
    heights = bw_table[bw_index]
    weight_self, weight_cross, row_loss, pull = pair_terms(
        dist[:, :z.samples], dist[:, z.samples:], same, [heights[m] for m in range(4)], z.latent)
    loss = sum_over(jnp.broadcast_to(jnp.sum(row_loss / sizes), (8, 128)), "pair", z.ny)[0, 0] / z.samples
    pulled = row_wide * pull
    pulled = pulled + jnp.dot(weight_self, students, preferred_element_type=F32)
    pulled = pulled - jnp.dot(weight_cross, teachers, preferred_element_type=F32)
    return unscaled(z, pulled / sizes) + (loss,)


def scaled(z, sent, scale):
    column = lax.broadcasted_iota(jnp.int32, (z.rows, z.tile), 1)
    wide = scale[:, z.ny - 1:z.ny]
    for source in reversed(range(z.ny - 1)):
        wide = jnp.where(column < (source + 1) * z.cols, scale[:, source:source + 1], wide)
    return sent.astype(F32) * wide


def unscaled(z, force):
    parts = force.reshape(z.rows, z.ny, z.cols)
    top = jnp.maximum(jnp.max(jnp.abs(parts), axis=2, keepdims=True), 1e-33)
    sent = jnp.round(parts * (32767.0 / top)).astype(jnp.int32).astype(jnp.int16)
    return sent.reshape(z.rows, z.tile), jnp.pad(top[:, :, 0] / 32767.0, ((0, 0), (0, 128 - z.ny)))


def build(mesh, z):
    def step(student, teacher, bw_table, bw_index, group_ids):
        sent, scale, loss, largest = sorted_path(z, student, teacher, bw_table, bw_index, group_ids)
        sent, scale, loss = lax.cond(
            largest <= z.most,
            lambda *held: held[:3],
            lambda *held: dense_path(z, *held[3:]),
            sent, scale, loss, student, teacher, bw_table, bw_index, group_ids)
        sent, scale, loss = lax.optimization_barrier((sent, scale, loss))
        return scaled(z, sent, scale), loss

    return jax.shard_map(
        step, mesh=mesh,
        in_specs=(P("pair", "value"), P("pair", "value"), P(None), P(None), P(None)),
        out_specs=(P("pair", "value"), P()),
        check_vma=False)


def solution(mesh):
    return build(mesh, Sizes(ny=4, nx=4, nz=8, nc=2, samples=1536, tile=1024, latent=65536))
```

```python
import functools

import jax
import jax.numpy as jnp
from jax import lax
from jax.experimental import pallas as pl
from jax.experimental.pallas import tpu as pltpu
from jax.sharding import PartitionSpec as P

MESH = pl.DeviceIdType.MESH
F32, BF16 = jnp.float32, jnp.bfloat16


TOGETHER = 4


class Sizes:
    def __init__(self, ny, nx, nz, nc, samples, tile, latent):
        self.ny, self.nx, self.nz, self.nc = ny, nx, nz, nc
        self.samples, self.tile, self.latent = samples, tile, float(latent)
        self.rows = samples // ny
        self.cols = tile // ny
        self.groups = 2 * nc * nx
        self.half = nz // 2
        self.cap = 8 * ny * self.half
        self.blocks = self.cap // 8
        self.most = self.cap - 3
        self.lanes = min(128, self.rows)


def pair_terms(dist_self, dist_cross, mask, heights, latent):
    kern_self = jnp.zeros_like(dist_self)
    kern_cross = jnp.zeros_like(dist_cross)
    weight_self = jnp.zeros_like(dist_self)
    weight_cross = jnp.zeros_like(dist_cross)
    count = len(heights)
    for height in heights:
        width_now = height * latent
        exp_self = jnp.exp(-dist_self / width_now)
        exp_cross = jnp.exp(-dist_cross / width_now)
        kern_self = kern_self + exp_self
        kern_cross = kern_cross + exp_cross
        weight_self = weight_self + exp_self / height
        weight_cross = weight_cross + exp_cross / height
    kern_self = kern_self / count * mask
    kern_cross = kern_cross / count * mask
    weight_self = weight_self / count * mask
    weight_cross = weight_cross / count * mask
    row_loss = jnp.sum(kern_self - 2.0 * kern_cross, axis=1, keepdims=True)
    pull = jnp.sum(weight_cross, axis=1, keepdims=True) - jnp.sum(weight_self, axis=1, keepdims=True)
    return weight_self.astype(BF16), weight_cross.astype(BF16), row_loss, pull


class Pool:
    def __init__(self):
        self.total = 0

    def take(self, count):
        first = self.total
        self.total += count
        return first

    def pair(self, count):
        return self.take(count), self.take(count)


def exchanges(z):
    pool = Pool()
    sizes = {
        "in_s": z.ny, "in_t": z.ny, "core_s": z.groups // 2, "core_c": z.groups // 2, "s1a": z.nx, "s1b": z.nx, "s2a": z.ny, "s2b": z.ny, "s3": z.nz,
        "a1": z.nx, "b1": z.ny, "a2": z.ny, "b2": z.nx, "z3": z.nz,
        "gz": z.nz, "g2a": z.ny, "g2b": z.nx, "g1a": z.nx, "g1b": z.ny, "gc": 2, "out": z.ny, "scale": z.ny, "own": 3,
    }
    return {name: pool.pair(count) for name, count in sizes.items()}, pool.total


def fused(z, ids, s_ref, t_ref, g_ref, tab_ref, idx_ref, f_ref, l_ref, most_ref,
          xin_s, xin_t, sort_ref, back_ref, xacc, xs, norms, ds_ref, dc_ref, rc_s, rc_c, r1sa, r1sb, r2sa, r2sb, sum_sa, sum_sb,
          us_ref, r3s, r1a, r1b, sums, r2a, r2b, u_ref, r3, wf, gr_ref, row_place, col_place, losses, fs, qs, ql, scales, landed, sems):
    y, v = lax.axis_index("pair"), lax.axis_index("value")
    c = lax.rem(v, z.nc)
    x = lax.rem(v // z.nc, z.nx)
    zc = v // (z.nc * z.nx)
    other = 1 - c
    hg = z.groups // 2
    quarter = z.cap // z.ny

    def at(yy=None, xx=None, zz=None, cc=None):
        yy = y if yy is None else yy
        xx = x if xx is None else xx
        zz = zc if zz is None else zz
        cc = c if cc is None else cc
        return (yy, (zz * z.nx + xx) * z.nc + cc)

    def on_y(k):
        return lax.rem(y + k, z.ny)

    def on_x(k):
        return lax.rem(x + k, z.nx)

    def on_z(k):
        return lax.rem(zc + k, z.nz)

    z_order = sorted(range(1, z.nz), key=lambda k: -min(k, z.nz - k))
    barrier = pltpu.get_barrier_semaphore()
    peers = [at(yy=on_y(k)) for k in range(1, z.ny)] + [at(xx=on_x(k)) for k in range(1, z.nx)]
    peers += [at(zz=on_z(k)) for k in range(1, z.nz)] + [at(cc=other)]
    for peer in peers:
        pl.semaphore_signal(barrier, inc=1, device_id=peer, device_id_type=MESH)
    pl.semaphore_wait(barrier, len(peers))

    def copy(name, src, dst, send, recv, device):
        first_send, first_recv = ids[name]
        return pltpu.make_async_remote_copy(
            src_ref=src, dst_ref=dst, send_sem=sems.at[first_send + send], recv_sem=sems.at[first_recv + recv],
            device_id=device, device_id_type=MESH)

    pending = []

    def drain():
        for one in pending:
            one.wait_send()

    order = sorted(range(1, z.ny), key=lambda k: min(k, z.ny - k))

    def in_copy(name, ref, land, k, source, target):
        cols = pl.ds(pl.multiple_of(target * z.cols, z.cols), z.cols)
        return copy(name, ref.at[:, cols], land.at[source], k, source, at(yy=on_y(k)))

    for k in order:
        in_copy("in_s", s_ref, xin_s, k, y, on_y(k)).start()
        pending.append(in_copy("in_t", t_ref, xin_t, k, y, on_y(k)))
    own_cols = pl.ds(pl.multiple_of(y * z.cols, z.cols), z.cols)
    own_s = pltpu.make_async_copy(s_ref.at[:, own_cols], xin_s.at[y], sems.at[ids["own"][0]])
    own_t = pltpu.make_async_copy(t_ref.at[:, own_cols], xin_t.at[y], sems.at[ids["own"][0] + 1])
    own_s.start()
    own_t.start()

    gr_ref[...] = g_ref[...].reshape(1, z.samples)
    slots = z.groups * z.cap
    eye = lax.broadcasted_iota(jnp.int32, (z.cap, z.cap), 0) == lax.broadcasted_iota(jnp.int32, (z.cap, z.cap), 1)
    above = lax.broadcasted_iota(jnp.int32, (z.cap, z.cap), 0) < lax.broadcasted_iota(jnp.int32, (z.cap, z.cap), 1)
    above = jnp.where(above, 1.0, 0.0).astype(BF16)

    def find_places(step, seen):
        first = pl.multiple_of(step * z.cap, z.cap)
        ids_row = gr_ref[:, pl.ds(first, z.cap)]
        hit = jnp.where(lax.broadcasted_iota(jnp.int32, (z.groups, z.cap), 0) == ids_row, 1.0, 0.0)
        before = seen + jnp.dot(hit.astype(BF16), above, preferred_element_type=F32)
        place = (ids_row * z.cap).astype(F32) + jnp.sum(hit * before, axis=0, keepdims=True)
        row_place[:, pl.ds(first, z.cap)] = place.astype(jnp.int32)
        turned = jnp.sum(jnp.where(eye, place, 0.0), axis=1, keepdims=True)
        col_place[pl.ds(first, z.cap), :] = turned.astype(jnp.int32)
        return seen + jnp.sum(hit, axis=1, keepdims=True)

    held = lax.fori_loop(0, z.samples // z.cap, find_places, jnp.zeros((z.groups, 1), F32))
    most_ref[...] = jnp.max(held, axis=0, keepdims=True).astype(jnp.int32)

    for part in range(z.ny):
        def fill_sort(step, _):
            first = pl.multiple_of(step * z.cap, z.cap)
            slot = first + lax.broadcasted_iota(jnp.int32, (z.cap, z.rows), 0)
            place = row_place[:, part * z.rows:(part + 1) * z.rows]
            sort_ref[part, pl.ds(first, z.cap), :] = jnp.where(slot == place, 1.0, 0.0).astype(BF16)
            return 0

        lax.fori_loop(0, z.groups, fill_sort, 0)

    for k in order:
        in_copy("in_s", s_ref, xin_s, k, y, on_y(k)).wait_send()
        in_copy("in_t", t_ref, xin_t, k, y, on_y(k)).start()

    own_s.wait()
    own_t.wait()
    xacc[...] = jnp.zeros_like(xacc)
    tall_rows = slots // 4

    def sort_from(source, values, first_col):
        def body(step, _):
            first = pl.multiple_of(step * tall_rows, tall_rows)
            place = sort_ref[source, pl.ds(first, tall_rows), :]
            xacc[pl.ds(first, tall_rows), first_col:first_col + z.cols] += jnp.dot(
                place, values[source], preferred_element_type=F32)
            return 0

        lax.fori_loop(0, 4, body, 0)

    sort_from(y, xin_s, 0)
    for k in order:
        source = on_y(z.ny - k)
        in_copy("in_s", s_ref, xin_s, k, source, on_y(k)).wait_recv()
        sort_from(source, xin_s, 0)

    def rows_of(group):
        return pl.ds(pl.multiple_of(group * z.cap, z.cap), z.cap)

    outer = (((1,), (1,)), ((), ()))

    def distances_self(groups):
        found = []
        for group in groups:
            mine = xacc[rows_of(group), 0:z.cols].astype(BF16)
            found.append((mine, lax.dot_general(mine, mine, outer, preferred_element_type=F32)))
        parts = []
        for mine, gram in found:
            diagonal = jnp.where(eye, gram, 0.0)
            norm_col = jnp.sum(diagonal, axis=1, keepdims=True)
            parts.append((norm_col, norm_col + jnp.sum(diagonal, axis=0, keepdims=True) - 2.0 * gram))
        for group, (mine, _), (norm_col, part) in zip(groups, found, parts):
            xs[group, 0:z.cap] = mine
            norms[group] = norm_col
            ds_ref[group] = part

    def distances_cross(groups):
        found = []
        for group in groups:
            theirs = xacc[rows_of(group), z.cols:2 * z.cols].astype(BF16)
            both = jnp.concatenate([xs[group, 0:z.cap], theirs], axis=0)
            found.append((theirs, lax.dot_general(both, theirs, outer, preferred_element_type=F32)))
        parts = []
        for group, (theirs, gram) in zip(groups, found):
            norm_row = jnp.sum(jnp.where(eye, gram[z.cap:2 * z.cap], 0.0), axis=0, keepdims=True)
            parts.append(norms[group] + norm_row - 2.0 * gram[0:z.cap])
        for group, (theirs, _), part in zip(groups, found, parts):
            xs[group, z.cap:2 * z.cap] = theirs
            dc_ref[group] = part

    def core_copy(name, part, land, i, group):
        return copy(name, part.at[group], land.at[i], i, i, at(cc=other))

    def quarter_of(k):
        return pl.ds(pl.multiple_of(k * quarter, quarter), quarter)

    def self_to_other(i, _):
        now = [TOGETHER * i + n for n in range(TOGETHER)]
        distances_self([other * hg + n for n in now])
        for n in now:
            core_copy("core_s", ds_ref, rc_s, n, other * hg + n).start()
        return 0

    lax.fori_loop(0, hg // TOGETHER, self_to_other, 0)

    def self_mine(i, _):
        now = [TOGETHER * i + n for n in range(TOGETHER)]
        distances_self([c * hg + n for n in now])
        for n in now:
            core_copy("core_s", ds_ref, rc_s, n, c * hg + n).wait_recv()
            ds_ref[c * hg + n] += rc_s[n]
        return 0

    lax.fori_loop(0, hg // TOGETHER, self_mine, 0)

    def s1_copies(k, source):
        second = ds_ref.at[pl.ds(c * hg + z.nx, z.nx), quarter_of(on_x(k))]
        return (copy("s1a", ds_ref.at[c * hg + on_x(k)], r1sa.at[source], k, source, at(xx=on_x(k))),
                copy("s1b", second, r1sb.at[source], k, source, at(xx=on_x(k))))

    def start(*copies):
        for one in copies:
            one.start()
            pending.append(one)

    for k in range(1, z.nx):
        start(*s1_copies(k, x))
    for i in range(hg):
        pending.append(core_copy("core_s", ds_ref, rc_s, i, other * hg + i))

    def fill_back(step, _):
        first = pl.multiple_of(step * z.cap, z.cap)
        slot = lax.broadcasted_iota(jnp.int32, (z.cap, slots), 1)
        back_ref[pl.ds(first, z.cap), :] = jnp.where(slot == col_place[pl.ds(first, z.cap), :], 1.0, 0.0).astype(BF16)
        return 0

    lax.fori_loop(0, z.samples // z.cap, fill_back, 0)

    sort_from(y, xin_t, z.cols)
    for k in order:
        source = on_y(z.ny - k)
        in_copy("in_t", t_ref, xin_t, k, source, on_y(k)).wait_recv()
        sort_from(source, xin_t, z.cols)

    def cross_to_other(i, _):
        now = [TOGETHER * i + n for n in range(TOGETHER)]
        distances_cross([other * hg + n for n in now])
        for n in now:
            core_copy("core_c", dc_ref, rc_c, n, other * hg + n).start()
        return 0

    lax.fori_loop(0, hg // TOGETHER, cross_to_other, 0)

    def a1_copy(k, source):
        return copy("a1", dc_ref.at[c * hg + on_x(k)], r1a.at[source], k, source, at(xx=on_x(k)))

    def b1_copy(k, source):
        return copy("b1", dc_ref.at[c * hg + z.nx + on_y(k)], r1b.at[source], k, source, at(yy=on_y(k)))

    def mine(k, _):
        now = (on_x(k), z.nx + on_y(k))
        distances_cross([c * hg + i for i in now])
        for i in now:
            core_copy("core_c", dc_ref, rc_c, i, c * hg + i).wait_recv()
            dc_ref[c * hg + i] += rc_c[i]

        @pl.when(k < z.nx)
        def _():
            a1_copy(k, x).start()
            b1_copy(k, y).start()

        return 0

    lax.fori_loop(1, z.nx + 1, mine, 0)
    for i in range(hg):
        pending.append(core_copy("core_c", dc_ref, rc_c, i, other * hg + i))
    for k in range(1, z.nx):
        pending.extend([a1_copy(k, x), b1_copy(k, y)])

    total_a = ds_ref[c * hg + x]
    total_b = ds_ref[pl.ds(c * hg + z.nx, z.nx), quarter_of(x), :]
    for k in range(1, z.nx):
        source = on_x(z.nx - k)
        for one in s1_copies(k, source):
            one.wait_recv()
        total_a = total_a + r1sa[source]
        total_b = total_b + r1sb[source]
    sum_sa[...] = total_a
    sum_sb[...] = total_b

    def s2_copies(k, source):
        return (copy("s2a", sum_sa.at[quarter_of(on_y(k))], r2sa.at[source], k, source, at(yy=on_y(k))),
                copy("s2b", sum_sb.at[on_y(k)], r2sb.at[source], k, source, at(yy=on_y(k))))

    for k in range(1, z.ny):
        start(*s2_copies(k, y))
    part_a = sum_sa[quarter_of(y), :]
    part_b = sum_sb[y]
    for k in range(1, z.ny):
        source = on_y(z.ny - k)
        for one in s2_copies(k, source):
            one.wait_recv()
        part_a = part_a + r2sa[source]
        part_b = part_b + r2sb[source]
    us_ref[0:z.half] = part_a.reshape(z.half, 8, z.cap)
    us_ref[z.half:2 * z.half] = part_b.reshape(z.half, 8, z.cap)

    def s3_copy(k, source):
        return copy("s3", us_ref.at[on_z(k)], r3s.at[source], k, source, at(zz=on_z(k)))

    for k in z_order:
        start(s3_copy(k, zc))

    total_a = dc_ref[c * hg + x]
    for k in range(1, z.nx):
        source = on_x(z.nx - k)
        a1_copy(k, source).wait_recv()
        total_a = total_a + r1a[source]
    sums[0] = total_a

    def a2_copy(k, source):
        return copy("a2", sums.at[0, quarter_of(on_y(k))], r2a.at[source], k, source, at(yy=on_y(k)))

    for k in range(1, z.ny):
        start(a2_copy(k, y))
    total_b = dc_ref[c * hg + z.nx + y]
    for k in range(1, z.ny):
        source = on_y(z.ny - k)
        b1_copy(k, source).wait_recv()
        total_b = total_b + r1b[source]
    sums[1] = total_b

    def b2_copy(k, source):
        return copy("b2", sums.at[1, quarter_of(on_x(k))], r2b.at[source], k, source, at(xx=on_x(k)))

    for k in range(1, z.nx):
        start(b2_copy(k, x))

    part_a = sums[0, quarter_of(y), :]
    for k in range(1, z.ny):
        source = on_y(z.ny - k)
        a2_copy(k, source).wait_recv()
        part_a = part_a + r2a[source]
    u_ref[0:z.half] = part_a.reshape(z.half, 8, z.cap)
    part_b = sums[1, quarter_of(x), :]
    for k in range(1, z.nx):
        source = on_x(z.nx - k)
        b2_copy(k, source).wait_recv()
        part_b = part_b + r2b[source]
    u_ref[z.half:2 * z.half] = part_b.reshape(z.half, 8, z.cap)

    def z3_copy(k, source):
        return copy("z3", u_ref.at[on_z(k)], r3.at[source], k, source, at(zz=on_z(k)))

    for k in z_order:
        start(z3_copy(k, zc))
    dist_self = us_ref[zc]
    for k in range(1, z.nz):
        source = on_z(z.nz - k)
        s3_copy(k, source).wait_recv()
        dist_self = dist_self + r3s[source]
    dist_cross = u_ref[zc]
    for k in range(1, z.nz):
        source = on_z(z.nz - k)
        z3_copy(k, source).wait_recv()
        dist_cross = dist_cross + r3[source]

    way = zc // z.half
    member = (1 - way) * x + way * y
    sub = (1 - way) * y + way * x
    group = c * hg + way * z.nx + member
    block = sub * z.half + lax.rem(zc, z.half)
    size = jnp.sum(jnp.where(gr_ref[...] == group, 1.0, 0.0), axis=1, keepdims=True)
    row_at = (block * 8 + lax.broadcasted_iota(jnp.int32, (8, z.cap), 0)).astype(F32)
    col_at = lax.broadcasted_iota(jnp.int32, (8, z.cap), 1).astype(F32)
    mask = jnp.where((row_at < size) & (col_at < size), 1.0, 0.0)
    heights = [tab_ref[idx_ref[m]] for m in range(4)]
    weight_self, weight_cross, row_loss, pull = pair_terms(
        jnp.maximum(dist_self, 0.0), jnp.maximum(dist_cross, 0.0), mask, heights, z.latent)
    lanes = lax.broadcasted_iota(jnp.int32, (8, z.cap), 1)

    def with_row_term(weights, term):
        first = term.astype(BF16).astype(F32)
        second = (term - first).astype(BF16).astype(F32)
        third = term - first - second
        columns = jnp.where(lanes == z.cap - 3, first, jnp.where(lanes == z.cap - 2, second, third))
        return jnp.where(lanes < z.most, weights, columns)

    wf[group, block] = jnp.concatenate(
        [with_row_term(weight_self.astype(F32), pull), with_row_term(-weight_cross.astype(F32), row_loss / size)],
        axis=0).astype(BF16)

    def gz_copy(k, source):
        way_of = source // z.half
        group_of = c * hg + way_of * z.nx + (1 - way_of) * x + way_of * y
        block_of = ((1 - way_of) * y + way_of * x) * z.half + lax.rem(source, z.half)
        place = wf.at[group_of, block_of]
        return copy("gz", place, place, k, source, at(zz=on_z(k)))

    for k in z_order:
        start(gz_copy(k, zc))
    for k in range(1, z.nz):
        gz_copy(k, on_z(z.nz - k)).wait_recv()

    def g2a_copy(k, source):
        place = wf.at[c * hg + x, pl.ds(source * z.half, z.half)]
        return copy("g2a", place, place, k, source, at(yy=on_y(k)))

    def g2b_copy(k, source):
        place = wf.at[c * hg + z.nx + y, pl.ds(source * z.half, z.half)]
        return copy("g2b", place, place, k, source, at(xx=on_x(k)))

    for k in range(1, z.nx):
        start(g2a_copy(k, y))
        start(g2b_copy(k, x))

    def g1a_copy(k, source):
        place = wf.at[c * hg + source]
        return copy("g1a", place, place, k, source, at(xx=on_x(k)))

    def g1b_copy(k, source):
        place = wf.at[c * hg + z.nx + source]
        return copy("g1b", place, place, k, source, at(yy=on_y(k)))

    for k in range(1, z.ny):
        g2a_copy(k, on_y(z.ny - k)).wait_recv()
    for k in range(1, z.nx):
        start(g1a_copy(k, x))
    for k in range(1, z.nx):
        g2b_copy(k, on_x(z.nx - k)).wait_recv()
    for k in range(1, z.ny):
        start(g1b_copy(k, y))
    def gc_copy(way_of, core):
        place = wf.at[pl.ds(core * hg + way_of * z.nx, z.nx)]
        return copy("gc", place, place, way_of, way_of, at(cc=other))

    for k in range(1, z.nx):
        g1a_copy(k, on_x(z.nx - k)).wait_recv()
    start(gc_copy(0, c))
    for k in range(1, z.ny):
        g1b_copy(k, on_y(z.ny - k)).wait_recv()
    start(gc_copy(1, c))

    last = lax.broadcasted_iota(jnp.int32, (z.cap, z.cap), 1) >= z.most

    def force_of(groups):
        found = []
        for g in groups:
            held = wf[g].astype(F32).reshape(z.blocks, 2, 8, z.cap)
            to_self, to_cross = held[:, 0].reshape(z.cap, z.cap), held[:, 1].reshape(z.cap, z.cap)
            pulls = jnp.sum(jnp.where(last, to_self, 0.0), axis=1, keepdims=True)
            loss = jnp.sum(jnp.where(last, to_cross, 0.0), axis=0, keepdims=True)
            weights = jnp.concatenate([to_self, to_cross], axis=1).astype(BF16)
            values = xs[g]
            pulled = values[0:z.cap].astype(F32) * pulls + jnp.dot(weights, values, preferred_element_type=F32)
            size_of = jnp.sum(jnp.where(gr_ref[...] == g, 1.0, 0.0), axis=1, keepdims=True)
            force = pulled / size_of
            high = force.astype(BF16)
            low = (force - high.astype(F32)).astype(BF16)
            found.append((loss, high, low))
        for g, (loss, high, low) in zip(groups, found):
            rows = pl.ds(pl.multiple_of(g * z.cap, z.cap), z.cap)
            losses[g] = loss
            fs[rows, 0:z.cols] = high
            fs[rows, z.cols:2 * z.cols] = low

    def forces(first):
        force_of([first + n for n in range(z.nx)])

    forces(c * hg)
    forces(c * hg + z.nx)
    for way_of in range(2):
        gc_copy(way_of, other).wait_recv()
        forces(other * hg + way_of * z.nx)

    l_ref[...] = jnp.sum(jnp.sum(losses[...], axis=0), axis=1, keepdims=True) / z.samples

    def out_copies(k, source):
        return (copy("out", qs.at[k], ql.at[source], k, source, at(yy=on_y(k))),
                copy("scale", scales.at[k], landed.at[source], k, source, at(yy=on_y(k))))

    parts = z.rows // z.lanes
    square = (z.lanes, z.lanes)
    same = lax.broadcasted_iota(jnp.int32, square, 0) == lax.broadcasted_iota(jnp.int32, square, 1)

    def unsorted(k):
        rows = pl.ds(pl.multiple_of(on_y(k) * z.rows, z.rows), z.rows)
        moved = jnp.dot(back_ref[rows, :], fs[...], preferred_element_type=F32)
        return moved[:, 0:z.cols] + moved[:, z.cols:2 * z.cols]

    def send_out(step, _):
        k = lax.rem(step + z.ny // 2 - 1, z.ny - 1) + 1
        force = unsorted(k)
        top = jnp.maximum(jnp.max(jnp.abs(force), axis=1, keepdims=True), 1e-33)
        qs[k] = jnp.round(force * (32767.0 / top)).astype(jnp.int32).astype(jnp.int16)
        unit = top / 32767.0
        for part in range(parts):
            spread = jnp.where(same, unit[part * z.lanes:(part + 1) * z.lanes], 0.0)
            scales[k, part:part + 1, :] = jnp.sum(spread, axis=0, keepdims=True)
        for one in out_copies(k, y):
            one.start()
        return 0

    scales[...] = jnp.zeros_like(scales)
    lax.fori_loop(0, z.ny - 1, send_out, 0)
    f_ref[:, own_cols] = unsorted(0)
    for k in order:
        source = on_y(z.ny - k)
        for one in out_copies(k, source):
            one.wait_recv()
        cols = pl.ds(pl.multiple_of(source * z.cols, z.cols), z.cols)
        for part in range(parts):
            rows = slice(part * z.lanes, (part + 1) * z.lanes)
            unit = jnp.sum(jnp.where(same, landed[source, part:part + 1, :], 0.0), axis=1, keepdims=True)
            f_ref[rows, cols] = ql[source, rows, :].astype(jnp.int32).astype(F32) * unit

    for k in range(1, z.ny):
        pending += out_copies(k, y)
    drain()


def sorted_path(z, student, teacher, bw_table, bw_index, group_ids):
    ids, count = exchanges(z)
    slots, hg = z.groups * z.cap, z.groups // 2
    quarter = z.cap // z.ny
    vmem, smem, anywhere = (pl.BlockSpec(memory_space=m) for m in (pltpu.VMEM, pltpu.SMEM, pl.ANY))
    force, loss, largest = pl.pallas_call(
        functools.partial(fused, z, ids),
        out_shape=(jax.ShapeDtypeStruct((z.rows, z.tile), F32), jax.ShapeDtypeStruct((1, 1), F32),
                   jax.ShapeDtypeStruct((1, 1), jnp.int32)),
        in_specs=[anywhere, anywhere, vmem, smem, smem],
        out_specs=(vmem, vmem, vmem),
        scratch_shapes=[
            pltpu.VMEM((z.ny, z.rows, z.cols), BF16),
            pltpu.VMEM((z.ny, z.rows, z.cols), BF16),
            pltpu.VMEM((z.ny, slots, z.rows), BF16),
            pltpu.VMEM((z.samples, slots), BF16),
            pltpu.VMEM((slots, 2 * z.cols), F32),
            pltpu.VMEM((z.groups, 2 * z.cap, z.cols), BF16),
            pltpu.VMEM((z.groups, z.cap, 1), F32),
            pltpu.VMEM((z.groups, z.cap, z.cap), F32),
            pltpu.VMEM((z.groups, z.cap, z.cap), F32),
            pltpu.VMEM((hg, z.cap, z.cap), F32),
            pltpu.VMEM((hg, z.cap, z.cap), F32),
            pltpu.VMEM((z.nx, z.cap, z.cap), F32),
            pltpu.VMEM((z.nx, z.nx, quarter, z.cap), F32),
            pltpu.VMEM((z.ny, quarter, z.cap), F32),
            pltpu.VMEM((z.ny, quarter, z.cap), F32),
            pltpu.VMEM((z.cap, z.cap), F32),
            pltpu.VMEM((z.nx, quarter, z.cap), F32),
            pltpu.VMEM((z.nz, 8, z.cap), F32),
            pltpu.VMEM((z.nz, 8, z.cap), F32),
            pltpu.VMEM((z.nx, z.cap, z.cap), F32),
            pltpu.VMEM((z.ny, z.cap, z.cap), F32),
            pltpu.VMEM((2, z.cap, z.cap), F32),
            pltpu.VMEM((z.ny, quarter, z.cap), F32),
            pltpu.VMEM((z.nx, quarter, z.cap), F32),
            pltpu.VMEM((z.nz, 8, z.cap), F32),
            pltpu.VMEM((z.nz, 8, z.cap), F32),
            pltpu.VMEM((z.groups, z.blocks, 16, z.cap), BF16),
            pltpu.VMEM((1, z.samples), jnp.int32),
            pltpu.VMEM((1, z.samples), jnp.int32),
            pltpu.VMEM((z.samples, 1), jnp.int32),
            pltpu.VMEM((z.groups, 1, z.cap), F32),
            pltpu.VMEM((slots, 2 * z.cols), BF16),
            pltpu.VMEM((z.ny, z.rows, z.cols), jnp.int16),
            pltpu.VMEM((z.ny, z.rows, z.cols), jnp.int16),
            pltpu.VMEM((z.ny, 8, z.lanes), F32),
            pltpu.VMEM((z.ny, 8, z.lanes), F32),
            pltpu.SemaphoreType.DMA((count,)),
        ],
        compiler_params=pltpu.CompilerParams(
            collective_id=1, has_side_effects=True, vmem_limit_bytes=56 * 1024 * 1024),
        name="grouped",
    )(student, teacher, group_ids, bw_table, bw_index)
    return force, loss.reshape(()), largest.reshape(())


def gather_pair(z, block):
    y = lax.axis_index("pair")
    out = jnp.zeros((z.ny,) + block.shape, block.dtype)
    for k in range(z.ny):
        moved = lax.ppermute(block, "pair", [(i, (i + k) % z.ny) for i in range(z.ny)]) if k else block
        out = lax.dynamic_update_index_in_dim(out, moved, lax.rem(y + z.ny - k, z.ny), 0)
    return out.reshape((z.ny * block.shape[0],) + block.shape[1:])


def sum_over(array, axis, count):
    step = 1
    while step < count:
        array = array + lax.ppermute(array, axis, [(i, i ^ step) for i in range(count)])
        step *= 2
    return array


def dense_path(z, student, teacher, bw_table, bw_index, group_ids):
    students = gather_pair(z, student)
    teachers = gather_pair(z, teacher)
    both = jnp.concatenate([students, teachers], axis=0)
    wide = both.astype(F32)
    row_wide = student.astype(F32)
    norms = jnp.sum(wide * wide, axis=1)
    row_norms = jnp.sum(row_wide * row_wide, axis=1)
    gram = lax.dot_general(student, both, (((1,), (1,)), ((), ())), preferred_element_type=F32)
    part = row_norms[:, None] + norms[None, :] - 2.0 * gram
    dist = jnp.maximum(sum_over(part, "value", z.nx * z.nz * z.nc), 0.0)
    row_ids = lax.dynamic_slice_in_dim(group_ids, lax.axis_index("pair") * z.rows, z.rows)
    same = (row_ids[:, None] == group_ids[None, :]).astype(F32)
    sizes = jnp.sum(same, axis=1, keepdims=True)
    heights = bw_table[bw_index]
    weight_self, weight_cross, row_loss, pull = pair_terms(
        dist[:, :z.samples], dist[:, z.samples:], same, [heights[m] for m in range(4)], z.latent)
    loss = sum_over(jnp.broadcast_to(jnp.sum(row_loss / sizes), (8, 128)), "pair", z.ny)[0, 0] / z.samples
    pulled = row_wide * pull
    pulled = pulled + jnp.dot(weight_self, students, preferred_element_type=F32)
    pulled = pulled - jnp.dot(weight_cross, teachers, preferred_element_type=F32)
    return pulled / sizes, loss


def build(mesh, z):
    def step(student, teacher, bw_table, bw_index, group_ids):
        force, loss, largest = sorted_path(z, student, teacher, bw_table, bw_index, group_ids)
        return lax.cond(
            largest <= z.most,
            lambda *held: held[:2],
            lambda *held: dense_path(z, *held[2:]),
            force, loss, student, teacher, bw_table, bw_index, group_ids)

    return jax.shard_map(
        step, mesh=mesh,
        in_specs=(P("pair", "value"), P("pair", "value"), P(None), P(None), P(None)),
        out_specs=(P("pair", "value"), P()),
        check_vma=False)


def solution(mesh):
    return build(mesh, Sizes(ny=4, nx=4, nz=8, nc=2, samples=1536, tile=1024, latent=65536))
```

```python
import functools

import jax
import jax.numpy as jnp
from jax import lax
from jax.experimental import pallas as pl
from jax.experimental.pallas import tpu as pltpu
from jax.sharding import PartitionSpec as P

MESH = pl.DeviceIdType.MESH
F32, BF16 = jnp.float32, jnp.bfloat16


TOGETHER = 4
STEPS = 32767.0


class Sizes:
    def __init__(self, ny, nx, nz, nc, samples, tile, latent):
        self.ny, self.nx, self.nz, self.nc = ny, nx, nz, nc
        self.samples, self.tile, self.latent = samples, tile, float(latent)
        self.rows = samples // ny
        self.cols = tile // ny
        self.groups = 2 * nc * nx
        self.half = nz // 2
        self.cap = 8 * ny * self.half
        self.blocks = self.cap // 8
        self.most = self.cap - 3
        self.lanes = min(128, self.rows)


def pair_terms(dist_self, dist_cross, mask, heights, latent):
    kern_self = jnp.zeros_like(dist_self)
    kern_cross = jnp.zeros_like(dist_cross)
    weight_self = jnp.zeros_like(dist_self)
    weight_cross = jnp.zeros_like(dist_cross)
    count = len(heights)
    for height in heights:
        width_now = height * latent
        exp_self = jnp.exp(-dist_self / width_now)
        exp_cross = jnp.exp(-dist_cross / width_now)
        kern_self = kern_self + exp_self
        kern_cross = kern_cross + exp_cross
        weight_self = weight_self + exp_self / height
        weight_cross = weight_cross + exp_cross / height
    kern_self = kern_self / count * mask
    kern_cross = kern_cross / count * mask
    weight_self = weight_self / count * mask
    weight_cross = weight_cross / count * mask
    row_loss = jnp.sum(kern_self - 2.0 * kern_cross, axis=1, keepdims=True)
    pull = jnp.sum(weight_cross, axis=1, keepdims=True) - jnp.sum(weight_self, axis=1, keepdims=True)
    return weight_self.astype(BF16), weight_cross.astype(BF16), row_loss, pull


class Pool:
    def __init__(self):
        self.total = 0

    def take(self, count):
        first = self.total
        self.total += count
        return first

    def pair(self, count):
        return self.take(count), self.take(count)


def exchanges(z):
    pool = Pool()
    sizes = {
        "in_s": z.ny, "in_t": z.ny, "core_s": z.groups // 2, "core_c": z.groups // 2, "s1a": z.nx, "s1b": z.nx, "s2a": z.ny, "s2b": z.ny, "s3": z.nz,
        "a1": z.nx, "b1": z.ny, "a2": z.ny, "b2": z.nx, "z3": z.nz,
        "gz": z.nz, "g2a": z.ny, "g2b": z.nx, "g1a": z.nx, "g1b": z.ny, "gc": 2, "out": z.ny, "scale": z.ny, "own": 2 + z.ny,
    }
    return {name: pool.pair(count) for name, count in sizes.items()}, pool.total


def fused(z, ids, s_ref, t_ref, g_ref, tab_ref, idx_ref, f_ref, l_ref, most_ref,
          xin_s, xin_t, sort_ref, back_ref, xacc, xs, norms, ds_ref, dc_ref, rc_s, rc_c, r1sa, r1sb, r2sa, r2sb, sum_sa, sum_sb,
          us_ref, r3s, r1a, r1b, sums, r2a, r2b, u_ref, r3, wf, gr_ref, row_place, col_place, sizes, losses, fs, qs, ql, fo, scales, landed, sems):
    y, v = lax.axis_index("pair"), lax.axis_index("value")
    c = lax.rem(v, z.nc)
    x = lax.rem(v // z.nc, z.nx)
    zc = v // (z.nc * z.nx)
    other = 1 - c
    hg = z.groups // 2
    quarter = z.cap // z.ny

    def at(yy=None, xx=None, zz=None, cc=None):
        yy = y if yy is None else yy
        xx = x if xx is None else xx
        zz = zc if zz is None else zz
        cc = c if cc is None else cc
        return (yy, (zz * z.nx + xx) * z.nc + cc)

    def on_y(k):
        return lax.rem(y + k, z.ny)

    def on_x(k):
        return lax.rem(x + k, z.nx)

    def on_z(k):
        return lax.rem(zc + k, z.nz)

    z_order = sorted(range(1, z.nz), key=lambda k: -min(k, z.nz - k))
    barrier = pltpu.get_barrier_semaphore()
    peers = [at(yy=on_y(k)) for k in range(1, z.ny)] + [at(xx=on_x(k)) for k in range(1, z.nx)]
    peers += [at(zz=on_z(k)) for k in range(1, z.nz)] + [at(cc=other)]
    for peer in peers:
        pl.semaphore_signal(barrier, inc=1, device_id=peer, device_id_type=MESH)
    pl.semaphore_wait(barrier, len(peers))

    def copy(name, src, dst, send, recv, device):
        first_send, first_recv = ids[name]
        return pltpu.make_async_remote_copy(
            src_ref=src, dst_ref=dst, send_sem=sems.at[first_send + send], recv_sem=sems.at[first_recv + recv],
            device_id=device, device_id_type=MESH)

    pending = []

    def drain():
        for one in pending:
            one.wait_send()

    order = sorted(range(1, z.ny), key=lambda k: min(k, z.ny - k))

    def in_copy(name, ref, land, k, source, target):
        cols = pl.ds(pl.multiple_of(target * z.cols, z.cols), z.cols)
        return copy(name, ref.at[:, cols], land.at[source], k, source, at(yy=on_y(k)))

    for k in order:
        in_copy("in_s", s_ref, xin_s, k, y, on_y(k)).start()
        pending.append(in_copy("in_t", t_ref, xin_t, k, y, on_y(k)))
    own_cols = pl.ds(pl.multiple_of(y * z.cols, z.cols), z.cols)
    own_s = pltpu.make_async_copy(s_ref.at[:, own_cols], xin_s.at[y], sems.at[ids["own"][0]])
    own_t = pltpu.make_async_copy(t_ref.at[:, own_cols], xin_t.at[y], sems.at[ids["own"][0] + 1])
    own_s.start()
    own_t.start()

    gr_ref[...] = g_ref[...].reshape(1, z.samples)
    slots = z.groups * z.cap
    eye = lax.broadcasted_iota(jnp.int32, (z.cap, z.cap), 0) == lax.broadcasted_iota(jnp.int32, (z.cap, z.cap), 1)
    above = lax.broadcasted_iota(jnp.int32, (z.cap, z.cap), 0) < lax.broadcasted_iota(jnp.int32, (z.cap, z.cap), 1)
    above = jnp.where(above, 1.0, 0.0).astype(BF16)

    def find_places(step, seen):
        first = pl.multiple_of(step * z.cap, z.cap)
        ids_row = gr_ref[:, pl.ds(first, z.cap)]
        hit = jnp.where(lax.broadcasted_iota(jnp.int32, (z.groups, z.cap), 0) == ids_row, 1.0, 0.0)
        before = seen + jnp.dot(hit.astype(BF16), above, preferred_element_type=F32)
        place = (ids_row * z.cap).astype(F32) + jnp.sum(hit * before, axis=0, keepdims=True)
        row_place[:, pl.ds(first, z.cap)] = place.astype(jnp.int32)
        turned = jnp.sum(jnp.where(eye, place, 0.0), axis=1, keepdims=True)
        col_place[pl.ds(first, z.cap), :] = turned.astype(jnp.int32)
        return seen + jnp.sum(hit, axis=1, keepdims=True)

    held = lax.fori_loop(0, z.samples // z.cap, find_places, jnp.zeros((z.groups, 1), F32))
    sizes[...] = jnp.broadcast_to(held[:, :, None], sizes.shape)
    most_ref[...] = jnp.max(held, axis=0, keepdims=True).astype(jnp.int32)

    for part in range(z.ny):
        def fill_sort(step, _):
            first = pl.multiple_of(step * z.cap, z.cap)
            slot = first + lax.broadcasted_iota(jnp.int32, (z.cap, z.rows), 0)
            place = row_place[:, part * z.rows:(part + 1) * z.rows]
            sort_ref[part, pl.ds(first, z.cap), :] = jnp.where(slot == place, 1.0, 0.0).astype(BF16)
            return 0

        lax.fori_loop(0, z.groups, fill_sort, 0)

    for k in order:
        in_copy("in_s", s_ref, xin_s, k, y, on_y(k)).wait_send()
        in_copy("in_t", t_ref, xin_t, k, y, on_y(k)).start()

    own_s.wait()
    own_t.wait()
    xacc[...] = jnp.zeros_like(xacc)
    tall_rows = slots // 4

    def sort_from(source, values, first_col):
        def body(step, _):
            first = pl.multiple_of(step * tall_rows, tall_rows)
            place = sort_ref[source, pl.ds(first, tall_rows), :]
            xacc[pl.ds(first, tall_rows), first_col:first_col + z.cols] += jnp.dot(
                place, values[source], preferred_element_type=F32)
            return 0

        lax.fori_loop(0, 4, body, 0)

    sort_from(y, xin_s, 0)
    for k in order:
        source = on_y(z.ny - k)
        in_copy("in_s", s_ref, xin_s, k, source, on_y(k)).wait_recv()
        sort_from(source, xin_s, 0)

    def rows_of(group):
        return pl.ds(pl.multiple_of(group * z.cap, z.cap), z.cap)

    outer = (((1,), (1,)), ((), ()))

    def distances_self(groups):
        found = []
        for group in groups:
            mine = xacc[rows_of(group), 0:z.cols].astype(BF16)
            found.append((mine, lax.dot_general(mine, mine, outer, preferred_element_type=F32)))
        parts = []
        for mine, gram in found:
            diagonal = jnp.where(eye, gram, 0.0)
            norm_col = jnp.sum(diagonal, axis=1, keepdims=True)
            parts.append((norm_col, norm_col + jnp.sum(diagonal, axis=0, keepdims=True) - 2.0 * gram))
        for group, (mine, _), (norm_col, part) in zip(groups, found, parts):
            xs[group, 0:z.cap] = mine
            norms[group] = norm_col
            ds_ref[group] = part

    def distances_cross(groups):
        found = []
        for group in groups:
            theirs = xacc[rows_of(group), z.cols:2 * z.cols].astype(BF16)
            both = jnp.concatenate([xs[group, 0:z.cap], theirs], axis=0)
            found.append((theirs, lax.dot_general(both, theirs, outer, preferred_element_type=F32)))
        parts = []
        for group, (theirs, gram) in zip(groups, found):
            norm_row = jnp.sum(jnp.where(eye, gram[z.cap:2 * z.cap], 0.0), axis=0, keepdims=True)
            parts.append(norms[group] + norm_row - 2.0 * gram[0:z.cap])
        for group, (theirs, _), part in zip(groups, found, parts):
            xs[group, z.cap:2 * z.cap] = theirs
            dc_ref[group] = part

    def core_copy(name, part, land, i, group):
        return copy(name, part.at[group], land.at[i], i, i, at(cc=other))

    def quarter_of(k):
        return pl.ds(pl.multiple_of(k * quarter, quarter), quarter)

    def self_to_other(i, _):
        now = [TOGETHER * i + n for n in range(TOGETHER)]
        distances_self([other * hg + n for n in now])
        for n in now:
            core_copy("core_s", ds_ref, rc_s, n, other * hg + n).start()
        return 0

    lax.fori_loop(0, hg // TOGETHER, self_to_other, 0)

    def self_mine(i, _):
        now = [TOGETHER * i + n for n in range(TOGETHER)]
        distances_self([c * hg + n for n in now])
        for n in now:
            core_copy("core_s", ds_ref, rc_s, n, c * hg + n).wait_recv()
            ds_ref[c * hg + n] += rc_s[n]
        return 0

    lax.fori_loop(0, hg // TOGETHER, self_mine, 0)

    def s1_copies(k, source):
        second = ds_ref.at[pl.ds(c * hg + z.nx, z.nx), quarter_of(on_x(k))]
        return (copy("s1a", ds_ref.at[c * hg + on_x(k)], r1sa.at[source], k, source, at(xx=on_x(k))),
                copy("s1b", second, r1sb.at[source], k, source, at(xx=on_x(k))))

    def start(*copies):
        for one in copies:
            one.start()
            pending.append(one)

    for k in range(1, z.nx):
        start(*s1_copies(k, x))
    for i in range(hg):
        pending.append(core_copy("core_s", ds_ref, rc_s, i, other * hg + i))

    def fill_back(step, _):
        first = pl.multiple_of(step * z.cap, z.cap)
        slot = lax.broadcasted_iota(jnp.int32, (z.cap, slots), 1)
        back_ref[pl.ds(first, z.cap), :] = jnp.where(slot == col_place[pl.ds(first, z.cap), :], 1.0, 0.0).astype(BF16)
        return 0

    lax.fori_loop(0, z.samples // z.cap, fill_back, 0)

    sort_from(y, xin_t, z.cols)
    for k in order:
        source = on_y(z.ny - k)
        in_copy("in_t", t_ref, xin_t, k, source, on_y(k)).wait_recv()
        sort_from(source, xin_t, z.cols)

    def a1_copy(k, source):
        return copy("a1", dc_ref.at[c * hg + on_x(k)], r1a.at[source], k, source, at(xx=on_x(k)))

    def b1_copy(k, source):
        return copy("b1", dc_ref.at[c * hg + z.nx + on_y(k)], r1b.at[source], k, source, at(yy=on_y(k)))

    def mine(k, _):
        now = (on_x(k), z.nx + on_y(k))
        distances_cross([other * hg + i for i in now])
        for i in now:
            core_copy("core_c", dc_ref, rc_c, i, other * hg + i).start()
        distances_cross([c * hg + i for i in now])
        for i in now:
            core_copy("core_c", dc_ref, rc_c, i, c * hg + i).wait_recv()
            dc_ref[c * hg + i] += rc_c[i]

        @pl.when(k < z.nx)
        def _():
            a1_copy(k, x).start()
            b1_copy(k, y).start()

        return 0

    lax.fori_loop(1, z.nx + 1, mine, 0)
    for i in range(hg):
        pending.append(core_copy("core_c", dc_ref, rc_c, i, other * hg + i))
    for k in range(1, z.nx):
        pending.extend([a1_copy(k, x), b1_copy(k, y)])

    total_a = ds_ref[c * hg + x]
    total_b = ds_ref[pl.ds(c * hg + z.nx, z.nx), quarter_of(x), :]
    for k in range(1, z.nx):
        source = on_x(z.nx - k)
        for one in s1_copies(k, source):
            one.wait_recv()
        total_a = total_a + r1sa[source]
        total_b = total_b + r1sb[source]
    sum_sa[...] = total_a
    sum_sb[...] = total_b

    def s2_copies(k, source):
        return (copy("s2a", sum_sa.at[quarter_of(on_y(k))], r2sa.at[source], k, source, at(yy=on_y(k))),
                copy("s2b", sum_sb.at[on_y(k)], r2sb.at[source], k, source, at(yy=on_y(k))))

    for k in range(1, z.ny):
        start(*s2_copies(k, y))
    part_a = sum_sa[quarter_of(y), :]
    part_b = sum_sb[y]
    for k in range(1, z.ny):
        source = on_y(z.ny - k)
        for one in s2_copies(k, source):
            one.wait_recv()
        part_a = part_a + r2sa[source]
        part_b = part_b + r2sb[source]
    us_ref[0:z.half] = part_a.reshape(z.half, 8, z.cap)
    us_ref[z.half:2 * z.half] = part_b.reshape(z.half, 8, z.cap)

    def s3_copy(k, source):
        return copy("s3", us_ref.at[on_z(k)], r3s.at[source], k, source, at(zz=on_z(k)))

    for k in z_order:
        start(s3_copy(k, zc))

    total_a = dc_ref[c * hg + x]
    for k in range(1, z.nx):
        source = on_x(z.nx - k)
        a1_copy(k, source).wait_recv()
        total_a = total_a + r1a[source]
    sums[0] = total_a

    def a2_copy(k, source):
        return copy("a2", sums.at[0, quarter_of(on_y(k))], r2a.at[source], k, source, at(yy=on_y(k)))

    for k in range(1, z.ny):
        start(a2_copy(k, y))
    total_b = dc_ref[c * hg + z.nx + y]
    for k in range(1, z.ny):
        source = on_y(z.ny - k)
        b1_copy(k, source).wait_recv()
        total_b = total_b + r1b[source]
    sums[1] = total_b

    def b2_copy(k, source):
        return copy("b2", sums.at[1, quarter_of(on_x(k))], r2b.at[source], k, source, at(xx=on_x(k)))

    for k in range(1, z.nx):
        start(b2_copy(k, x))

    part_a = sums[0, quarter_of(y), :]
    for k in range(1, z.ny):
        source = on_y(z.ny - k)
        a2_copy(k, source).wait_recv()
        part_a = part_a + r2a[source]
    u_ref[0:z.half] = part_a.reshape(z.half, 8, z.cap)
    part_b = sums[1, quarter_of(x), :]
    for k in range(1, z.nx):
        source = on_x(z.nx - k)
        b2_copy(k, source).wait_recv()
        part_b = part_b + r2b[source]
    u_ref[z.half:2 * z.half] = part_b.reshape(z.half, 8, z.cap)

    def z3_copy(k, source):
        return copy("z3", u_ref.at[on_z(k)], r3.at[source], k, source, at(zz=on_z(k)))

    for k in z_order:
        start(z3_copy(k, zc))
    dist_self = us_ref[zc]
    for k in range(1, z.nz):
        source = on_z(z.nz - k)
        s3_copy(k, source).wait_recv()
        dist_self = dist_self + r3s[source]
    dist_cross = u_ref[zc]
    for k in range(1, z.nz):
        source = on_z(z.nz - k)
        z3_copy(k, source).wait_recv()
        dist_cross = dist_cross + r3[source]

    way = zc // z.half
    member = (1 - way) * x + way * y
    sub = (1 - way) * y + way * x
    group = c * hg + way * z.nx + member
    block = sub * z.half + lax.rem(zc, z.half)
    size = sizes[group]
    row_at = (block * 8 + lax.broadcasted_iota(jnp.int32, (8, z.cap), 0)).astype(F32)
    col_at = lax.broadcasted_iota(jnp.int32, (8, z.cap), 1).astype(F32)
    mask = jnp.where((row_at < size) & (col_at < size), 1.0, 0.0)
    heights = [tab_ref[idx_ref[m]] for m in range(4)]
    weight_self, weight_cross, row_loss, pull = pair_terms(
        jnp.maximum(dist_self, 0.0), jnp.maximum(dist_cross, 0.0), mask, heights, z.latent)
    lanes = lax.broadcasted_iota(jnp.int32, (8, z.cap), 1)

    def with_row_term(weights, term):
        first = term.astype(BF16).astype(F32)
        second = (term - first).astype(BF16).astype(F32)
        third = term - first - second
        columns = jnp.where(lanes == z.cap - 3, first, jnp.where(lanes == z.cap - 2, second, third))
        return jnp.where(lanes < z.most, weights, columns)

    wf[group, block] = jnp.concatenate(
        [with_row_term(weight_self.astype(F32), pull), with_row_term(-weight_cross.astype(F32), row_loss / size)],
        axis=0).astype(BF16)

    def gz_copy(k, source):
        way_of = source // z.half
        group_of = c * hg + way_of * z.nx + (1 - way_of) * x + way_of * y
        block_of = ((1 - way_of) * y + way_of * x) * z.half + lax.rem(source, z.half)
        place = wf.at[group_of, block_of]
        return copy("gz", place, place, k, source, at(zz=on_z(k)))

    for k in z_order:
        start(gz_copy(k, zc))
    for k in range(1, z.nz):
        gz_copy(k, on_z(z.nz - k)).wait_recv()

    def g2a_copy(k, source):
        place = wf.at[c * hg + x, pl.ds(source * z.half, z.half)]
        return copy("g2a", place, place, k, source, at(yy=on_y(k)))

    def g2b_copy(k, source):
        place = wf.at[c * hg + z.nx + y, pl.ds(source * z.half, z.half)]
        return copy("g2b", place, place, k, source, at(xx=on_x(k)))

    for k in range(1, z.nx):
        start(g2a_copy(k, y))
        start(g2b_copy(k, x))

    def g1a_copy(k, source):
        place = wf.at[c * hg + source]
        return copy("g1a", place, place, k, source, at(xx=on_x(k)))

    def g1b_copy(k, source):
        place = wf.at[c * hg + z.nx + source]
        return copy("g1b", place, place, k, source, at(yy=on_y(k)))

    for k in range(1, z.ny):
        g2a_copy(k, on_y(z.ny - k)).wait_recv()
    for k in range(1, z.nx):
        start(g1a_copy(k, x))
    for k in range(1, z.nx):
        g2b_copy(k, on_x(z.nx - k)).wait_recv()
    for k in range(1, z.ny):
        start(g1b_copy(k, y))
    def gc_copy(way_of, core):
        place = wf.at[pl.ds(core * hg + way_of * z.nx, z.nx)]
        return copy("gc", place, place, way_of, way_of, at(cc=other))

    for k in range(1, z.nx):
        g1a_copy(k, on_x(z.nx - k)).wait_recv()
    start(gc_copy(0, c))
    for k in range(1, z.ny):
        g1b_copy(k, on_y(z.ny - k)).wait_recv()
    start(gc_copy(1, c))

    last = lax.broadcasted_iota(jnp.int32, (z.cap, z.cap), 1) >= z.most

    def force_of(groups):
        found = []
        for g in groups:
            held = wf[g].astype(F32).reshape(z.blocks, 2, 8, z.cap)
            to_self, to_cross = held[:, 0].reshape(z.cap, z.cap), held[:, 1].reshape(z.cap, z.cap)
            pulls = jnp.sum(jnp.where(last, to_self, 0.0), axis=1, keepdims=True)
            loss = jnp.sum(jnp.where(last, to_cross, 0.0), axis=0, keepdims=True)
            weights = jnp.concatenate([to_self, to_cross], axis=1).astype(BF16)
            values = xs[g]
            pulled = values[0:z.cap].astype(F32) * pulls + jnp.dot(weights, values, preferred_element_type=F32)
            force = pulled / sizes[g]
            high = force.astype(BF16)
            low = (force - high.astype(F32)).astype(BF16)
            found.append((loss, high, low))
        for g, (loss, high, low) in zip(groups, found):
            rows = pl.ds(pl.multiple_of(g * z.cap, z.cap), z.cap)
            losses[g] = loss
            fs[rows, 0:z.cols] = high
            fs[rows, z.cols:2 * z.cols] = low

    def forces(first):
        force_of([first + n for n in range(z.nx)])

    forces(c * hg)
    forces(c * hg + z.nx)
    for way_of in range(2):
        gc_copy(way_of, other).wait_recv()
        forces(other * hg + way_of * z.nx)

    l_ref[...] = jnp.sum(jnp.sum(losses[...], axis=0), axis=1, keepdims=True) / z.samples

    def out_copies(k, source):
        return (copy("out", qs.at[k], ql.at[source], k, source, at(yy=on_y(k))),
                copy("scale", scales.at[k], landed.at[source], k, source, at(yy=on_y(k))))

    parts = z.rows // z.lanes
    square = (z.lanes, z.lanes)
    same = lax.broadcasted_iota(jnp.int32, square, 0) == lax.broadcasted_iota(jnp.int32, square, 1)

    def unsorted(k):
        rows = pl.ds(pl.multiple_of(on_y(k) * z.rows, z.rows), z.rows)
        moved = jnp.dot(back_ref[rows, :], fs[...], preferred_element_type=F32)
        return moved[:, 0:z.cols] + moved[:, z.cols:2 * z.cols]

    def send_out(step, _):
        k = lax.rem(step + z.ny // 2 - 1, z.ny - 1) + 1
        force = unsorted(k)
        top = jnp.maximum(jnp.max(jnp.abs(force), axis=1, keepdims=True), 1e-33)
        qs[k] = jnp.round(force * (STEPS / top)).astype(jnp.int32).astype(jnp.int16)
        for part in range(parts):
            spread = jnp.where(same, top[part * z.lanes:(part + 1) * z.lanes], 0.0)
            scales[k, part:part + 1, :] = jnp.sum(spread, axis=0, keepdims=True)
        for one in out_copies(k, y):
            one.start()
        return 0

    scales[...] = jnp.zeros_like(scales)
    lax.fori_loop(0, z.ny - 1, send_out, 0)
    def leave(source):
        cols = pl.ds(pl.multiple_of(source * z.cols, z.cols), z.cols)
        return pltpu.make_async_copy(fo.at[source], f_ref.at[:, cols], sems.at[ids["own"][0] + 2 + source])

    fo[y] = unsorted(0) * STEPS
    leave(y).start()
    for k in order:
        source = on_y(z.ny - k)
        for one in out_copies(k, source):
            one.wait_recv()
        for part in range(parts):
            rows = slice(part * z.lanes, (part + 1) * z.lanes)
            unit = jnp.sum(jnp.where(same, landed[source, part:part + 1, :], 0.0), axis=1, keepdims=True)
            fo[source, rows, :] = ql[source, rows, :].astype(jnp.int32).astype(F32) * unit
        leave(source).start()
    for source in range(z.ny):
        leave(source).wait()

    for k in range(1, z.ny):
        pending += out_copies(k, y)
    drain()


def sorted_path(z, student, teacher, bw_table, bw_index, group_ids):
    ids, count = exchanges(z)
    slots, hg = z.groups * z.cap, z.groups // 2
    quarter = z.cap // z.ny
    vmem, smem, anywhere = (pl.BlockSpec(memory_space=m) for m in (pltpu.VMEM, pltpu.SMEM, pl.ANY))
    force, loss, largest = pl.pallas_call(
        functools.partial(fused, z, ids),
        out_shape=(jax.ShapeDtypeStruct((z.rows, z.tile), F32), jax.ShapeDtypeStruct((1, 1), F32),
                   jax.ShapeDtypeStruct((1, 1), jnp.int32)),
        in_specs=[anywhere, anywhere, vmem, smem, smem],
        out_specs=(anywhere, vmem, vmem),
        scratch_shapes=[
            pltpu.VMEM((z.ny, z.rows, z.cols), BF16),
            pltpu.VMEM((z.ny, z.rows, z.cols), BF16),
            pltpu.VMEM((z.ny, slots, z.rows), BF16),
            pltpu.VMEM((z.samples, slots), BF16),
            pltpu.VMEM((slots, 2 * z.cols), F32),
            pltpu.VMEM((z.groups, 2 * z.cap, z.cols), BF16),
            pltpu.VMEM((z.groups, z.cap, 1), F32),
            pltpu.VMEM((z.groups, z.cap, z.cap), F32),
            pltpu.VMEM((z.groups, z.cap, z.cap), F32),
            pltpu.VMEM((hg, z.cap, z.cap), F32),
            pltpu.VMEM((hg, z.cap, z.cap), F32),
            pltpu.VMEM((z.nx, z.cap, z.cap), F32),
            pltpu.VMEM((z.nx, z.nx, quarter, z.cap), F32),
            pltpu.VMEM((z.ny, quarter, z.cap), F32),
            pltpu.VMEM((z.ny, quarter, z.cap), F32),
            pltpu.VMEM((z.cap, z.cap), F32),
            pltpu.VMEM((z.nx, quarter, z.cap), F32),
            pltpu.VMEM((z.nz, 8, z.cap), F32),
            pltpu.VMEM((z.nz, 8, z.cap), F32),
            pltpu.VMEM((z.nx, z.cap, z.cap), F32),
            pltpu.VMEM((z.ny, z.cap, z.cap), F32),
            pltpu.VMEM((2, z.cap, z.cap), F32),
            pltpu.VMEM((z.ny, quarter, z.cap), F32),
            pltpu.VMEM((z.nx, quarter, z.cap), F32),
            pltpu.VMEM((z.nz, 8, z.cap), F32),
            pltpu.VMEM((z.nz, 8, z.cap), F32),
            pltpu.VMEM((z.groups, z.blocks, 16, z.cap), BF16),
            pltpu.VMEM((1, z.samples), jnp.int32),
            pltpu.VMEM((1, z.samples), jnp.int32),
            pltpu.VMEM((z.samples, 1), jnp.int32),
            pltpu.VMEM((z.groups, 1, 1), F32),
            pltpu.VMEM((z.groups, 1, z.cap), F32),
            pltpu.VMEM((slots, 2 * z.cols), BF16),
            pltpu.VMEM((z.ny, z.rows, z.cols), jnp.int16),
            pltpu.VMEM((z.ny, z.rows, z.cols), jnp.int16),
            pltpu.VMEM((z.ny, z.rows, z.cols), F32),
            pltpu.VMEM((z.ny, 8, z.lanes), F32),
            pltpu.VMEM((z.ny, 8, z.lanes), F32),
            pltpu.SemaphoreType.DMA((count,)),
        ],
        compiler_params=pltpu.CompilerParams(
            collective_id=1, has_side_effects=True, vmem_limit_bytes=56 * 1024 * 1024),
        name="grouped",
    )(student, teacher, group_ids, bw_table, bw_index)
    return force, loss.reshape(()), largest.reshape(())


def gather_pair(z, block):
    y = lax.axis_index("pair")
    out = jnp.zeros((z.ny,) + block.shape, block.dtype)
    for k in range(z.ny):
        moved = lax.ppermute(block, "pair", [(i, (i + k) % z.ny) for i in range(z.ny)]) if k else block
        out = lax.dynamic_update_index_in_dim(out, moved, lax.rem(y + z.ny - k, z.ny), 0)
    return out.reshape((z.ny * block.shape[0],) + block.shape[1:])


def sum_over(array, axis, count):
    step = 1
    while step < count:
        array = array + lax.ppermute(array, axis, [(i, i ^ step) for i in range(count)])
        step *= 2
    return array


def dense_path(z, student, teacher, bw_table, bw_index, group_ids):
    students = gather_pair(z, student)
    teachers = gather_pair(z, teacher)
    both = jnp.concatenate([students, teachers], axis=0)
    wide = both.astype(F32)
    row_wide = student.astype(F32)
    norms = jnp.sum(wide * wide, axis=1)
    row_norms = jnp.sum(row_wide * row_wide, axis=1)
    gram = lax.dot_general(student, both, (((1,), (1,)), ((), ())), preferred_element_type=F32)
    part = row_norms[:, None] + norms[None, :] - 2.0 * gram
    dist = jnp.maximum(sum_over(part, "value", z.nx * z.nz * z.nc), 0.0)
    row_ids = lax.dynamic_slice_in_dim(group_ids, lax.axis_index("pair") * z.rows, z.rows)
    same = (row_ids[:, None] == group_ids[None, :]).astype(F32)
    sizes = jnp.sum(same, axis=1, keepdims=True)
    heights = bw_table[bw_index]
    weight_self, weight_cross, row_loss, pull = pair_terms(
        dist[:, :z.samples], dist[:, z.samples:], same, [heights[m] for m in range(4)], z.latent)
    loss = sum_over(jnp.broadcast_to(jnp.sum(row_loss / sizes), (8, 128)), "pair", z.ny)[0, 0] / z.samples
    pulled = row_wide * pull
    pulled = pulled + jnp.dot(weight_self, students, preferred_element_type=F32)
    pulled = pulled - jnp.dot(weight_cross, teachers, preferred_element_type=F32)
    return pulled / sizes * STEPS, loss


def build(mesh, z):
    def step(student, teacher, bw_table, bw_index, group_ids):
        force, loss, largest = sorted_path(z, student, teacher, bw_table, bw_index, group_ids)
        force, loss = lax.cond(
            largest <= z.most,
            lambda *held: held[:2],
            lambda *held: dense_path(z, *held[2:]),
            force, loss, student, teacher, bw_table, bw_index, group_ids)
        force, loss = lax.optimization_barrier((force, loss))
        return force * (1.0 / STEPS), loss

    return jax.shard_map(
        step, mesh=mesh,
        in_specs=(P("pair", "value"), P("pair", "value"), P(None), P(None), P(None)),
        out_specs=(P("pair", "value"), P()),
        check_vma=False)


def solution(mesh):
    return build(mesh, Sizes(ny=4, nx=4, nz=8, nc=2, samples=1536, tile=1024, latent=65536))
```

```python
import functools

import jax
import jax.numpy as jnp
from jax import lax
from jax.experimental import pallas as pl
from jax.experimental.pallas import tpu as pltpu
from jax.sharding import PartitionSpec as P

MESH = pl.DeviceIdType.MESH
F32, BF16 = jnp.float32, jnp.bfloat16


TOGETHER = 4


class Sizes:
    def __init__(self, ny, nx, nz, nc, samples, tile, latent):
        self.ny, self.nx, self.nz, self.nc = ny, nx, nz, nc
        self.samples, self.tile, self.latent = samples, tile, float(latent)
        self.rows = samples // ny
        self.cols = tile // ny
        self.groups = 2 * nc * nx
        self.half = nz // 2
        self.cap = 8 * ny * self.half
        self.blocks = self.cap // 8
        self.most = self.cap - 3
        self.lanes = min(128, self.rows)


def pair_terms(dist_self, dist_cross, mask, heights, latent):
    kern_self = jnp.zeros_like(dist_self)
    kern_cross = jnp.zeros_like(dist_cross)
    weight_self = jnp.zeros_like(dist_self)
    weight_cross = jnp.zeros_like(dist_cross)
    count = len(heights)
    for height in heights:
        width_now = height * latent
        exp_self = jnp.exp(-dist_self / width_now)
        exp_cross = jnp.exp(-dist_cross / width_now)
        kern_self = kern_self + exp_self
        kern_cross = kern_cross + exp_cross
        weight_self = weight_self + exp_self / height
        weight_cross = weight_cross + exp_cross / height
    kern_self = kern_self / count * mask
    kern_cross = kern_cross / count * mask
    weight_self = weight_self / count * mask
    weight_cross = weight_cross / count * mask
    row_loss = jnp.sum(kern_self - 2.0 * kern_cross, axis=1, keepdims=True)
    pull = jnp.sum(weight_cross, axis=1, keepdims=True) - jnp.sum(weight_self, axis=1, keepdims=True)
    return weight_self.astype(BF16), weight_cross.astype(BF16), row_loss, pull


class Pool:
    def __init__(self):
        self.total = 0

    def take(self, count):
        first = self.total
        self.total += count
        return first

    def pair(self, count):
        return self.take(count), self.take(count)


def exchanges(z):
    pool = Pool()
    sizes = {
        "in_s": z.ny, "in_t": z.ny, "core_s": z.groups // 2, "core_c": z.groups // 2, "s1a": z.nx, "s1b": z.nx, "s2a": z.ny, "s2b": z.ny, "s3": z.nz,
        "a1": z.nx, "b1": z.ny, "a2": z.ny, "b2": z.nx, "z3": z.nz,
        "gz": z.nz, "g2a": z.ny, "g2b": z.nx, "g1a": z.nx, "g1b": z.ny, "gc": 2, "out": z.ny, "scale": z.ny, "own": 2,
    }
    return {name: pool.pair(count) for name, count in sizes.items()}, pool.total


def fused(z, ids, s_ref, t_ref, g_ref, tab_ref, idx_ref, f_ref, l_ref, most_ref,
          xin_s, xin_t, sort_ref, back_ref, xacc, xs, norms, ds_ref, dc_ref, rc_s, rc_c, r1sa, r1sb, r2sa, r2sb, sum_sa, sum_sb,
          us_ref, r3s, r1a, r1b, sums, r2a, r2b, u_ref, r3, wf, gr_ref, row_place, col_place, sizes, losses, fs, qs, ql, scales, landed, sems):
    y, v = lax.axis_index("pair"), lax.axis_index("value")
    c = lax.rem(v, z.nc)
    x = lax.rem(v // z.nc, z.nx)
    zc = v // (z.nc * z.nx)
    other = 1 - c
    hg = z.groups // 2
    quarter = z.cap // z.ny

    def at(yy=None, xx=None, zz=None, cc=None):
        yy = y if yy is None else yy
        xx = x if xx is None else xx
        zz = zc if zz is None else zz
        cc = c if cc is None else cc
        return (yy, (zz * z.nx + xx) * z.nc + cc)

    def on_y(k):
        return lax.rem(y + k, z.ny)

    def on_x(k):
        return lax.rem(x + k, z.nx)

    def on_z(k):
        return lax.rem(zc + k, z.nz)

    z_order = sorted(range(1, z.nz), key=lambda k: -min(k, z.nz - k))
    barrier = pltpu.get_barrier_semaphore()
    peers = [at(yy=on_y(k)) for k in range(1, z.ny)] + [at(xx=on_x(k)) for k in range(1, z.nx)]
    peers += [at(zz=on_z(k)) for k in range(1, z.nz)] + [at(cc=other)]
    for peer in peers:
        pl.semaphore_signal(barrier, inc=1, device_id=peer, device_id_type=MESH)
    pl.semaphore_wait(barrier, len(peers))

    def copy(name, src, dst, send, recv, device):
        first_send, first_recv = ids[name]
        return pltpu.make_async_remote_copy(
            src_ref=src, dst_ref=dst, send_sem=sems.at[first_send + send], recv_sem=sems.at[first_recv + recv],
            device_id=device, device_id_type=MESH)

    pending = []

    def drain():
        for one in pending:
            one.wait_send()

    order = sorted(range(1, z.ny), key=lambda k: min(k, z.ny - k))

    def in_copy(name, ref, land, k, source, target):
        cols = pl.ds(pl.multiple_of(target * z.cols, z.cols), z.cols)
        return copy(name, ref.at[:, cols], land.at[source], k, source, at(yy=on_y(k)))

    for k in order:
        in_copy("in_s", s_ref, xin_s, k, y, on_y(k)).start()
        pending.append(in_copy("in_t", t_ref, xin_t, k, y, on_y(k)))
    own_cols = pl.ds(pl.multiple_of(y * z.cols, z.cols), z.cols)
    own_s = pltpu.make_async_copy(s_ref.at[:, own_cols], xin_s.at[y], sems.at[ids["own"][0]])
    own_t = pltpu.make_async_copy(t_ref.at[:, own_cols], xin_t.at[y], sems.at[ids["own"][0] + 1])
    own_s.start()
    own_t.start()

    gr_ref[...] = g_ref[...].reshape(1, z.samples)
    slots = z.groups * z.cap
    eye = lax.broadcasted_iota(jnp.int32, (z.cap, z.cap), 0) == lax.broadcasted_iota(jnp.int32, (z.cap, z.cap), 1)
    above = lax.broadcasted_iota(jnp.int32, (z.cap, z.cap), 0) < lax.broadcasted_iota(jnp.int32, (z.cap, z.cap), 1)
    above = jnp.where(above, 1.0, 0.0).astype(BF16)

    def find_places(step, seen):
        first = pl.multiple_of(step * z.cap, z.cap)
        ids_row = gr_ref[:, pl.ds(first, z.cap)]
        hit = jnp.where(lax.broadcasted_iota(jnp.int32, (z.groups, z.cap), 0) == ids_row, 1.0, 0.0)
        before = seen + jnp.dot(hit.astype(BF16), above, preferred_element_type=F32)
        place = (ids_row * z.cap).astype(F32) + jnp.sum(hit * before, axis=0, keepdims=True)
        row_place[:, pl.ds(first, z.cap)] = place.astype(jnp.int32)
        turned = jnp.sum(jnp.where(eye, place, 0.0), axis=1, keepdims=True)
        col_place[pl.ds(first, z.cap), :] = turned.astype(jnp.int32)
        return seen + jnp.sum(hit, axis=1, keepdims=True)

    held = lax.fori_loop(0, z.samples // z.cap, find_places, jnp.zeros((z.groups, 1), F32))
    sizes[...] = jnp.broadcast_to(held[:, :, None], sizes.shape)
    most_ref[...] = jnp.max(held, axis=0, keepdims=True).astype(jnp.int32)

    for part in range(z.ny):
        def fill_sort(step, _):
            first = pl.multiple_of(step * z.cap, z.cap)
            slot = first + lax.broadcasted_iota(jnp.int32, (z.cap, z.rows), 0)
            place = row_place[:, part * z.rows:(part + 1) * z.rows]
            sort_ref[part, pl.ds(first, z.cap), :] = jnp.where(slot == place, 1.0, 0.0).astype(BF16)
            return 0

        lax.fori_loop(0, z.groups, fill_sort, 0)

    for k in order:
        in_copy("in_s", s_ref, xin_s, k, y, on_y(k)).wait_send()
        in_copy("in_t", t_ref, xin_t, k, y, on_y(k)).start()

    own_s.wait()
    own_t.wait()
    xacc[...] = jnp.zeros_like(xacc)
    tall_rows = slots // 4

    def sort_from(source, values, first_col):
        def body(step, _):
            first = pl.multiple_of(step * tall_rows, tall_rows)
            place = sort_ref[source, pl.ds(first, tall_rows), :]
            xacc[pl.ds(first, tall_rows), first_col:first_col + z.cols] += jnp.dot(
                place, values[source], preferred_element_type=F32)
            return 0

        lax.fori_loop(0, 4, body, 0)

    sort_from(y, xin_s, 0)
    for k in order:
        source = on_y(z.ny - k)
        in_copy("in_s", s_ref, xin_s, k, source, on_y(k)).wait_recv()
        sort_from(source, xin_s, 0)

    def rows_of(group):
        return pl.ds(pl.multiple_of(group * z.cap, z.cap), z.cap)

    outer = (((1,), (1,)), ((), ()))

    def distances_self(groups):
        found = []
        for group in groups:
            mine = xacc[rows_of(group), 0:z.cols].astype(BF16)
            found.append((mine, lax.dot_general(mine, mine, outer, preferred_element_type=F32)))
        parts = []
        for mine, gram in found:
            diagonal = jnp.where(eye, gram, 0.0)
            norm_col = jnp.sum(diagonal, axis=1, keepdims=True)
            parts.append((norm_col, norm_col + jnp.sum(diagonal, axis=0, keepdims=True) - 2.0 * gram))
        for group, (mine, _), (norm_col, part) in zip(groups, found, parts):
            xs[group, 0:z.cap] = mine
            norms[group] = norm_col
            ds_ref[group] = part

    def distances_cross(groups):
        found = []
        for group in groups:
            theirs = xacc[rows_of(group), z.cols:2 * z.cols].astype(BF16)
            both = jnp.concatenate([xs[group, 0:z.cap], theirs], axis=0)
            found.append((theirs, lax.dot_general(both, theirs, outer, preferred_element_type=F32)))
        parts = []
        for group, (theirs, gram) in zip(groups, found):
            norm_row = jnp.sum(jnp.where(eye, gram[z.cap:2 * z.cap], 0.0), axis=0, keepdims=True)
            parts.append(norms[group] + norm_row - 2.0 * gram[0:z.cap])
        for group, (theirs, _), part in zip(groups, found, parts):
            xs[group, z.cap:2 * z.cap] = theirs
            dc_ref[group] = part

    def core_copy(name, part, land, i, group):
        return copy(name, part.at[group], land.at[i], i, i, at(cc=other))

    def quarter_of(k):
        return pl.ds(pl.multiple_of(k * quarter, quarter), quarter)

    def self_to_other(i, _):
        now = [TOGETHER * i + n for n in range(TOGETHER)]
        distances_self([other * hg + n for n in now])
        for n in now:
            core_copy("core_s", ds_ref, rc_s, n, other * hg + n).start()
        return 0

    lax.fori_loop(0, hg // TOGETHER, self_to_other, 0)

    def self_mine(i, _):
        now = [TOGETHER * i + n for n in range(TOGETHER)]
        distances_self([c * hg + n for n in now])
        for n in now:
            core_copy("core_s", ds_ref, rc_s, n, c * hg + n).wait_recv()
            ds_ref[c * hg + n] += rc_s[n]
        return 0

    lax.fori_loop(0, hg // TOGETHER, self_mine, 0)

    def s1_copies(k, source):
        second = ds_ref.at[pl.ds(c * hg + z.nx, z.nx), quarter_of(on_x(k))]
        return (copy("s1a", ds_ref.at[c * hg + on_x(k)], r1sa.at[source], k, source, at(xx=on_x(k))),
                copy("s1b", second, r1sb.at[source], k, source, at(xx=on_x(k))))

    def start(*copies):
        for one in copies:
            one.start()
            pending.append(one)

    for k in range(1, z.nx):
        start(*s1_copies(k, x))
    for i in range(hg):
        pending.append(core_copy("core_s", ds_ref, rc_s, i, other * hg + i))

    def fill_back(step, _):
        first = pl.multiple_of(step * z.cap, z.cap)
        slot = lax.broadcasted_iota(jnp.int32, (z.cap, slots), 1)
        back_ref[pl.ds(first, z.cap), :] = jnp.where(slot == col_place[pl.ds(first, z.cap), :], 1.0, 0.0).astype(BF16)
        return 0

    lax.fori_loop(0, z.samples // z.cap, fill_back, 0)

    sort_from(y, xin_t, z.cols)
    for k in order:
        source = on_y(z.ny - k)
        in_copy("in_t", t_ref, xin_t, k, source, on_y(k)).wait_recv()
        sort_from(source, xin_t, z.cols)

    def cross_to_other(i, _):
        now = [TOGETHER * i + n for n in range(TOGETHER)]
        distances_cross([other * hg + n for n in now])
        for n in now:
            core_copy("core_c", dc_ref, rc_c, n, other * hg + n).start()
        return 0

    lax.fori_loop(0, hg // TOGETHER, cross_to_other, 0)

    def a1_copy(k, source):
        return copy("a1", dc_ref.at[c * hg + on_x(k)], r1a.at[source], k, source, at(xx=on_x(k)))

    def b1_copy(k, source):
        return copy("b1", dc_ref.at[c * hg + z.nx + on_y(k)], r1b.at[source], k, source, at(yy=on_y(k)))

    def mine(k, _):
        now = (on_x(k), z.nx + on_y(k))
        distances_cross([c * hg + i for i in now])
        for i in now:
            core_copy("core_c", dc_ref, rc_c, i, c * hg + i).wait_recv()
            dc_ref[c * hg + i] += rc_c[i]

        @pl.when(k < z.nx)
        def _():
            a1_copy(k, x).start()
            b1_copy(k, y).start()

        return 0

    lax.fori_loop(1, z.nx + 1, mine, 0)
    for i in range(hg):
        pending.append(core_copy("core_c", dc_ref, rc_c, i, other * hg + i))
    for k in range(1, z.nx):
        pending.extend([a1_copy(k, x), b1_copy(k, y)])

    total_a = ds_ref[c * hg + x]
    total_b = ds_ref[pl.ds(c * hg + z.nx, z.nx), quarter_of(x), :]
    for k in range(1, z.nx):
        source = on_x(z.nx - k)
        for one in s1_copies(k, source):
            one.wait_recv()
        total_a = total_a + r1sa[source]
        total_b = total_b + r1sb[source]
    sum_sa[...] = total_a
    sum_sb[...] = total_b

    def s2_copies(k, source):
        return (copy("s2a", sum_sa.at[quarter_of(on_y(k))], r2sa.at[source], k, source, at(yy=on_y(k))),
                copy("s2b", sum_sb.at[on_y(k)], r2sb.at[source], k, source, at(yy=on_y(k))))

    for k in range(1, z.ny):
        start(*s2_copies(k, y))
    part_a = sum_sa[quarter_of(y), :]
    part_b = sum_sb[y]
    for k in range(1, z.ny):
        source = on_y(z.ny - k)
        for one in s2_copies(k, source):
            one.wait_recv()
        part_a = part_a + r2sa[source]
        part_b = part_b + r2sb[source]
    us_ref[0:z.half] = part_a.reshape(z.half, 8, z.cap)
    us_ref[z.half:2 * z.half] = part_b.reshape(z.half, 8, z.cap)

    def s3_copy(k, source):
        return copy("s3", us_ref.at[on_z(k)], r3s.at[source], k, source, at(zz=on_z(k)))

    for k in z_order:
        start(s3_copy(k, zc))

    total_a = dc_ref[c * hg + x]
    for k in range(1, z.nx):
        source = on_x(z.nx - k)
        a1_copy(k, source).wait_recv()
        total_a = total_a + r1a[source]
    sums[0] = total_a

    def a2_copy(k, source):
        return copy("a2", sums.at[0, quarter_of(on_y(k))], r2a.at[source], k, source, at(yy=on_y(k)))

    for k in range(1, z.ny):
        start(a2_copy(k, y))
    total_b = dc_ref[c * hg + z.nx + y]
    for k in range(1, z.ny):
        source = on_y(z.ny - k)
        b1_copy(k, source).wait_recv()
        total_b = total_b + r1b[source]
    sums[1] = total_b

    def b2_copy(k, source):
        return copy("b2", sums.at[1, quarter_of(on_x(k))], r2b.at[source], k, source, at(xx=on_x(k)))

    for k in range(1, z.nx):
        start(b2_copy(k, x))

    part_a = sums[0, quarter_of(y), :]
    for k in range(1, z.ny):
        source = on_y(z.ny - k)
        a2_copy(k, source).wait_recv()
        part_a = part_a + r2a[source]
    u_ref[0:z.half] = part_a.reshape(z.half, 8, z.cap)
    part_b = sums[1, quarter_of(x), :]
    for k in range(1, z.nx):
        source = on_x(z.nx - k)
        b2_copy(k, source).wait_recv()
        part_b = part_b + r2b[source]
    u_ref[z.half:2 * z.half] = part_b.reshape(z.half, 8, z.cap)

    def z3_copy(k, source):
        return copy("z3", u_ref.at[on_z(k)], r3.at[source], k, source, at(zz=on_z(k)))

    for k in z_order:
        start(z3_copy(k, zc))
    dist_self = us_ref[zc]
    for k in range(1, z.nz):
        source = on_z(z.nz - k)
        s3_copy(k, source).wait_recv()
        dist_self = dist_self + r3s[source]
    dist_cross = u_ref[zc]
    for k in range(1, z.nz):
        source = on_z(z.nz - k)
        z3_copy(k, source).wait_recv()
        dist_cross = dist_cross + r3[source]

    way = zc // z.half
    member = (1 - way) * x + way * y
    sub = (1 - way) * y + way * x
    group = c * hg + way * z.nx + member
    block = sub * z.half + lax.rem(zc, z.half)
    size = sizes[group]
    row_at = (block * 8 + lax.broadcasted_iota(jnp.int32, (8, z.cap), 0)).astype(F32)
    col_at = lax.broadcasted_iota(jnp.int32, (8, z.cap), 1).astype(F32)
    mask = jnp.where((row_at < size) & (col_at < size), 1.0, 0.0)
    heights = [tab_ref[idx_ref[m]] for m in range(4)]
    weight_self, weight_cross, row_loss, pull = pair_terms(
        jnp.maximum(dist_self, 0.0), jnp.maximum(dist_cross, 0.0), mask, heights, z.latent)
    lanes = lax.broadcasted_iota(jnp.int32, (8, z.cap), 1)

    def with_row_term(weights, term):
        first = term.astype(BF16).astype(F32)
        second = (term - first).astype(BF16).astype(F32)
        third = term - first - second
        columns = jnp.where(lanes == z.cap - 3, first, jnp.where(lanes == z.cap - 2, second, third))
        return jnp.where(lanes < z.most, weights, columns)

    wf[group, block] = jnp.concatenate(
        [with_row_term(weight_self.astype(F32), pull), with_row_term(-weight_cross.astype(F32), row_loss / size)],
        axis=0).astype(BF16)

    def gz_copy(k, source):
        way_of = source // z.half
        group_of = c * hg + way_of * z.nx + (1 - way_of) * x + way_of * y
        block_of = ((1 - way_of) * y + way_of * x) * z.half + lax.rem(source, z.half)
        place = wf.at[group_of, block_of]
        return copy("gz", place, place, k, source, at(zz=on_z(k)))

    for k in z_order:
        start(gz_copy(k, zc))
    for k in range(1, z.nz):
        gz_copy(k, on_z(z.nz - k)).wait_recv()

    def g2a_copy(k, source):
        place = wf.at[c * hg + x, pl.ds(source * z.half, z.half)]
        return copy("g2a", place, place, k, source, at(yy=on_y(k)))

    def g2b_copy(k, source):
        place = wf.at[c * hg + z.nx + y, pl.ds(source * z.half, z.half)]
        return copy("g2b", place, place, k, source, at(xx=on_x(k)))

    for k in range(1, z.nx):
        start(g2a_copy(k, y))
        start(g2b_copy(k, x))

    def g1a_copy(k, source):
        place = wf.at[c * hg + source]
        return copy("g1a", place, place, k, source, at(xx=on_x(k)))

    def g1b_copy(k, source):
        place = wf.at[c * hg + z.nx + source]
        return copy("g1b", place, place, k, source, at(yy=on_y(k)))

    for k in range(1, z.ny):
        g2a_copy(k, on_y(z.ny - k)).wait_recv()
    for k in range(1, z.nx):
        start(g1a_copy(k, x))
    for k in range(1, z.nx):
        g2b_copy(k, on_x(z.nx - k)).wait_recv()
    for k in range(1, z.ny):
        start(g1b_copy(k, y))
    def gc_copy(way_of, core):
        place = wf.at[pl.ds(core * hg + way_of * z.nx, z.nx)]
        return copy("gc", place, place, way_of, way_of, at(cc=other))

    for k in range(1, z.nx):
        g1a_copy(k, on_x(z.nx - k)).wait_recv()
    start(gc_copy(0, c))
    for k in range(1, z.ny):
        g1b_copy(k, on_y(z.ny - k)).wait_recv()
    start(gc_copy(1, c))

    last = lax.broadcasted_iota(jnp.int32, (z.cap, z.cap), 1) >= z.most

    def force_of(groups):
        found = []
        for g in groups:
            held = wf[g].astype(F32).reshape(z.blocks, 2, 8, z.cap)
            to_self, to_cross = held[:, 0].reshape(z.cap, z.cap), held[:, 1].reshape(z.cap, z.cap)
            pulls = jnp.sum(jnp.where(last, to_self, 0.0), axis=1, keepdims=True)
            loss = jnp.sum(jnp.where(last, to_cross, 0.0), axis=0, keepdims=True)
            weights = jnp.concatenate([to_self, to_cross], axis=1).astype(BF16)
            values = xs[g]
            pulled = values[0:z.cap].astype(F32) * pulls + jnp.dot(weights, values, preferred_element_type=F32)
            force = pulled / sizes[g]
            high = force.astype(BF16)
            low = (force - high.astype(F32)).astype(BF16)
            found.append((loss, high, low))
        for g, (loss, high, low) in zip(groups, found):
            rows = pl.ds(pl.multiple_of(g * z.cap, z.cap), z.cap)
            losses[g] = loss
            fs[rows, 0:z.cols] = high
            fs[rows, z.cols:2 * z.cols] = low

    def forces(first):
        force_of([first + n for n in range(z.nx)])

    forces(c * hg)
    forces(c * hg + z.nx)
    for way_of in range(2):
        gc_copy(way_of, other).wait_recv()
        forces(other * hg + way_of * z.nx)

    l_ref[...] = jnp.sum(jnp.sum(losses[...], axis=0), axis=1, keepdims=True) / z.samples

    def out_copies(k, source):
        return (copy("out", qs.at[k], ql.at[source], k, source, at(yy=on_y(k))),
                copy("scale", scales.at[k], landed.at[source], k, source, at(yy=on_y(k))))

    parts = z.rows // z.lanes
    square = (z.lanes, z.lanes)
    same = lax.broadcasted_iota(jnp.int32, square, 0) == lax.broadcasted_iota(jnp.int32, square, 1)

    def unsorted(k):
        rows = pl.ds(pl.multiple_of(on_y(k) * z.rows, z.rows), z.rows)
        moved = jnp.dot(back_ref[rows, :], fs[...], preferred_element_type=F32)
        return moved[:, 0:z.cols] + moved[:, z.cols:2 * z.cols]

    def send_out(step, _):
        k = lax.rem(step + z.ny // 2 - 1, z.ny - 1) + 1
        force = unsorted(k)
        top = jnp.maximum(jnp.max(jnp.abs(force), axis=1, keepdims=True), 1e-33)
        qs[k] = jnp.round(force * (32767.0 / top)).astype(jnp.int32).astype(jnp.int16)
        unit = top / 32767.0
        for part in range(parts):
            spread = jnp.where(same, unit[part * z.lanes:(part + 1) * z.lanes], 0.0)
            scales[k, part:part + 1, :] = jnp.sum(spread, axis=0, keepdims=True)
        for one in out_copies(k, y):
            one.start()
        return 0

    scales[...] = jnp.zeros_like(scales)
    lax.fori_loop(0, z.ny - 1, send_out, 0)
    f_ref[:, own_cols] = unsorted(0)
    for k in order:
        source = on_y(z.ny - k)
        for one in out_copies(k, source):
            one.wait_recv()
        cols = pl.ds(pl.multiple_of(source * z.cols, z.cols), z.cols)
        for part in range(parts):
            rows = slice(part * z.lanes, (part + 1) * z.lanes)
            unit = jnp.sum(jnp.where(same, landed[source, part:part + 1, :], 0.0), axis=1, keepdims=True)
            f_ref[rows, cols] = ql[source, rows, :].astype(jnp.int32).astype(F32) * unit

    for k in range(1, z.ny):
        pending += out_copies(k, y)
    drain()


def sorted_path(z, student, teacher, bw_table, bw_index, group_ids):
    ids, count = exchanges(z)
    slots, hg = z.groups * z.cap, z.groups // 2
    quarter = z.cap // z.ny
    vmem, smem, anywhere = (pl.BlockSpec(memory_space=m) for m in (pltpu.VMEM, pltpu.SMEM, pl.ANY))
    force, loss, largest = pl.pallas_call(
        functools.partial(fused, z, ids),
        out_shape=(pltpu.VMEM((z.rows, z.tile), F32), jax.ShapeDtypeStruct((1, 1), F32),
                   jax.ShapeDtypeStruct((1, 1), jnp.int32)),
        in_specs=[anywhere, anywhere, vmem, smem, smem],
        out_specs=(vmem, vmem, vmem),
        scratch_shapes=[
            pltpu.VMEM((z.ny, z.rows, z.cols), BF16),
            pltpu.VMEM((z.ny, z.rows, z.cols), BF16),
            pltpu.VMEM((z.ny, slots, z.rows), BF16),
            pltpu.VMEM((z.samples, slots), BF16),
            pltpu.VMEM((slots, 2 * z.cols), F32),
            pltpu.VMEM((z.groups, 2 * z.cap, z.cols), BF16),
            pltpu.VMEM((z.groups, z.cap, 1), F32),
            pltpu.VMEM((z.groups, z.cap, z.cap), F32),
            pltpu.VMEM((z.groups, z.cap, z.cap), F32),
            pltpu.VMEM((hg, z.cap, z.cap), F32),
            pltpu.VMEM((hg, z.cap, z.cap), F32),
            pltpu.VMEM((z.nx, z.cap, z.cap), F32),
            pltpu.VMEM((z.nx, z.nx, quarter, z.cap), F32),
            pltpu.VMEM((z.ny, quarter, z.cap), F32),
            pltpu.VMEM((z.ny, quarter, z.cap), F32),
            pltpu.VMEM((z.cap, z.cap), F32),
            pltpu.VMEM((z.nx, quarter, z.cap), F32),
            pltpu.VMEM((z.nz, 8, z.cap), F32),
            pltpu.VMEM((z.nz, 8, z.cap), F32),
            pltpu.VMEM((z.nx, z.cap, z.cap), F32),
            pltpu.VMEM((z.ny, z.cap, z.cap), F32),
            pltpu.VMEM((2, z.cap, z.cap), F32),
            pltpu.VMEM((z.ny, quarter, z.cap), F32),
            pltpu.VMEM((z.nx, quarter, z.cap), F32),
            pltpu.VMEM((z.nz, 8, z.cap), F32),
            pltpu.VMEM((z.nz, 8, z.cap), F32),
            pltpu.VMEM((z.groups, z.blocks, 16, z.cap), BF16),
            pltpu.VMEM((1, z.samples), jnp.int32),
            pltpu.VMEM((1, z.samples), jnp.int32),
            pltpu.VMEM((z.samples, 1), jnp.int32),
            pltpu.VMEM((z.groups, 1, 1), F32),
            pltpu.VMEM((z.groups, 1, z.cap), F32),
            pltpu.VMEM((slots, 2 * z.cols), BF16),
            pltpu.VMEM((z.ny, z.rows, z.cols), jnp.int16),
            pltpu.VMEM((z.ny, z.rows, z.cols), jnp.int16),
            pltpu.VMEM((z.ny, 8, z.lanes), F32),
            pltpu.VMEM((z.ny, 8, z.lanes), F32),
            pltpu.SemaphoreType.DMA((count,)),
        ],
        compiler_params=pltpu.CompilerParams(
            collective_id=1, has_side_effects=True, vmem_limit_bytes=56 * 1024 * 1024),
        name="grouped",
    )(student, teacher, group_ids, bw_table, bw_index)
    return force, loss.reshape(()), largest.reshape(())


def gather_pair(z, block):
    y = lax.axis_index("pair")
    out = jnp.zeros((z.ny,) + block.shape, block.dtype)
    for k in range(z.ny):
        moved = lax.ppermute(block, "pair", [(i, (i + k) % z.ny) for i in range(z.ny)]) if k else block
        out = lax.dynamic_update_index_in_dim(out, moved, lax.rem(y + z.ny - k, z.ny), 0)
    return out.reshape((z.ny * block.shape[0],) + block.shape[1:])


def sum_over(array, axis, count):
    step = 1
    while step < count:
        array = array + lax.ppermute(array, axis, [(i, i ^ step) for i in range(count)])
        step *= 2
    return array


def dense_path(z, student, teacher, bw_table, bw_index, group_ids):
    students = gather_pair(z, student)
    teachers = gather_pair(z, teacher)
    both = jnp.concatenate([students, teachers], axis=0)
    wide = both.astype(F32)
    row_wide = student.astype(F32)
    norms = jnp.sum(wide * wide, axis=1)
    row_norms = jnp.sum(row_wide * row_wide, axis=1)
    gram = lax.dot_general(student, both, (((1,), (1,)), ((), ())), preferred_element_type=F32)
    part = row_norms[:, None] + norms[None, :] - 2.0 * gram
    dist = jnp.maximum(sum_over(part, "value", z.nx * z.nz * z.nc), 0.0)
    row_ids = lax.dynamic_slice_in_dim(group_ids, lax.axis_index("pair") * z.rows, z.rows)
    same = (row_ids[:, None] == group_ids[None, :]).astype(F32)
    sizes = jnp.sum(same, axis=1, keepdims=True)
    heights = bw_table[bw_index]
    weight_self, weight_cross, row_loss, pull = pair_terms(
        dist[:, :z.samples], dist[:, z.samples:], same, [heights[m] for m in range(4)], z.latent)
    loss = sum_over(jnp.broadcast_to(jnp.sum(row_loss / sizes), (8, 128)), "pair", z.ny)[0, 0] / z.samples
    pulled = row_wide * pull
    pulled = pulled + jnp.dot(weight_self, students, preferred_element_type=F32)
    pulled = pulled - jnp.dot(weight_cross, teachers, preferred_element_type=F32)
    return pulled / sizes, loss


def build(mesh, z):
    def step(student, teacher, bw_table, bw_index, group_ids):
        force, loss, largest = sorted_path(z, student, teacher, bw_table, bw_index, group_ids)
        return lax.cond(
            largest <= z.most,
            lambda *held: held[:2],
            lambda *held: dense_path(z, *held[2:]),
            force, loss, student, teacher, bw_table, bw_index, group_ids)

    return jax.shard_map(
        step, mesh=mesh,
        in_specs=(P("pair", "value"), P("pair", "value"), P(None), P(None), P(None)),
        out_specs=(P("pair", "value"), P()),
        check_vma=False)


def solution(mesh):
    return build(mesh, Sizes(ny=4, nx=4, nz=8, nc=2, samples=1536, tile=1024, latent=65536))
```

```python
import functools

import jax
import jax.numpy as jnp
from jax import lax
from jax.experimental import pallas as pl
from jax.experimental.pallas import tpu as pltpu
from jax.sharding import PartitionSpec as P

MESH = pl.DeviceIdType.MESH
F32, BF16 = jnp.float32, jnp.bfloat16


TOGETHER = 4


class Sizes:
    def __init__(self, ny, nx, nz, nc, samples, tile, latent):
        self.ny, self.nx, self.nz, self.nc = ny, nx, nz, nc
        self.samples, self.tile, self.latent = samples, tile, float(latent)
        self.rows = samples // ny
        self.cols = tile // ny
        self.groups = 2 * nc * nx
        self.half = nz // 2
        self.cap = 8 * ny * self.half
        self.blocks = self.cap // 8
        self.most = self.cap - 3
        self.lanes = min(128, self.rows)


def pair_terms(dist_self, dist_cross, mask, heights, latent):
    kern_self = jnp.zeros_like(dist_self)
    kern_cross = jnp.zeros_like(dist_cross)
    weight_self = jnp.zeros_like(dist_self)
    weight_cross = jnp.zeros_like(dist_cross)
    count = len(heights)
    for height in heights:
        width_now = height * latent
        exp_self = jnp.exp(-dist_self / width_now)
        exp_cross = jnp.exp(-dist_cross / width_now)
        kern_self = kern_self + exp_self
        kern_cross = kern_cross + exp_cross
        weight_self = weight_self + exp_self / height
        weight_cross = weight_cross + exp_cross / height
    kern_self = kern_self / count * mask
    kern_cross = kern_cross / count * mask
    weight_self = weight_self / count * mask
    weight_cross = weight_cross / count * mask
    row_loss = jnp.sum(kern_self - 2.0 * kern_cross, axis=1, keepdims=True)
    pull = jnp.sum(weight_cross, axis=1, keepdims=True) - jnp.sum(weight_self, axis=1, keepdims=True)
    return weight_self.astype(BF16), weight_cross.astype(BF16), row_loss, pull


class Pool:
    def __init__(self):
        self.total = 0

    def take(self, count):
        first = self.total
        self.total += count
        return first

    def pair(self, count):
        return self.take(count), self.take(count)


def exchanges(z):
    pool = Pool()
    sizes = {
        "in_s": z.ny, "in_t": z.ny, "core_s": z.groups // 2, "core_c": z.groups // 2, "s1a": z.nx, "s1b": z.nx, "s2a": z.ny, "s2b": z.ny, "s3": z.nz,
        "a1": z.nx, "b1": z.ny, "a2": z.ny, "b2": z.nx, "z3": z.nz,
        "gz": z.nz, "g2a": z.ny, "g2b": z.nx, "g1a": z.nx, "g1b": z.ny, "gc": 2, "out": z.ny, "scale": z.ny, "own": 2,
    }
    return {name: pool.pair(count) for name, count in sizes.items()}, pool.total


def fused(z, ids, s_ref, t_ref, g_ref, tab_ref, idx_ref, f_ref, l_ref, most_ref,
          xin_s, xin_t, sort_ref, back_ref, xacc, xs, norms, ds_ref, dc_ref, rc_s, rc_c, r1sa, r1sb, r2sa, r2sb, sum_sa, sum_sb,
          us_ref, r3s, r1a, r1b, sums, r2a, r2b, u_ref, r3, wf, gr_ref, row_place, col_place, sizes, losses, fs, qs, ql, scales, landed, sems):
    y, v = lax.axis_index("pair"), lax.axis_index("value")
    c = lax.rem(v, z.nc)
    x = lax.rem(v // z.nc, z.nx)
    zc = v // (z.nc * z.nx)
    other = 1 - c
    hg = z.groups // 2
    quarter = z.cap // z.ny

    def at(yy=None, xx=None, zz=None, cc=None):
        yy = y if yy is None else yy
        xx = x if xx is None else xx
        zz = zc if zz is None else zz
        cc = c if cc is None else cc
        return (yy, (zz * z.nx + xx) * z.nc + cc)

    def on_y(k):
        return lax.rem(y + k, z.ny)

    def on_x(k):
        return lax.rem(x + k, z.nx)

    def on_z(k):
        return lax.rem(zc + k, z.nz)

    z_order = sorted(range(1, z.nz), key=lambda k: -min(k, z.nz - k))
    barrier = pltpu.get_barrier_semaphore()
    peers = [at(yy=on_y(k)) for k in range(1, z.ny)] + [at(xx=on_x(k)) for k in range(1, z.nx)]
    peers += [at(zz=on_z(k)) for k in range(1, z.nz)] + [at(cc=other)]
    for peer in peers:
        pl.semaphore_signal(barrier, inc=1, device_id=peer, device_id_type=MESH)
    pl.semaphore_wait(barrier, len(peers))

    def copy(name, src, dst, send, recv, device):
        first_send, first_recv = ids[name]
        return pltpu.make_async_remote_copy(
            src_ref=src, dst_ref=dst, send_sem=sems.at[first_send + send], recv_sem=sems.at[first_recv + recv],
            device_id=device, device_id_type=MESH)

    pending = []

    def drain():
        for one in pending:
            one.wait_send()

    order = sorted(range(1, z.ny), key=lambda k: min(k, z.ny - k))

    def in_copy(name, ref, land, k, source, target):
        cols = pl.ds(pl.multiple_of(target * z.cols, z.cols), z.cols)
        return copy(name, ref.at[:, cols], land.at[source], k, source, at(yy=on_y(k)))

    for k in order:
        in_copy("in_s", s_ref, xin_s, k, y, on_y(k)).start()
        pending.append(in_copy("in_t", t_ref, xin_t, k, y, on_y(k)))
    own_cols = pl.ds(pl.multiple_of(y * z.cols, z.cols), z.cols)
    own_s = pltpu.make_async_copy(s_ref.at[:, own_cols], xin_s.at[y], sems.at[ids["own"][0]])
    own_t = pltpu.make_async_copy(t_ref.at[:, own_cols], xin_t.at[y], sems.at[ids["own"][0] + 1])
    own_s.start()
    own_t.start()

    gr_ref[...] = g_ref[...].reshape(1, z.samples)
    slots = z.groups * z.cap
    eye = lax.broadcasted_iota(jnp.int32, (z.cap, z.cap), 0) == lax.broadcasted_iota(jnp.int32, (z.cap, z.cap), 1)
    above = lax.broadcasted_iota(jnp.int32, (z.cap, z.cap), 0) < lax.broadcasted_iota(jnp.int32, (z.cap, z.cap), 1)
    above = jnp.where(above, 1.0, 0.0).astype(BF16)

    def find_places(step, seen):
        first = pl.multiple_of(step * z.cap, z.cap)
        ids_row = gr_ref[:, pl.ds(first, z.cap)]
        hit = jnp.where(lax.broadcasted_iota(jnp.int32, (z.groups, z.cap), 0) == ids_row, 1.0, 0.0)
        before = seen + jnp.dot(hit.astype(BF16), above, preferred_element_type=F32)
        place = (ids_row * z.cap).astype(F32) + jnp.sum(hit * before, axis=0, keepdims=True)
        row_place[:, pl.ds(first, z.cap)] = place.astype(jnp.int32)
        turned = jnp.sum(jnp.where(eye, place, 0.0), axis=1, keepdims=True)
        col_place[pl.ds(first, z.cap), :] = turned.astype(jnp.int32)
        return seen + jnp.sum(hit, axis=1, keepdims=True)

    held = lax.fori_loop(0, z.samples // z.cap, find_places, jnp.zeros((z.groups, 1), F32))
    sizes[...] = jnp.broadcast_to(held[:, :, None], sizes.shape)
    most_ref[...] = jnp.max(held, axis=0, keepdims=True).astype(jnp.int32)

    for part in range(z.ny):
        def fill_sort(step, _):
            first = pl.multiple_of(step * z.cap, z.cap)
            slot = first + lax.broadcasted_iota(jnp.int32, (z.cap, z.rows), 0)
            place = row_place[:, part * z.rows:(part + 1) * z.rows]
            sort_ref[part, pl.ds(first, z.cap), :] = jnp.where(slot == place, 1.0, 0.0).astype(BF16)
            return 0

        lax.fori_loop(0, z.groups, fill_sort, 0)

    for k in order:
        in_copy("in_s", s_ref, xin_s, k, y, on_y(k)).wait_send()
        in_copy("in_t", t_ref, xin_t, k, y, on_y(k)).start()

    own_s.wait()
    own_t.wait()
    xacc[...] = jnp.zeros_like(xacc)
    scales[...] = jnp.zeros_like(scales)
    tall_rows = slots // 4

    def sort_from(source, values, first_col):
        def body(step, _):
            first = pl.multiple_of(step * tall_rows, tall_rows)
            place = sort_ref[source, pl.ds(first, tall_rows), :]
            xacc[pl.ds(first, tall_rows), first_col:first_col + z.cols] += jnp.dot(
                place, values[source], preferred_element_type=F32)
            return 0

        lax.fori_loop(0, 4, body, 0)

    sort_from(y, xin_s, 0)
    for k in order:
        source = on_y(z.ny - k)
        in_copy("in_s", s_ref, xin_s, k, source, on_y(k)).wait_recv()
        sort_from(source, xin_s, 0)

    def rows_of(group):
        return pl.ds(pl.multiple_of(group * z.cap, z.cap), z.cap)

    outer = (((1,), (1,)), ((), ()))

    def distances_self(groups):
        found = []
        for group in groups:
            mine = xacc[rows_of(group), 0:z.cols].astype(BF16)
            found.append((mine, lax.dot_general(mine, mine, outer, preferred_element_type=F32)))
        parts = []
        for mine, gram in found:
            diagonal = jnp.where(eye, gram, 0.0)
            norm_col = jnp.sum(diagonal, axis=1, keepdims=True)
            parts.append((norm_col, norm_col + jnp.sum(diagonal, axis=0, keepdims=True) - 2.0 * gram))
        for group, (mine, _), (norm_col, part) in zip(groups, found, parts):
            xs[group, 0:z.cap] = mine
            norms[group] = norm_col
            ds_ref[group] = part

    def distances_cross(groups):
        found = []
        for group in groups:
            theirs = xacc[rows_of(group), z.cols:2 * z.cols].astype(BF16)
            both = jnp.concatenate([xs[group, 0:z.cap], theirs], axis=0)
            found.append((theirs, lax.dot_general(both, theirs, outer, preferred_element_type=F32)))
        parts = []
        for group, (theirs, gram) in zip(groups, found):
            norm_row = jnp.sum(jnp.where(eye, gram[z.cap:2 * z.cap], 0.0), axis=0, keepdims=True)
            parts.append(norms[group] + norm_row - 2.0 * gram[0:z.cap])
        for group, (theirs, _), part in zip(groups, found, parts):
            xs[group, z.cap:2 * z.cap] = theirs
            dc_ref[group] = part

    def core_copy(name, part, land, i, group):
        return copy(name, part.at[group], land.at[i], i, i, at(cc=other))

    def quarter_of(k):
        return pl.ds(pl.multiple_of(k * quarter, quarter), quarter)

    def self_to_other(i, _):
        now = [TOGETHER * i + n for n in range(TOGETHER)]
        distances_self([other * hg + n for n in now])
        for n in now:
            core_copy("core_s", ds_ref, rc_s, n, other * hg + n).start()
        return 0

    lax.fori_loop(0, hg // TOGETHER, self_to_other, 0)

    def self_mine(i, _):
        now = [TOGETHER * i + n for n in range(TOGETHER)]
        distances_self([c * hg + n for n in now])
        for n in now:
            core_copy("core_s", ds_ref, rc_s, n, c * hg + n).wait_recv()
            ds_ref[c * hg + n] += rc_s[n]
        return 0

    lax.fori_loop(0, hg // TOGETHER, self_mine, 0)

    def s1_copies(k, source):
        second = ds_ref.at[pl.ds(c * hg + z.nx, z.nx), quarter_of(on_x(k))]
        return (copy("s1a", ds_ref.at[c * hg + on_x(k)], r1sa.at[source], k, source, at(xx=on_x(k))),
                copy("s1b", second, r1sb.at[source], k, source, at(xx=on_x(k))))

    def start(*copies):
        for one in copies:
            one.start()
            pending.append(one)

    for k in range(1, z.nx):
        start(*s1_copies(k, x))
    for i in range(hg):
        pending.append(core_copy("core_s", ds_ref, rc_s, i, other * hg + i))

    def fill_back(step, _):
        first = pl.multiple_of(step * z.cap, z.cap)
        slot = lax.broadcasted_iota(jnp.int32, (z.cap, slots), 1)
        back_ref[pl.ds(first, z.cap), :] = jnp.where(slot == col_place[pl.ds(first, z.cap), :], 1.0, 0.0).astype(BF16)
        return 0

    lax.fori_loop(0, z.samples // z.cap, fill_back, 0)

    sort_from(y, xin_t, z.cols)
    for k in order:
        source = on_y(z.ny - k)
        in_copy("in_t", t_ref, xin_t, k, source, on_y(k)).wait_recv()
        sort_from(source, xin_t, z.cols)

    def cross_to_other(i, _):
        now = [TOGETHER * i + n for n in range(TOGETHER)]
        distances_cross([other * hg + n for n in now])
        for n in now:
            core_copy("core_c", dc_ref, rc_c, n, other * hg + n).start()
        return 0

    lax.fori_loop(0, hg // TOGETHER, cross_to_other, 0)

    def a1_copy(k, source):
        return copy("a1", dc_ref.at[c * hg + on_x(k)], r1a.at[source], k, source, at(xx=on_x(k)))

    def b1_copy(k, source):
        return copy("b1", dc_ref.at[c * hg + z.nx + on_y(k)], r1b.at[source], k, source, at(yy=on_y(k)))

    def mine(k, _):
        now = (on_x(k), z.nx + on_y(k))
        distances_cross([c * hg + i for i in now])
        for i in now:
            core_copy("core_c", dc_ref, rc_c, i, c * hg + i).wait_recv()
            dc_ref[c * hg + i] += rc_c[i]

        @pl.when(k < z.nx)
        def _():
            a1_copy(k, x).start()
            b1_copy(k, y).start()

        return 0

    lax.fori_loop(1, z.nx + 1, mine, 0)
    for i in range(hg):
        pending.append(core_copy("core_c", dc_ref, rc_c, i, other * hg + i))
    for k in range(1, z.nx):
        pending.extend([a1_copy(k, x), b1_copy(k, y)])

    total_a = ds_ref[c * hg + x]
    total_b = ds_ref[pl.ds(c * hg + z.nx, z.nx), quarter_of(x), :]
    for k in range(1, z.nx):
        source = on_x(z.nx - k)
        for one in s1_copies(k, source):
            one.wait_recv()
        total_a = total_a + r1sa[source]
        total_b = total_b + r1sb[source]
    sum_sa[...] = total_a
    sum_sb[...] = total_b

    def s2_copies(k, source):
        return (copy("s2a", sum_sa.at[quarter_of(on_y(k))], r2sa.at[source], k, source, at(yy=on_y(k))),
                copy("s2b", sum_sb.at[on_y(k)], r2sb.at[source], k, source, at(yy=on_y(k))))

    for k in range(1, z.ny):
        start(*s2_copies(k, y))
    part_a = sum_sa[quarter_of(y), :]
    part_b = sum_sb[y]
    for k in range(1, z.ny):
        source = on_y(z.ny - k)
        for one in s2_copies(k, source):
            one.wait_recv()
        part_a = part_a + r2sa[source]
        part_b = part_b + r2sb[source]
    us_ref[0:z.half] = part_a.reshape(z.half, 8, z.cap)
    us_ref[z.half:2 * z.half] = part_b.reshape(z.half, 8, z.cap)

    def s3_copy(k, source):
        return copy("s3", us_ref.at[on_z(k)], r3s.at[source], k, source, at(zz=on_z(k)))

    for k in z_order:
        start(s3_copy(k, zc))

    total_a = dc_ref[c * hg + x]
    for k in range(1, z.nx):
        source = on_x(z.nx - k)
        a1_copy(k, source).wait_recv()
        total_a = total_a + r1a[source]
    sums[0] = total_a

    def a2_copy(k, source):
        return copy("a2", sums.at[0, quarter_of(on_y(k))], r2a.at[source], k, source, at(yy=on_y(k)))

    for k in range(1, z.ny):
        start(a2_copy(k, y))
    total_b = dc_ref[c * hg + z.nx + y]
    for k in range(1, z.ny):
        source = on_y(z.ny - k)
        b1_copy(k, source).wait_recv()
        total_b = total_b + r1b[source]
    sums[1] = total_b

    def b2_copy(k, source):
        return copy("b2", sums.at[1, quarter_of(on_x(k))], r2b.at[source], k, source, at(xx=on_x(k)))

    for k in range(1, z.nx):
        start(b2_copy(k, x))

    part_a = sums[0, quarter_of(y), :]
    for k in range(1, z.ny):
        source = on_y(z.ny - k)
        a2_copy(k, source).wait_recv()
        part_a = part_a + r2a[source]
    u_ref[0:z.half] = part_a.reshape(z.half, 8, z.cap)
    part_b = sums[1, quarter_of(x), :]
    for k in range(1, z.nx):
        source = on_x(z.nx - k)
        b2_copy(k, source).wait_recv()
        part_b = part_b + r2b[source]
    u_ref[z.half:2 * z.half] = part_b.reshape(z.half, 8, z.cap)

    def z3_copy(k, source):
        return copy("z3", u_ref.at[on_z(k)], r3.at[source], k, source, at(zz=on_z(k)))

    for k in z_order:
        start(z3_copy(k, zc))
    dist_self = us_ref[zc]
    for k in range(1, z.nz):
        source = on_z(z.nz - k)
        s3_copy(k, source).wait_recv()
        dist_self = dist_self + r3s[source]
    dist_cross = u_ref[zc]
    for k in range(1, z.nz):
        source = on_z(z.nz - k)
        z3_copy(k, source).wait_recv()
        dist_cross = dist_cross + r3[source]

    way = zc // z.half
    member = (1 - way) * x + way * y
    sub = (1 - way) * y + way * x
    group = c * hg + way * z.nx + member
    block = sub * z.half + lax.rem(zc, z.half)
    size = sizes[group]
    row_at = (block * 8 + lax.broadcasted_iota(jnp.int32, (8, z.cap), 0)).astype(F32)
    col_at = lax.broadcasted_iota(jnp.int32, (8, z.cap), 1).astype(F32)
    mask = jnp.where((row_at < size) & (col_at < size), 1.0, 0.0)
    heights = [tab_ref[idx_ref[m]] for m in range(4)]
    weight_self, weight_cross, row_loss, pull = pair_terms(
        jnp.maximum(dist_self, 0.0), jnp.maximum(dist_cross, 0.0), mask, heights, z.latent)
    lanes = lax.broadcasted_iota(jnp.int32, (8, z.cap), 1)

    def with_row_term(weights, term):
        first = term.astype(BF16).astype(F32)
        second = (term - first).astype(BF16).astype(F32)
        third = term - first - second
        columns = jnp.where(lanes == z.cap - 3, first, jnp.where(lanes == z.cap - 2, second, third))
        return jnp.where(lanes < z.most, weights, columns)

    wf[group, block] = jnp.concatenate(
        [with_row_term(weight_self.astype(F32), pull), with_row_term(-weight_cross.astype(F32), row_loss / size)],
        axis=0).astype(BF16)

    def gz_copy(k, source):
        way_of = source // z.half
        group_of = c * hg + way_of * z.nx + (1 - way_of) * x + way_of * y
        block_of = ((1 - way_of) * y + way_of * x) * z.half + lax.rem(source, z.half)
        place = wf.at[group_of, block_of]
        return copy("gz", place, place, k, source, at(zz=on_z(k)))

    for k in z_order:
        start(gz_copy(k, zc))
    for k in range(1, z.nz):
        gz_copy(k, on_z(z.nz - k)).wait_recv()

    def g2a_copy(k, source):
        place = wf.at[c * hg + x, pl.ds(source * z.half, z.half)]
        return copy("g2a", place, place, k, source, at(yy=on_y(k)))

    def g2b_copy(k, source):
        place = wf.at[c * hg + z.nx + y, pl.ds(source * z.half, z.half)]
        return copy("g2b", place, place, k, source, at(xx=on_x(k)))

    for k in range(1, z.nx):
        start(g2a_copy(k, y))
        start(g2b_copy(k, x))

    def g1a_copy(k, source):
        place = wf.at[c * hg + source]
        return copy("g1a", place, place, k, source, at(xx=on_x(k)))

    def g1b_copy(k, source):
        place = wf.at[c * hg + z.nx + source]
        return copy("g1b", place, place, k, source, at(yy=on_y(k)))

    for k in range(1, z.ny):
        g2a_copy(k, on_y(z.ny - k)).wait_recv()
    for k in range(1, z.nx):
        start(g1a_copy(k, x))
    for k in range(1, z.nx):
        g2b_copy(k, on_x(z.nx - k)).wait_recv()
    for k in range(1, z.ny):
        start(g1b_copy(k, y))
    def gc_copy(way_of, core):
        place = wf.at[pl.ds(core * hg + way_of * z.nx, z.nx)]
        return copy("gc", place, place, way_of, way_of, at(cc=other))

    for k in range(1, z.nx):
        g1a_copy(k, on_x(z.nx - k)).wait_recv()
    start(gc_copy(0, c))
    for k in range(1, z.ny):
        g1b_copy(k, on_y(z.ny - k)).wait_recv()
    start(gc_copy(1, c))

    last = lax.broadcasted_iota(jnp.int32, (z.cap, z.cap), 1) >= z.most

    def force_of(groups):
        found = []
        for g in groups:
            held = wf[g].astype(F32).reshape(z.blocks, 2, 8, z.cap)
            to_self, to_cross = held[:, 0].reshape(z.cap, z.cap), held[:, 1].reshape(z.cap, z.cap)
            pulls = jnp.sum(jnp.where(last, to_self, 0.0), axis=1, keepdims=True)
            loss = jnp.sum(jnp.where(last, to_cross, 0.0), axis=0, keepdims=True)
            weights = jnp.concatenate([to_self, to_cross], axis=1).astype(BF16)
            values = xs[g]
            pulled = values[0:z.cap].astype(F32) * pulls + jnp.dot(weights, values, preferred_element_type=F32)
            force = pulled / sizes[g]
            high = force.astype(BF16)
            low = (force - high.astype(F32)).astype(BF16)
            found.append((loss, high, low))
        for g, (loss, high, low) in zip(groups, found):
            rows = pl.ds(pl.multiple_of(g * z.cap, z.cap), z.cap)
            losses[g] = loss
            fs[rows, 0:z.cols] = high
            fs[rows, z.cols:2 * z.cols] = low

    def forces(first):
        force_of([first + n for n in range(z.nx)])

    forces(c * hg)
    forces(c * hg + z.nx)
    for way_of in range(2):
        gc_copy(way_of, other).wait_recv()
        forces(other * hg + way_of * z.nx)

    def out_copies(k, source):
        return (copy("out", qs.at[k], ql.at[source], k, source, at(yy=on_y(k))),
                copy("scale", scales.at[k], landed.at[source], k, source, at(yy=on_y(k))))

    parts = z.rows // z.lanes
    square = (z.lanes, z.lanes)
    same = lax.broadcasted_iota(jnp.int32, square, 0) == lax.broadcasted_iota(jnp.int32, square, 1)

    def unsorted(k):
        rows = pl.ds(pl.multiple_of(on_y(k) * z.rows, z.rows), z.rows)
        moved = jnp.dot(back_ref[rows, :], fs[...], preferred_element_type=F32)
        return moved[:, 0:z.cols] + moved[:, z.cols:2 * z.cols]

    def send_out(step, _):
        k = lax.rem(step + z.ny // 2 - 1, z.ny - 1) + 1
        force = unsorted(k)
        top = jnp.maximum(jnp.max(jnp.abs(force), axis=1, keepdims=True), 1e-33)
        qs[k] = jnp.round(force * (32767.0 / top)).astype(jnp.int32).astype(jnp.int16)
        unit = top / 32767.0
        for part in range(parts):
            spread = jnp.where(same, unit[part * z.lanes:(part + 1) * z.lanes], 0.0)
            scales[k, part:part + 1, :] = jnp.sum(spread, axis=0, keepdims=True)
        for one in out_copies(k, y):
            one.start()
        return 0

    lax.fori_loop(0, z.ny - 1, send_out, 0)
    f_ref[:, own_cols] = unsorted(0)
    l_ref[...] = jnp.sum(jnp.sum(losses[...], axis=0), axis=1, keepdims=True) / z.samples
    drain()
    for k in order:
        source = on_y(z.ny - k)
        for one in out_copies(k, source):
            one.wait_recv()
        cols = pl.ds(pl.multiple_of(source * z.cols, z.cols), z.cols)
        for part in range(parts):
            rows = slice(part * z.lanes, (part + 1) * z.lanes)
            unit = jnp.sum(jnp.where(same, landed[source, part:part + 1, :], 0.0), axis=1, keepdims=True)
            f_ref[rows, cols] = ql[source, rows, :].astype(jnp.int32).astype(F32) * unit

    for k in range(1, z.ny):
        for one in out_copies(k, y):
            one.wait_send()


def sorted_path(z, student, teacher, bw_table, bw_index, group_ids):
    ids, count = exchanges(z)
    slots, hg = z.groups * z.cap, z.groups // 2
    quarter = z.cap // z.ny
    vmem, smem, anywhere = (pl.BlockSpec(memory_space=m) for m in (pltpu.VMEM, pltpu.SMEM, pl.ANY))
    force, loss, largest = pl.pallas_call(
        functools.partial(fused, z, ids),
        out_shape=(pltpu.VMEM((z.rows, z.tile), F32), jax.ShapeDtypeStruct((1, 1), F32),
                   jax.ShapeDtypeStruct((1, 1), jnp.int32)),
        in_specs=[anywhere, anywhere, vmem, smem, smem],
        out_specs=(vmem, vmem, vmem),
        scratch_shapes=[
            pltpu.VMEM((z.ny, z.rows, z.cols), BF16),
            pltpu.VMEM((z.ny, z.rows, z.cols), BF16),
            pltpu.VMEM((z.ny, slots, z.rows), BF16),
            pltpu.VMEM((z.samples, slots), BF16),
            pltpu.VMEM((slots, 2 * z.cols), F32),
            pltpu.VMEM((z.groups, 2 * z.cap, z.cols), BF16),
            pltpu.VMEM((z.groups, z.cap, 1), F32),
            pltpu.VMEM((z.groups, z.cap, z.cap), F32),
            pltpu.VMEM((z.groups, z.cap, z.cap), F32),
            pltpu.VMEM((hg, z.cap, z.cap), F32),
            pltpu.VMEM((hg, z.cap, z.cap), F32),
            pltpu.VMEM((z.nx, z.cap, z.cap), F32),
            pltpu.VMEM((z.nx, z.nx, quarter, z.cap), F32),
            pltpu.VMEM((z.ny, quarter, z.cap), F32),
            pltpu.VMEM((z.ny, quarter, z.cap), F32),
            pltpu.VMEM((z.cap, z.cap), F32),
            pltpu.VMEM((z.nx, quarter, z.cap), F32),
            pltpu.VMEM((z.nz, 8, z.cap), F32),
            pltpu.VMEM((z.nz, 8, z.cap), F32),
            pltpu.VMEM((z.nx, z.cap, z.cap), F32),
            pltpu.VMEM((z.ny, z.cap, z.cap), F32),
            pltpu.VMEM((2, z.cap, z.cap), F32),
            pltpu.VMEM((z.ny, quarter, z.cap), F32),
            pltpu.VMEM((z.nx, quarter, z.cap), F32),
            pltpu.VMEM((z.nz, 8, z.cap), F32),
            pltpu.VMEM((z.nz, 8, z.cap), F32),
            pltpu.VMEM((z.groups, z.blocks, 16, z.cap), BF16),
            pltpu.VMEM((1, z.samples), jnp.int32),
            pltpu.VMEM((1, z.samples), jnp.int32),
            pltpu.VMEM((z.samples, 1), jnp.int32),
            pltpu.VMEM((z.groups, 1, 1), F32),
            pltpu.VMEM((z.groups, 1, z.cap), F32),
            pltpu.VMEM((slots, 2 * z.cols), BF16),
            pltpu.VMEM((z.ny, z.rows, z.cols), jnp.int16),
            pltpu.VMEM((z.ny, z.rows, z.cols), jnp.int16),
            pltpu.VMEM((z.ny, 8, z.lanes), F32),
            pltpu.VMEM((z.ny, 8, z.lanes), F32),
            pltpu.SemaphoreType.DMA((count,)),
        ],
        compiler_params=pltpu.CompilerParams(
            collective_id=1, has_side_effects=True, vmem_limit_bytes=56 * 1024 * 1024),
        name="grouped",
    )(student, teacher, group_ids, bw_table, bw_index)
    return force, loss.reshape(()), largest.reshape(())


def gather_pair(z, block):
    y = lax.axis_index("pair")
    out = jnp.zeros((z.ny,) + block.shape, block.dtype)
    for k in range(z.ny):
        moved = lax.ppermute(block, "pair", [(i, (i + k) % z.ny) for i in range(z.ny)]) if k else block
        out = lax.dynamic_update_index_in_dim(out, moved, lax.rem(y + z.ny - k, z.ny), 0)
    return out.reshape((z.ny * block.shape[0],) + block.shape[1:])


def sum_over(array, axis, count):
    step = 1
    while step < count:
        array = array + lax.ppermute(array, axis, [(i, i ^ step) for i in range(count)])
        step *= 2
    return array


def dense_path(z, student, teacher, bw_table, bw_index, group_ids):
    students = gather_pair(z, student)
    teachers = gather_pair(z, teacher)
    both = jnp.concatenate([students, teachers], axis=0)
    wide = both.astype(F32)
    row_wide = student.astype(F32)
    norms = jnp.sum(wide * wide, axis=1)
    row_norms = jnp.sum(row_wide * row_wide, axis=1)
    gram = lax.dot_general(student, both, (((1,), (1,)), ((), ())), preferred_element_type=F32)
    part = row_norms[:, None] + norms[None, :] - 2.0 * gram
    dist = jnp.maximum(sum_over(part, "value", z.nx * z.nz * z.nc), 0.0)
    row_ids = lax.dynamic_slice_in_dim(group_ids, lax.axis_index("pair") * z.rows, z.rows)
    same = (row_ids[:, None] == group_ids[None, :]).astype(F32)
    sizes = jnp.sum(same, axis=1, keepdims=True)
    heights = bw_table[bw_index]
    weight_self, weight_cross, row_loss, pull = pair_terms(
        dist[:, :z.samples], dist[:, z.samples:], same, [heights[m] for m in range(4)], z.latent)
    loss = sum_over(jnp.broadcast_to(jnp.sum(row_loss / sizes), (8, 128)), "pair", z.ny)[0, 0] / z.samples
    pulled = row_wide * pull
    pulled = pulled + jnp.dot(weight_self, students, preferred_element_type=F32)
    pulled = pulled - jnp.dot(weight_cross, teachers, preferred_element_type=F32)
    return pulled / sizes, loss


def build(mesh, z):
    def step(student, teacher, bw_table, bw_index, group_ids):
        force, loss, largest = sorted_path(z, student, teacher, bw_table, bw_index, group_ids)
        return lax.cond(
            largest <= z.most,
            lambda *held: held[:2],
            lambda *held: dense_path(z, *held[2:]),
            force, loss, student, teacher, bw_table, bw_index, group_ids)

    return jax.shard_map(
        step, mesh=mesh,
        in_specs=(P("pair", "value"), P("pair", "value"), P(None), P(None), P(None)),
        out_specs=(P("pair", "value"), P()),
        check_vma=False)


def solution(mesh):
    return build(mesh, Sizes(ny=4, nx=4, nz=8, nc=2, samples=1536, tile=1024, latent=65536))
```

```python
import functools

import jax
import jax.numpy as jnp
from jax import lax
from jax.experimental import pallas as pl
from jax.experimental.pallas import tpu as pltpu
from jax.sharding import PartitionSpec as P

MESH = pl.DeviceIdType.MESH
F32, BF16 = jnp.float32, jnp.bfloat16


TOGETHER = 4


class Sizes:
    def __init__(self, ny, nx, nz, nc, samples, tile, latent):
        self.ny, self.nx, self.nz, self.nc = ny, nx, nz, nc
        self.samples, self.tile, self.latent = samples, tile, float(latent)
        self.rows = samples // ny
        self.cols = tile // ny
        self.groups = 2 * nc * nx
        self.half = nz // 2
        self.cap = 8 * ny * self.half
        self.blocks = self.cap // 8
        self.most = self.cap - 3
        self.lanes = min(128, self.rows)


def pair_terms(dist_self, dist_cross, mask, heights, latent):
    kern_self = jnp.zeros_like(dist_self)
    kern_cross = jnp.zeros_like(dist_cross)
    weight_self = jnp.zeros_like(dist_self)
    weight_cross = jnp.zeros_like(dist_cross)
    count = len(heights)
    for height in heights:
        width_now = height * latent
        exp_self = jnp.exp(-dist_self / width_now)
        exp_cross = jnp.exp(-dist_cross / width_now)
        kern_self = kern_self + exp_self
        kern_cross = kern_cross + exp_cross
        weight_self = weight_self + exp_self / height
        weight_cross = weight_cross + exp_cross / height
    kern_self = kern_self / count * mask
    kern_cross = kern_cross / count * mask
    weight_self = weight_self / count * mask
    weight_cross = weight_cross / count * mask
    row_loss = jnp.sum(kern_self - 2.0 * kern_cross, axis=1, keepdims=True)
    pull = jnp.sum(weight_cross, axis=1, keepdims=True) - jnp.sum(weight_self, axis=1, keepdims=True)
    return weight_self.astype(BF16), weight_cross.astype(BF16), row_loss, pull


class Pool:
    def __init__(self):
        self.total = 0

    def take(self, count):
        first = self.total
        self.total += count
        return first

    def pair(self, count):
        return self.take(count), self.take(count)


def exchanges(z):
    pool = Pool()
    sizes = {
        "in_s": z.ny, "in_t": z.ny, "core_s": z.groups // 2, "core_c": z.groups // 2, "s1a": z.nx, "s1b": z.nx, "s2a": z.ny, "s2b": z.ny, "s3": z.nz,
        "a1": z.nx, "b1": z.ny, "a2": z.ny, "b2": z.nx, "z3": z.nz,
        "gz": z.nz, "g2a": z.ny, "g2b": z.nx, "g1a": z.nx, "g1b": z.ny, "gc": z.groups // 2, "out": z.ny, "scale": z.ny, "own": 2,
    }
    return {name: pool.pair(count) for name, count in sizes.items()}, pool.total


def fused(z, ids, s_ref, t_ref, g_ref, tab_ref, idx_ref, f_ref, l_ref, most_ref,
          xin_s, xin_t, sort_ref, back_ref, xacc, xs, norms, ds_ref, dc_ref, rc_s, rc_c, r1sa, r1sb, r2sa, r2sb, sum_sa, sum_sb,
          us_ref, r3s, r1a, r1b, sums, r2a, r2b, u_ref, r3, wf, gr_ref, row_place, col_place, sizes, losses, fs, qs, ql, scales, landed, sems):
    y, v = lax.axis_index("pair"), lax.axis_index("value")
    c = lax.rem(v, z.nc)
    x = lax.rem(v // z.nc, z.nx)
    zc = v // (z.nc * z.nx)
    other = 1 - c
    hg = z.groups // 2
    quarter = z.cap // z.ny

    def at(yy=None, xx=None, zz=None, cc=None):
        yy = y if yy is None else yy
        xx = x if xx is None else xx
        zz = zc if zz is None else zz
        cc = c if cc is None else cc
        return (yy, (zz * z.nx + xx) * z.nc + cc)

    def on_y(k):
        return lax.rem(y + k, z.ny)

    def on_x(k):
        return lax.rem(x + k, z.nx)

    def on_z(k):
        return lax.rem(zc + k, z.nz)

    z_order = sorted(range(1, z.nz), key=lambda k: -min(k, z.nz - k))
    barrier = pltpu.get_barrier_semaphore()
    peers = [at(yy=on_y(k)) for k in range(1, z.ny)] + [at(xx=on_x(k)) for k in range(1, z.nx)]
    peers += [at(zz=on_z(k)) for k in range(1, z.nz)] + [at(cc=other)]
    for peer in peers:
        pl.semaphore_signal(barrier, inc=1, device_id=peer, device_id_type=MESH)
    pl.semaphore_wait(barrier, len(peers))

    def copy(name, src, dst, send, recv, device):
        first_send, first_recv = ids[name]
        return pltpu.make_async_remote_copy(
            src_ref=src, dst_ref=dst, send_sem=sems.at[first_send + send], recv_sem=sems.at[first_recv + recv],
            device_id=device, device_id_type=MESH)

    pending = []

    def drain():
        for one in pending:
            one.wait_send()

    order = sorted(range(1, z.ny), key=lambda k: min(k, z.ny - k))

    def in_copy(name, ref, land, k, source, target):
        cols = pl.ds(pl.multiple_of(target * z.cols, z.cols), z.cols)
        return copy(name, ref.at[:, cols], land.at[source], k, source, at(yy=on_y(k)))

    for k in order:
        in_copy("in_s", s_ref, xin_s, k, y, on_y(k)).start()
        pending.append(in_copy("in_t", t_ref, xin_t, k, y, on_y(k)))
    own_cols = pl.ds(pl.multiple_of(y * z.cols, z.cols), z.cols)
    own_s = pltpu.make_async_copy(s_ref.at[:, own_cols], xin_s.at[y], sems.at[ids["own"][0]])
    own_t = pltpu.make_async_copy(t_ref.at[:, own_cols], xin_t.at[y], sems.at[ids["own"][0] + 1])
    own_s.start()
    own_t.start()

    gr_ref[...] = g_ref[...].reshape(1, z.samples)
    slots = z.groups * z.cap
    eye = lax.broadcasted_iota(jnp.int32, (z.cap, z.cap), 0) == lax.broadcasted_iota(jnp.int32, (z.cap, z.cap), 1)
    above = lax.broadcasted_iota(jnp.int32, (z.cap, z.cap), 0) < lax.broadcasted_iota(jnp.int32, (z.cap, z.cap), 1)
    above = jnp.where(above, 1.0, 0.0).astype(BF16)

    def find_places(step, seen):
        first = pl.multiple_of(step * z.cap, z.cap)
        ids_row = gr_ref[:, pl.ds(first, z.cap)]
        hit = jnp.where(lax.broadcasted_iota(jnp.int32, (z.groups, z.cap), 0) == ids_row, 1.0, 0.0)
        before = seen + jnp.dot(hit.astype(BF16), above, preferred_element_type=F32)
        place = (ids_row * z.cap).astype(F32) + jnp.sum(hit * before, axis=0, keepdims=True)
        row_place[:, pl.ds(first, z.cap)] = place.astype(jnp.int32)
        turned = jnp.sum(jnp.where(eye, place, 0.0), axis=1, keepdims=True)
        col_place[pl.ds(first, z.cap), :] = turned.astype(jnp.int32)
        return seen + jnp.sum(hit, axis=1, keepdims=True)

    held = lax.fori_loop(0, z.samples // z.cap, find_places, jnp.zeros((z.groups, 1), F32))
    sizes[...] = jnp.broadcast_to(held[:, :, None], sizes.shape)
    most_ref[...] = jnp.max(held, axis=0, keepdims=True).astype(jnp.int32)

    for part in range(z.ny):
        def fill_sort(step, _):
            first = pl.multiple_of(step * z.cap, z.cap)
            slot = first + lax.broadcasted_iota(jnp.int32, (z.cap, z.rows), 0)
            place = row_place[:, part * z.rows:(part + 1) * z.rows]
            sort_ref[part, pl.ds(first, z.cap), :] = jnp.where(slot == place, 1.0, 0.0).astype(BF16)
            return 0

        lax.fori_loop(0, z.groups, fill_sort, 0)

    for k in order:
        in_copy("in_s", s_ref, xin_s, k, y, on_y(k)).wait_send()
        in_copy("in_t", t_ref, xin_t, k, y, on_y(k)).start()

    own_s.wait()
    own_t.wait()
    xacc[...] = jnp.zeros_like(xacc)
    scales[...] = jnp.zeros_like(scales)
    tall_rows = slots // 4

    def sort_from(source, values, first_col):
        def body(step, _):
            first = pl.multiple_of(step * tall_rows, tall_rows)
            place = sort_ref[source, pl.ds(first, tall_rows), :]
            xacc[pl.ds(first, tall_rows), first_col:first_col + z.cols] += jnp.dot(
                place, values[source], preferred_element_type=F32)
            return 0

        lax.fori_loop(0, 4, body, 0)

    sort_from(y, xin_s, 0)
    for k in order:
        source = on_y(z.ny - k)
        in_copy("in_s", s_ref, xin_s, k, source, on_y(k)).wait_recv()
        sort_from(source, xin_s, 0)

    def rows_of(group):
        return pl.ds(pl.multiple_of(group * z.cap, z.cap), z.cap)

    outer = (((1,), (1,)), ((), ()))

    def distances_self(groups):
        found = []
        for group in groups:
            mine = xacc[rows_of(group), 0:z.cols].astype(BF16)
            found.append((mine, lax.dot_general(mine, mine, outer, preferred_element_type=F32)))
        parts = []
        for mine, gram in found:
            diagonal = jnp.where(eye, gram, 0.0)
            norm_col = jnp.sum(diagonal, axis=1, keepdims=True)
            parts.append((norm_col, norm_col + jnp.sum(diagonal, axis=0, keepdims=True) - 2.0 * gram))
        for group, (mine, _), (norm_col, part) in zip(groups, found, parts):
            xs[group, 0:z.cap] = mine
            norms[group] = norm_col
            ds_ref[group] = part

    def distances_cross(groups):
        found = []
        for group in groups:
            theirs = xacc[rows_of(group), z.cols:2 * z.cols].astype(BF16)
            both = jnp.concatenate([xs[group, 0:z.cap], theirs], axis=0)
            found.append((theirs, lax.dot_general(both, theirs, outer, preferred_element_type=F32)))
        parts = []
        for group, (theirs, gram) in zip(groups, found):
            norm_row = jnp.sum(jnp.where(eye, gram[z.cap:2 * z.cap], 0.0), axis=0, keepdims=True)
            parts.append(norms[group] + norm_row - 2.0 * gram[0:z.cap])
        for group, (theirs, _), part in zip(groups, found, parts):
            xs[group, z.cap:2 * z.cap] = theirs
            dc_ref[group] = part

    def core_copy(name, part, land, i, group):
        return copy(name, part.at[group], land.at[i], i, i, at(cc=other))

    def quarter_of(k):
        return pl.ds(pl.multiple_of(k * quarter, quarter), quarter)

    def self_to_other(i, _):
        now = [TOGETHER * i + n for n in range(TOGETHER)]
        distances_self([other * hg + n for n in now])
        for n in now:
            core_copy("core_s", ds_ref, rc_s, n, other * hg + n).start()
        return 0

    lax.fori_loop(0, hg // TOGETHER, self_to_other, 0)

    def self_mine(i, _):
        now = [TOGETHER * i + n for n in range(TOGETHER)]
        distances_self([c * hg + n for n in now])
        for n in now:
            core_copy("core_s", ds_ref, rc_s, n, c * hg + n).wait_recv()
            ds_ref[c * hg + n] += rc_s[n]
        return 0

    lax.fori_loop(0, hg // TOGETHER, self_mine, 0)

    def s1_copies(k, source):
        second = ds_ref.at[pl.ds(c * hg + z.nx, z.nx), quarter_of(on_x(k))]
        return (copy("s1a", ds_ref.at[c * hg + on_x(k)], r1sa.at[source], k, source, at(xx=on_x(k))),
                copy("s1b", second, r1sb.at[source], k, source, at(xx=on_x(k))))

    def start(*copies):
        for one in copies:
            one.start()
            pending.append(one)

    for k in range(1, z.nx):
        start(*s1_copies(k, x))
    for i in range(hg):
        pending.append(core_copy("core_s", ds_ref, rc_s, i, other * hg + i))

    def fill_back(step, _):
        first = pl.multiple_of(step * z.cap, z.cap)
        slot = lax.broadcasted_iota(jnp.int32, (z.cap, slots), 1)
        back_ref[pl.ds(first, z.cap), :] = jnp.where(slot == col_place[pl.ds(first, z.cap), :], 1.0, 0.0).astype(BF16)
        return 0

    lax.fori_loop(0, z.samples // z.cap, fill_back, 0)

    sort_from(y, xin_t, z.cols)
    for k in order:
        source = on_y(z.ny - k)
        in_copy("in_t", t_ref, xin_t, k, source, on_y(k)).wait_recv()
        sort_from(source, xin_t, z.cols)

    def cross_to_other(i, _):
        now = [TOGETHER * i + n for n in range(TOGETHER)]
        distances_cross([other * hg + n for n in now])
        for n in now:
            core_copy("core_c", dc_ref, rc_c, n, other * hg + n).start()
        return 0

    lax.fori_loop(0, hg // TOGETHER, cross_to_other, 0)

    def a1_copy(k, source):
        return copy("a1", dc_ref.at[c * hg + on_x(k)], r1a.at[source], k, source, at(xx=on_x(k)))

    def b1_copy(k, source):
        return copy("b1", dc_ref.at[c * hg + z.nx + on_y(k)], r1b.at[source], k, source, at(yy=on_y(k)))

    def mine(k, _):
        now = (on_x(k), z.nx + on_y(k))
        distances_cross([c * hg + i for i in now])
        for i in now:
            core_copy("core_c", dc_ref, rc_c, i, c * hg + i).wait_recv()
            dc_ref[c * hg + i] += rc_c[i]

        @pl.when(k < z.nx)
        def _():
            a1_copy(k, x).start()
            b1_copy(k, y).start()

        return 0

    lax.fori_loop(1, z.nx + 1, mine, 0)
    for i in range(hg):
        pending.append(core_copy("core_c", dc_ref, rc_c, i, other * hg + i))
    for k in range(1, z.nx):
        pending.extend([a1_copy(k, x), b1_copy(k, y)])

    total_a = ds_ref[c * hg + x]
    total_b = ds_ref[pl.ds(c * hg + z.nx, z.nx), quarter_of(x), :]
    for k in range(1, z.nx):
        source = on_x(z.nx - k)
        for one in s1_copies(k, source):
            one.wait_recv()
        total_a = total_a + r1sa[source]
        total_b = total_b + r1sb[source]
    sum_sa[...] = total_a
    sum_sb[...] = total_b

    def s2_copies(k, source):
        return (copy("s2a", sum_sa.at[quarter_of(on_y(k))], r2sa.at[source], k, source, at(yy=on_y(k))),
                copy("s2b", sum_sb.at[on_y(k)], r2sb.at[source], k, source, at(yy=on_y(k))))

    for k in range(1, z.ny):
        start(*s2_copies(k, y))
    part_a = sum_sa[quarter_of(y), :]
    part_b = sum_sb[y]
    for k in range(1, z.ny):
        source = on_y(z.ny - k)
        for one in s2_copies(k, source):
            one.wait_recv()
        part_a = part_a + r2sa[source]
        part_b = part_b + r2sb[source]
    us_ref[0:z.half] = part_a.reshape(z.half, 8, z.cap)
    us_ref[z.half:2 * z.half] = part_b.reshape(z.half, 8, z.cap)

    def s3_copy(k, source):
        return copy("s3", us_ref.at[on_z(k)], r3s.at[source], k, source, at(zz=on_z(k)))

    for k in z_order:
        start(s3_copy(k, zc))

    total_a = dc_ref[c * hg + x]
    for k in range(1, z.nx):
        source = on_x(z.nx - k)
        a1_copy(k, source).wait_recv()
        total_a = total_a + r1a[source]
    sums[0] = total_a

    def a2_copy(k, source):
        return copy("a2", sums.at[0, quarter_of(on_y(k))], r2a.at[source], k, source, at(yy=on_y(k)))

    for k in range(1, z.ny):
        start(a2_copy(k, y))
    total_b = dc_ref[c * hg + z.nx + y]
    for k in range(1, z.ny):
        source = on_y(z.ny - k)
        b1_copy(k, source).wait_recv()
        total_b = total_b + r1b[source]
    sums[1] = total_b

    def b2_copy(k, source):
        return copy("b2", sums.at[1, quarter_of(on_x(k))], r2b.at[source], k, source, at(xx=on_x(k)))

    for k in range(1, z.nx):
        start(b2_copy(k, x))

    part_a = sums[0, quarter_of(y), :]
    for k in range(1, z.ny):
        source = on_y(z.ny - k)
        a2_copy(k, source).wait_recv()
        part_a = part_a + r2a[source]
    u_ref[0:z.half] = part_a.reshape(z.half, 8, z.cap)
    part_b = sums[1, quarter_of(x), :]
    for k in range(1, z.nx):
        source = on_x(z.nx - k)
        b2_copy(k, source).wait_recv()
        part_b = part_b + r2b[source]
    u_ref[z.half:2 * z.half] = part_b.reshape(z.half, 8, z.cap)

    def z3_copy(k, source):
        return copy("z3", u_ref.at[on_z(k)], r3.at[source], k, source, at(zz=on_z(k)))

    for k in z_order:
        start(z3_copy(k, zc))
    dist_self = us_ref[zc]
    for k in range(1, z.nz):
        source = on_z(z.nz - k)
        s3_copy(k, source).wait_recv()
        dist_self = dist_self + r3s[source]
    dist_cross = u_ref[zc]
    for k in range(1, z.nz):
        source = on_z(z.nz - k)
        z3_copy(k, source).wait_recv()
        dist_cross = dist_cross + r3[source]

    way = zc // z.half
    member = (1 - way) * x + way * y
    sub = (1 - way) * y + way * x
    group = c * hg + way * z.nx + member
    block = sub * z.half + lax.rem(zc, z.half)
    size = sizes[group]
    row_at = (block * 8 + lax.broadcasted_iota(jnp.int32, (8, z.cap), 0)).astype(F32)
    col_at = lax.broadcasted_iota(jnp.int32, (8, z.cap), 1).astype(F32)
    mask = jnp.where((row_at < size) & (col_at < size), 1.0, 0.0)
    heights = [tab_ref[idx_ref[m]] for m in range(4)]
    weight_self, weight_cross, row_loss, pull = pair_terms(
        jnp.maximum(dist_self, 0.0), jnp.maximum(dist_cross, 0.0), mask, heights, z.latent)
    lanes = lax.broadcasted_iota(jnp.int32, (8, z.cap), 1)

    def with_row_term(weights, term):
        first = term.astype(BF16).astype(F32)
        second = (term - first).astype(BF16).astype(F32)
        third = term - first - second
        columns = jnp.where(lanes == z.cap - 3, first, jnp.where(lanes == z.cap - 2, second, third))
        return jnp.where(lanes < z.most, weights, columns)

    wf[group, block] = jnp.concatenate(
        [with_row_term(weight_self.astype(F32), pull), with_row_term(-weight_cross.astype(F32), row_loss / size)],
        axis=0).astype(BF16)

    def gz_copy(k, source):
        way_of = source // z.half
        group_of = c * hg + way_of * z.nx + (1 - way_of) * x + way_of * y
        block_of = ((1 - way_of) * y + way_of * x) * z.half + lax.rem(source, z.half)
        place = wf.at[group_of, block_of]
        return copy("gz", place, place, k, source, at(zz=on_z(k)))

    for k in z_order:
        start(gz_copy(k, zc))
    for k in range(1, z.nz):
        gz_copy(k, on_z(z.nz - k)).wait_recv()

    def g2a_copy(k, source):
        place = wf.at[c * hg + x, pl.ds(source * z.half, z.half)]
        return copy("g2a", place, place, k, source, at(yy=on_y(k)))

    def g2b_copy(k, source):
        place = wf.at[c * hg + z.nx + y, pl.ds(source * z.half, z.half)]
        return copy("g2b", place, place, k, source, at(xx=on_x(k)))

    for k in range(1, z.nx):
        start(g2a_copy(k, y))
        start(g2b_copy(k, x))

    def g1a_copy(k, source):
        place = wf.at[c * hg + source]
        return copy("g1a", place, place, k, source, at(xx=on_x(k)))

    def g1b_copy(k, source):
        place = wf.at[c * hg + z.nx + source]
        return copy("g1b", place, place, k, source, at(yy=on_y(k)))

    for k in range(1, z.ny):
        g2a_copy(k, on_y(z.ny - k)).wait_recv()
    for k in order:
        start(g1a_copy(k, x))
    for k in range(1, z.nx):
        g2b_copy(k, on_x(z.nx - k)).wait_recv()
    for k in order:
        start(g1b_copy(k, y))

    def gc_copy(i, core):
        place = wf.at[core * hg + i]
        return copy("gc", place, place, i, i, at(cc=other))

    last = lax.broadcasted_iota(jnp.int32, (z.cap, z.cap), 1) >= z.most

    def force_of(groups):
        found = []
        for g in groups:
            held = wf[g].astype(F32).reshape(z.blocks, 2, 8, z.cap)
            to_self, to_cross = held[:, 0].reshape(z.cap, z.cap), held[:, 1].reshape(z.cap, z.cap)
            pulls = jnp.sum(jnp.where(last, to_self, 0.0), axis=1, keepdims=True)
            loss = jnp.sum(jnp.where(last, to_cross, 0.0), axis=0, keepdims=True)
            weights = jnp.concatenate([to_self, to_cross], axis=1).astype(BF16)
            values = xs[g]
            pulled = values[0:z.cap].astype(F32) * pulls + jnp.dot(weights, values, preferred_element_type=F32)
            force = pulled / sizes[g]
            high = force.astype(BF16)
            low = (force - high.astype(F32)).astype(BF16)
            found.append((loss, high, low))
        for g, (loss, high, low) in zip(groups, found):
            rows = pl.ds(pl.multiple_of(g * z.cap, z.cap), z.cap)
            losses[g] = loss
            fs[rows, 0:z.cols] = high
            fs[rows, z.cols:2 * z.cols] = low

    for k in [0] + order:
        now = (on_x(z.nx - k), z.nx + on_y(z.ny - k))
        if k:
            g1a_copy(k, now[0]).wait_recv()
            g1b_copy(k, now[1] - z.nx).wait_recv()
        for i in now:
            start(gc_copy(i, c))
        force_of([c * hg + i for i in now])
    for k in [0] + order:
        now = (on_x(z.nx - k), z.nx + on_y(z.ny - k))
        for i in now:
            gc_copy(i, other).wait_recv()
        force_of([other * hg + i for i in now])

    def out_copies(k, source):
        return (copy("out", qs.at[k], ql.at[source], k, source, at(yy=on_y(k))),
                copy("scale", scales.at[k], landed.at[source], k, source, at(yy=on_y(k))))

    parts = z.rows // z.lanes
    square = (z.lanes, z.lanes)
    same = lax.broadcasted_iota(jnp.int32, square, 0) == lax.broadcasted_iota(jnp.int32, square, 1)

    def unsorted(k):
        rows = pl.ds(pl.multiple_of(on_y(k) * z.rows, z.rows), z.rows)
        moved = jnp.dot(back_ref[rows, :], fs[...], preferred_element_type=F32)
        return moved[:, 0:z.cols] + moved[:, z.cols:2 * z.cols]

    def send_out(step, _):
        k = lax.rem(step + z.ny // 2 - 1, z.ny - 1) + 1
        force = unsorted(k)
        top = jnp.maximum(jnp.max(jnp.abs(force), axis=1, keepdims=True), 1e-33)
        qs[k] = jnp.round(force * (32767.0 / top)).astype(jnp.int32).astype(jnp.int16)
        unit = top / 32767.0
        for part in range(parts):
            spread = jnp.where(same, unit[part * z.lanes:(part + 1) * z.lanes], 0.0)
            scales[k, part:part + 1, :] = jnp.sum(spread, axis=0, keepdims=True)
        for one in out_copies(k, y):
            one.start()
        return 0

    lax.fori_loop(0, z.ny - 1, send_out, 0)
    f_ref[:, own_cols] = unsorted(0)
    l_ref[...] = jnp.sum(jnp.sum(losses[...], axis=0), axis=1, keepdims=True) / z.samples
    drain()
    for k in order:
        source = on_y(z.ny - k)
        for one in out_copies(k, source):
            one.wait_recv()
        cols = pl.ds(pl.multiple_of(source * z.cols, z.cols), z.cols)
        for part in range(parts):
            rows = slice(part * z.lanes, (part + 1) * z.lanes)
            unit = jnp.sum(jnp.where(same, landed[source, part:part + 1, :], 0.0), axis=1, keepdims=True)
            f_ref[rows, cols] = ql[source, rows, :].astype(jnp.int32).astype(F32) * unit

    for k in range(1, z.ny):
        for one in out_copies(k, y):
            one.wait_send()


def sorted_path(z, student, teacher, bw_table, bw_index, group_ids):
    ids, count = exchanges(z)
    slots, hg = z.groups * z.cap, z.groups // 2
    quarter = z.cap // z.ny
    vmem, smem, anywhere = (pl.BlockSpec(memory_space=m) for m in (pltpu.VMEM, pltpu.SMEM, pl.ANY))
    force, loss, largest = pl.pallas_call(
        functools.partial(fused, z, ids),
        out_shape=(pltpu.VMEM((z.rows, z.tile), F32), jax.ShapeDtypeStruct((1, 1), F32),
                   jax.ShapeDtypeStruct((1, 1), jnp.int32)),
        in_specs=[anywhere, anywhere, vmem, smem, smem],
        out_specs=(vmem, vmem, vmem),
        scratch_shapes=[
            pltpu.VMEM((z.ny, z.rows, z.cols), BF16),
            pltpu.VMEM((z.ny, z.rows, z.cols), BF16),
            pltpu.VMEM((z.ny, slots, z.rows), BF16),
            pltpu.VMEM((z.samples, slots), BF16),
            pltpu.VMEM((slots, 2 * z.cols), F32),
            pltpu.VMEM((z.groups, 2 * z.cap, z.cols), BF16),
            pltpu.VMEM((z.groups, z.cap, 1), F32),
            pltpu.VMEM((z.groups, z.cap, z.cap), F32),
            pltpu.VMEM((z.groups, z.cap, z.cap), F32),
            pltpu.VMEM((hg, z.cap, z.cap), F32),
            pltpu.VMEM((hg, z.cap, z.cap), F32),
            pltpu.VMEM((z.nx, z.cap, z.cap), F32),
            pltpu.VMEM((z.nx, z.nx, quarter, z.cap), F32),
            pltpu.VMEM((z.ny, quarter, z.cap), F32),
            pltpu.VMEM((z.ny, quarter, z.cap), F32),
            pltpu.VMEM((z.cap, z.cap), F32),
            pltpu.VMEM((z.nx, quarter, z.cap), F32),
            pltpu.VMEM((z.nz, 8, z.cap), F32),
            pltpu.VMEM((z.nz, 8, z.cap), F32),
            pltpu.VMEM((z.nx, z.cap, z.cap), F32),
            pltpu.VMEM((z.ny, z.cap, z.cap), F32),
            pltpu.VMEM((2, z.cap, z.cap), F32),
            pltpu.VMEM((z.ny, quarter, z.cap), F32),
            pltpu.VMEM((z.nx, quarter, z.cap), F32),
            pltpu.VMEM((z.nz, 8, z.cap), F32),
            pltpu.VMEM((z.nz, 8, z.cap), F32),
            pltpu.VMEM((z.groups, z.blocks, 16, z.cap), BF16),
            pltpu.VMEM((1, z.samples), jnp.int32),
            pltpu.VMEM((1, z.samples), jnp.int32),
            pltpu.VMEM((z.samples, 1), jnp.int32),
            pltpu.VMEM((z.groups, 1, 1), F32),
            pltpu.VMEM((z.groups, 1, z.cap), F32),
            pltpu.VMEM((slots, 2 * z.cols), BF16),
            pltpu.VMEM((z.ny, z.rows, z.cols), jnp.int16),
            pltpu.VMEM((z.ny, z.rows, z.cols), jnp.int16),
            pltpu.VMEM((z.ny, 8, z.lanes), F32),
            pltpu.VMEM((z.ny, 8, z.lanes), F32),
            pltpu.SemaphoreType.DMA((count,)),
        ],
        compiler_params=pltpu.CompilerParams(
            collective_id=1, has_side_effects=True, vmem_limit_bytes=56 * 1024 * 1024),
        name="grouped",
    )(student, teacher, group_ids, bw_table, bw_index)
    return force, loss.reshape(()), largest.reshape(())


def gather_pair(z, block):
    y = lax.axis_index("pair")
    out = jnp.zeros((z.ny,) + block.shape, block.dtype)
    for k in range(z.ny):
        moved = lax.ppermute(block, "pair", [(i, (i + k) % z.ny) for i in range(z.ny)]) if k else block
        out = lax.dynamic_update_index_in_dim(out, moved, lax.rem(y + z.ny - k, z.ny), 0)
    return out.reshape((z.ny * block.shape[0],) + block.shape[1:])


def sum_over(array, axis, count):
    step = 1
    while step < count:
        array = array + lax.ppermute(array, axis, [(i, i ^ step) for i in range(count)])
        step *= 2
    return array


def dense_path(z, student, teacher, bw_table, bw_index, group_ids):
    students = gather_pair(z, student)
    teachers = gather_pair(z, teacher)
    both = jnp.concatenate([students, teachers], axis=0)
    wide = both.astype(F32)
    row_wide = student.astype(F32)
    norms = jnp.sum(wide * wide, axis=1)
    row_norms = jnp.sum(row_wide * row_wide, axis=1)
    gram = lax.dot_general(student, both, (((1,), (1,)), ((), ())), preferred_element_type=F32)
    part = row_norms[:, None] + norms[None, :] - 2.0 * gram
    dist = jnp.maximum(sum_over(part, "value", z.nx * z.nz * z.nc), 0.0)
    row_ids = lax.dynamic_slice_in_dim(group_ids, lax.axis_index("pair") * z.rows, z.rows)
    same = (row_ids[:, None] == group_ids[None, :]).astype(F32)
    sizes = jnp.sum(same, axis=1, keepdims=True)
    heights = bw_table[bw_index]
    weight_self, weight_cross, row_loss, pull = pair_terms(
        dist[:, :z.samples], dist[:, z.samples:], same, [heights[m] for m in range(4)], z.latent)
    loss = sum_over(jnp.broadcast_to(jnp.sum(row_loss / sizes), (8, 128)), "pair", z.ny)[0, 0] / z.samples
    pulled = row_wide * pull
    pulled = pulled + jnp.dot(weight_self, students, preferred_element_type=F32)
    pulled = pulled - jnp.dot(weight_cross, teachers, preferred_element_type=F32)
    return pulled / sizes, loss


def build(mesh, z):
    def step(student, teacher, bw_table, bw_index, group_ids):
        force, loss, largest = sorted_path(z, student, teacher, bw_table, bw_index, group_ids)
        return lax.cond(
            largest <= z.most,
            lambda *held: held[:2],
            lambda *held: dense_path(z, *held[2:]),
            force, loss, student, teacher, bw_table, bw_index, group_ids)

    return jax.shard_map(
        step, mesh=mesh,
        in_specs=(P("pair", "value"), P("pair", "value"), P(None), P(None), P(None)),
        out_specs=(P("pair", "value"), P()),
        check_vma=False)


def solution(mesh):
    return build(mesh, Sizes(ny=4, nx=4, nz=8, nc=2, samples=1536, tile=1024, latent=65536))
```

```python
import functools

import jax
import jax.numpy as jnp
from jax import lax
from jax.experimental import pallas as pl
from jax.experimental.pallas import tpu as pltpu
from jax.sharding import PartitionSpec as P

MESH = pl.DeviceIdType.MESH
F32, BF16 = jnp.float32, jnp.bfloat16


TOGETHER = 8


class Sizes:
    def __init__(self, ny, nx, nz, nc, samples, tile, latent):
        self.ny, self.nx, self.nz, self.nc = ny, nx, nz, nc
        self.samples, self.tile, self.latent = samples, tile, float(latent)
        self.rows = samples // ny
        self.cols = tile // ny
        self.groups = 2 * nc * nx
        self.half = nz // 2
        self.cap = 8 * ny * self.half
        self.blocks = self.cap // 8
        self.most = self.cap - 3
        self.lanes = min(128, self.rows)


def pair_terms(dist_self, dist_cross, mask, heights, latent):
    kern_self = jnp.zeros_like(dist_self)
    kern_cross = jnp.zeros_like(dist_cross)
    weight_self = jnp.zeros_like(dist_self)
    weight_cross = jnp.zeros_like(dist_cross)
    count = len(heights)
    for height in heights:
        width_now = height * latent
        exp_self = jnp.exp(-dist_self / width_now)
        exp_cross = jnp.exp(-dist_cross / width_now)
        kern_self = kern_self + exp_self
        kern_cross = kern_cross + exp_cross
        weight_self = weight_self + exp_self / height
        weight_cross = weight_cross + exp_cross / height
    kern_self = kern_self / count * mask
    kern_cross = kern_cross / count * mask
    weight_self = weight_self / count * mask
    weight_cross = weight_cross / count * mask
    row_loss = jnp.sum(kern_self - 2.0 * kern_cross, axis=1, keepdims=True)
    pull = jnp.sum(weight_cross, axis=1, keepdims=True) - jnp.sum(weight_self, axis=1, keepdims=True)
    return weight_self.astype(BF16), weight_cross.astype(BF16), row_loss, pull


class Pool:
    def __init__(self):
        self.total = 0

    def take(self, count):
        first = self.total
        self.total += count
        return first

    def pair(self, count):
        return self.take(count), self.take(count)


def exchanges(z):
    pool = Pool()
    sizes = {
        "in_s": z.ny, "in_t": z.ny, "core_s": z.groups // 2, "core_c": z.groups // 2, "s1a": z.nx, "s1b": z.nx, "s2a": z.ny, "s2b": z.ny, "s3": z.nz,
        "a1": z.nx, "b1": z.ny, "a2": z.ny, "b2": z.nx, "z3": z.nz,
        "gz": z.nz, "g2a": z.ny, "g2b": z.nx, "g1a": z.nx, "g1b": z.ny, "gc": z.groups // 2, "out": z.ny, "scale": z.ny, "own": 2,
    }
    return {name: pool.pair(count) for name, count in sizes.items()}, pool.total


def fused(z, ids, s_ref, t_ref, g_ref, tab_ref, idx_ref, f_ref, l_ref, most_ref,
          xin_s, xin_t, sort_ref, back_ref, xacc, xs, norms, ds_ref, dc_ref, rc_s, rc_c, r1sa, r1sb, r2sa, r2sb, sum_sa, sum_sb,
          us_ref, r3s, r1a, r1b, sums, r2a, r2b, u_ref, r3, wf, gr_ref, row_place, col_place, sizes, losses, fs, qs, ql, scales, landed, sems):
    y, v = lax.axis_index("pair"), lax.axis_index("value")
    c = lax.rem(v, z.nc)
    x = lax.rem(v // z.nc, z.nx)
    zc = v // (z.nc * z.nx)
    other = 1 - c
    hg = z.groups // 2
    quarter = z.cap // z.ny

    def at(yy=None, xx=None, zz=None, cc=None):
        yy = y if yy is None else yy
        xx = x if xx is None else xx
        zz = zc if zz is None else zz
        cc = c if cc is None else cc
        return (yy, (zz * z.nx + xx) * z.nc + cc)

    def on_y(k):
        return lax.rem(y + k, z.ny)

    def on_x(k):
        return lax.rem(x + k, z.nx)

    def on_z(k):
        return lax.rem(zc + k, z.nz)

    z_order = sorted(range(1, z.nz), key=lambda k: -min(k, z.nz - k))
    barrier = pltpu.get_barrier_semaphore()
    peers = [at(yy=on_y(k)) for k in range(1, z.ny)] + [at(xx=on_x(k)) for k in range(1, z.nx)]
    peers += [at(zz=on_z(k)) for k in range(1, z.nz)] + [at(cc=other)]
    for peer in peers:
        pl.semaphore_signal(barrier, inc=1, device_id=peer, device_id_type=MESH)
    pl.semaphore_wait(barrier, len(peers))

    def copy(name, src, dst, send, recv, device):
        first_send, first_recv = ids[name]
        return pltpu.make_async_remote_copy(
            src_ref=src, dst_ref=dst, send_sem=sems.at[first_send + send], recv_sem=sems.at[first_recv + recv],
            device_id=device, device_id_type=MESH)

    pending = []

    def drain():
        for one in pending:
            one.wait_send()

    order = sorted(range(1, z.ny), key=lambda k: min(k, z.ny - k))

    def in_copy(name, ref, land, k, source, target):
        cols = pl.ds(pl.multiple_of(target * z.cols, z.cols), z.cols)
        return copy(name, ref.at[:, cols], land.at[source], k, source, at(yy=on_y(k)))

    for k in order:
        in_copy("in_s", s_ref, xin_s, k, y, on_y(k)).start()
        pending.append(in_copy("in_t", t_ref, xin_t, k, y, on_y(k)))
    own_cols = pl.ds(pl.multiple_of(y * z.cols, z.cols), z.cols)
    own_s = pltpu.make_async_copy(s_ref.at[:, own_cols], xin_s.at[y], sems.at[ids["own"][0]])
    own_t = pltpu.make_async_copy(t_ref.at[:, own_cols], xin_t.at[y], sems.at[ids["own"][0] + 1])
    own_s.start()
    own_t.start()

    gr_ref[...] = g_ref[...].reshape(1, z.samples)
    slots = z.groups * z.cap
    eye = lax.broadcasted_iota(jnp.int32, (z.cap, z.cap), 0) == lax.broadcasted_iota(jnp.int32, (z.cap, z.cap), 1)
    above = lax.broadcasted_iota(jnp.int32, (z.cap, z.cap), 0) < lax.broadcasted_iota(jnp.int32, (z.cap, z.cap), 1)
    above = jnp.where(above, 1.0, 0.0).astype(BF16)

    def find_places(step, seen):
        first = pl.multiple_of(step * z.cap, z.cap)
        ids_row = gr_ref[:, pl.ds(first, z.cap)]
        hit = jnp.where(lax.broadcasted_iota(jnp.int32, (z.groups, z.cap), 0) == ids_row, 1.0, 0.0)
        before = seen + jnp.dot(hit.astype(BF16), above, preferred_element_type=F32)
        place = (ids_row * z.cap).astype(F32) + jnp.sum(hit * before, axis=0, keepdims=True)
        row_place[:, pl.ds(first, z.cap)] = place.astype(jnp.int32)
        turned = jnp.sum(jnp.where(eye, place, 0.0), axis=1, keepdims=True)
        col_place[pl.ds(first, z.cap), :] = turned.astype(jnp.int32)
        return seen + jnp.sum(hit, axis=1, keepdims=True)

    held = lax.fori_loop(0, z.samples // z.cap, find_places, jnp.zeros((z.groups, 1), F32))
    sizes[...] = jnp.broadcast_to(held[:, :, None], sizes.shape)
    most_ref[...] = jnp.max(held, axis=0, keepdims=True).astype(jnp.int32)

    for part in range(z.ny):
        def fill_sort(step, _):
            first = pl.multiple_of(step * z.cap, z.cap)
            slot = first + lax.broadcasted_iota(jnp.int32, (z.cap, z.rows), 0)
            place = row_place[:, part * z.rows:(part + 1) * z.rows]
            sort_ref[part, pl.ds(first, z.cap), :] = jnp.where(slot == place, 1.0, 0.0).astype(BF16)
            return 0

        lax.fori_loop(0, z.groups, fill_sort, 0)

    for k in order:
        in_copy("in_s", s_ref, xin_s, k, y, on_y(k)).wait_send()
        in_copy("in_t", t_ref, xin_t, k, y, on_y(k)).start()

    own_s.wait()
    own_t.wait()
    xacc[...] = jnp.zeros_like(xacc)
    scales[...] = jnp.zeros_like(scales)
    tall_rows = slots // 4

    def sort_from(source, values, first_col):
        def body(step, _):
            first = pl.multiple_of(step * tall_rows, tall_rows)
            place = sort_ref[source, pl.ds(first, tall_rows), :]
            xacc[pl.ds(first, tall_rows), first_col:first_col + z.cols] += jnp.dot(
                place, values[source], preferred_element_type=F32)
            return 0

        lax.fori_loop(0, 4, body, 0)

    sort_from(y, xin_s, 0)
    for k in order:
        source = on_y(z.ny - k)
        in_copy("in_s", s_ref, xin_s, k, source, on_y(k)).wait_recv()
        sort_from(source, xin_s, 0)

    def rows_of(group):
        return pl.ds(pl.multiple_of(group * z.cap, z.cap), z.cap)

    outer = (((1,), (1,)), ((), ()))

    def distances_self(groups):
        found = []
        for group in groups:
            mine = xacc[rows_of(group), 0:z.cols].astype(BF16)
            found.append((mine, lax.dot_general(mine, mine, outer, preferred_element_type=F32)))
        parts = []
        for mine, gram in found:
            diagonal = jnp.where(eye, gram, 0.0)
            norm_col = jnp.sum(diagonal, axis=1, keepdims=True)
            parts.append((norm_col, norm_col + jnp.sum(diagonal, axis=0, keepdims=True) - 2.0 * gram))
        for group, (mine, _), (norm_col, part) in zip(groups, found, parts):
            xs[group, 0:z.cap] = mine
            norms[group] = norm_col
            ds_ref[group] = part

    def distances_cross(groups):
        found = []
        for group in groups:
            theirs = xacc[rows_of(group), z.cols:2 * z.cols].astype(BF16)
            both = jnp.concatenate([xs[group, 0:z.cap], theirs], axis=0)
            found.append((theirs, lax.dot_general(both, theirs, outer, preferred_element_type=F32)))
        parts = []
        for group, (theirs, gram) in zip(groups, found):
            norm_row = jnp.sum(jnp.where(eye, gram[z.cap:2 * z.cap], 0.0), axis=0, keepdims=True)
            parts.append(norms[group] + norm_row - 2.0 * gram[0:z.cap])
        for group, (theirs, _), part in zip(groups, found, parts):
            xs[group, z.cap:2 * z.cap] = theirs
            dc_ref[group] = part

    def core_copy(name, part, land, i, group):
        return copy(name, part.at[group], land.at[i], i, i, at(cc=other))

    def quarter_of(k):
        return pl.ds(pl.multiple_of(k * quarter, quarter), quarter)

    def self_to_other(i, _):
        now = [TOGETHER * i + n for n in range(TOGETHER)]
        distances_self([other * hg + n for n in now])
        for n in now:
            core_copy("core_s", ds_ref, rc_s, n, other * hg + n).start()
        return 0

    lax.fori_loop(0, hg // TOGETHER, self_to_other, 0)

    def self_mine(i, _):
        now = [TOGETHER * i + n for n in range(TOGETHER)]
        distances_self([c * hg + n for n in now])
        for n in now:
            core_copy("core_s", ds_ref, rc_s, n, c * hg + n).wait_recv()
            ds_ref[c * hg + n] += rc_s[n]
        return 0

    lax.fori_loop(0, hg // TOGETHER, self_mine, 0)

    def s1_copies(k, source):
        second = ds_ref.at[pl.ds(c * hg + z.nx, z.nx), quarter_of(on_x(k))]
        return (copy("s1a", ds_ref.at[c * hg + on_x(k)], r1sa.at[source], k, source, at(xx=on_x(k))),
                copy("s1b", second, r1sb.at[source], k, source, at(xx=on_x(k))))

    def start(*copies):
        for one in copies:
            one.start()
            pending.append(one)

    for k in range(1, z.nx):
        start(*s1_copies(k, x))
    for i in range(hg):
        pending.append(core_copy("core_s", ds_ref, rc_s, i, other * hg + i))

    def fill_back(step, _):
        first = pl.multiple_of(step * z.cap, z.cap)
        slot = lax.broadcasted_iota(jnp.int32, (z.cap, slots), 1)
        back_ref[pl.ds(first, z.cap), :] = jnp.where(slot == col_place[pl.ds(first, z.cap), :], 1.0, 0.0).astype(BF16)
        return 0

    lax.fori_loop(0, z.samples // z.cap, fill_back, 0)

    sort_from(y, xin_t, z.cols)
    for k in order:
        source = on_y(z.ny - k)
        in_copy("in_t", t_ref, xin_t, k, source, on_y(k)).wait_recv()
        sort_from(source, xin_t, z.cols)

    def cross_to_other(i, _):
        now = [TOGETHER * i + n for n in range(TOGETHER)]
        distances_cross([other * hg + n for n in now])
        for n in now:
            core_copy("core_c", dc_ref, rc_c, n, other * hg + n).start()
        return 0

    lax.fori_loop(0, hg // TOGETHER, cross_to_other, 0)

    def a1_copy(k, source):
        return copy("a1", dc_ref.at[c * hg + on_x(k)], r1a.at[source], k, source, at(xx=on_x(k)))

    def b1_copy(k, source):
        return copy("b1", dc_ref.at[c * hg + z.nx + on_y(k)], r1b.at[source], k, source, at(yy=on_y(k)))

    def mine(k, _):
        now = (on_x(k), z.nx + on_y(k))
        distances_cross([c * hg + i for i in now])
        for i in now:
            core_copy("core_c", dc_ref, rc_c, i, c * hg + i).wait_recv()
            dc_ref[c * hg + i] += rc_c[i]

        @pl.when(k < z.nx)
        def _():
            a1_copy(k, x).start()
            b1_copy(k, y).start()

        return 0

    lax.fori_loop(1, z.nx + 1, mine, 0)
    for i in range(hg):
        pending.append(core_copy("core_c", dc_ref, rc_c, i, other * hg + i))
    for k in range(1, z.nx):
        pending.extend([a1_copy(k, x), b1_copy(k, y)])

    total_a = ds_ref[c * hg + x]
    total_b = ds_ref[pl.ds(c * hg + z.nx, z.nx), quarter_of(x), :]
    for k in range(1, z.nx):
        source = on_x(z.nx - k)
        for one in s1_copies(k, source):
            one.wait_recv()
        total_a = total_a + r1sa[source]
        total_b = total_b + r1sb[source]
    sum_sa[...] = total_a
    sum_sb[...] = total_b

    def s2_copies(k, source):
        return (copy("s2a", sum_sa.at[quarter_of(on_y(k))], r2sa.at[source], k, source, at(yy=on_y(k))),
                copy("s2b", sum_sb.at[on_y(k)], r2sb.at[source], k, source, at(yy=on_y(k))))

    for k in range(1, z.ny):
        start(*s2_copies(k, y))
    part_a = sum_sa[quarter_of(y), :]
    part_b = sum_sb[y]
    for k in range(1, z.ny):
        source = on_y(z.ny - k)
        for one in s2_copies(k, source):
            one.wait_recv()
        part_a = part_a + r2sa[source]
        part_b = part_b + r2sb[source]
    us_ref[0:z.half] = part_a.reshape(z.half, 8, z.cap)
    us_ref[z.half:2 * z.half] = part_b.reshape(z.half, 8, z.cap)

    def s3_copy(k, source):
        return copy("s3", us_ref.at[on_z(k)], r3s.at[source], k, source, at(zz=on_z(k)))

    for k in z_order:
        start(s3_copy(k, zc))

    total_a = dc_ref[c * hg + x]
    for k in range(1, z.nx):
        source = on_x(z.nx - k)
        a1_copy(k, source).wait_recv()
        total_a = total_a + r1a[source]
    sums[0] = total_a

    def a2_copy(k, source):
        return copy("a2", sums.at[0, quarter_of(on_y(k))], r2a.at[source], k, source, at(yy=on_y(k)))

    for k in range(1, z.ny):
        start(a2_copy(k, y))
    total_b = dc_ref[c * hg + z.nx + y]
    for k in range(1, z.ny):
        source = on_y(z.ny - k)
        b1_copy(k, source).wait_recv()
        total_b = total_b + r1b[source]
    sums[1] = total_b

    def b2_copy(k, source):
        return copy("b2", sums.at[1, quarter_of(on_x(k))], r2b.at[source], k, source, at(xx=on_x(k)))

    for k in range(1, z.nx):
        start(b2_copy(k, x))

    part_a = sums[0, quarter_of(y), :]
    for k in range(1, z.ny):
        source = on_y(z.ny - k)
        a2_copy(k, source).wait_recv()
        part_a = part_a + r2a[source]
    u_ref[0:z.half] = part_a.reshape(z.half, 8, z.cap)
    part_b = sums[1, quarter_of(x), :]
    for k in range(1, z.nx):
        source = on_x(z.nx - k)
        b2_copy(k, source).wait_recv()
        part_b = part_b + r2b[source]
    u_ref[z.half:2 * z.half] = part_b.reshape(z.half, 8, z.cap)

    def z3_copy(k, source):
        return copy("z3", u_ref.at[on_z(k)], r3.at[source], k, source, at(zz=on_z(k)))

    for k in z_order:
        start(z3_copy(k, zc))
    dist_self = us_ref[zc]
    for k in range(1, z.nz):
        source = on_z(z.nz - k)
        s3_copy(k, source).wait_recv()
        dist_self = dist_self + r3s[source]
    dist_cross = u_ref[zc]
    for k in range(1, z.nz):
        source = on_z(z.nz - k)
        z3_copy(k, source).wait_recv()
        dist_cross = dist_cross + r3[source]

    way = zc // z.half
    member = (1 - way) * x + way * y
    sub = (1 - way) * y + way * x
    group = c * hg + way * z.nx + member
    block = sub * z.half + lax.rem(zc, z.half)
    size = sizes[group]
    row_at = (block * 8 + lax.broadcasted_iota(jnp.int32, (8, z.cap), 0)).astype(F32)
    col_at = lax.broadcasted_iota(jnp.int32, (8, z.cap), 1).astype(F32)
    mask = jnp.where((row_at < size) & (col_at < size), 1.0, 0.0)
    heights = [tab_ref[idx_ref[m]] for m in range(4)]
    weight_self, weight_cross, row_loss, pull = pair_terms(
        jnp.maximum(dist_self, 0.0), jnp.maximum(dist_cross, 0.0), mask, heights, z.latent)
    lanes = lax.broadcasted_iota(jnp.int32, (8, z.cap), 1)

    def with_row_term(weights, term):
        first = term.astype(BF16).astype(F32)
        second = (term - first).astype(BF16).astype(F32)
        third = term - first - second
        columns = jnp.where(lanes == z.cap - 3, first, jnp.where(lanes == z.cap - 2, second, third))
        return jnp.where(lanes < z.most, weights, columns)

    wf[group, block] = jnp.concatenate(
        [with_row_term(weight_self.astype(F32), pull), with_row_term(-weight_cross.astype(F32), row_loss / size)],
        axis=0).astype(BF16)

    def gz_copy(k, source):
        way_of = source // z.half
        group_of = c * hg + way_of * z.nx + (1 - way_of) * x + way_of * y
        block_of = ((1 - way_of) * y + way_of * x) * z.half + lax.rem(source, z.half)
        place = wf.at[group_of, block_of]
        return copy("gz", place, place, k, source, at(zz=on_z(k)))

    for k in z_order:
        start(gz_copy(k, zc))
    for k in range(1, z.nz):
        gz_copy(k, on_z(z.nz - k)).wait_recv()

    def g2a_copy(k, source):
        place = wf.at[c * hg + x, pl.ds(source * z.half, z.half)]
        return copy("g2a", place, place, k, source, at(yy=on_y(k)))

    def g2b_copy(k, source):
        place = wf.at[c * hg + z.nx + y, pl.ds(source * z.half, z.half)]
        return copy("g2b", place, place, k, source, at(xx=on_x(k)))

    for k in range(1, z.nx):
        start(g2a_copy(k, y))
        start(g2b_copy(k, x))

    def g1a_copy(k, source):
        place = wf.at[c * hg + source]
        return copy("g1a", place, place, k, source, at(xx=on_x(k)))

    def g1b_copy(k, source):
        place = wf.at[c * hg + z.nx + source]
        return copy("g1b", place, place, k, source, at(yy=on_y(k)))

    for k in range(1, z.ny):
        g2a_copy(k, on_y(z.ny - k)).wait_recv()
    for k in order:
        start(g1a_copy(k, x))
    for k in range(1, z.nx):
        g2b_copy(k, on_x(z.nx - k)).wait_recv()
    for k in order:
        start(g1b_copy(k, y))

    def gc_copy(i, core):
        place = wf.at[core * hg + i]
        return copy("gc", place, place, i, i, at(cc=other))

    last = lax.broadcasted_iota(jnp.int32, (z.cap, z.cap), 1) >= z.most

    def force_of(groups):
        found = []
        for g in groups:
            held = wf[g].astype(F32).reshape(z.blocks, 2, 8, z.cap)
            to_self, to_cross = held[:, 0].reshape(z.cap, z.cap), held[:, 1].reshape(z.cap, z.cap)
            pulls = jnp.sum(jnp.where(last, to_self, 0.0), axis=1, keepdims=True)
            loss = jnp.sum(jnp.where(last, to_cross, 0.0), axis=0, keepdims=True)
            weights = jnp.concatenate([to_self, to_cross], axis=1).astype(BF16)
            values = xs[g]
            pulled = values[0:z.cap].astype(F32) * pulls + jnp.dot(weights, values, preferred_element_type=F32)
            force = pulled / sizes[g]
            high = force.astype(BF16)
            low = (force - high.astype(F32)).astype(BF16)
            found.append((loss, high, low))
        for g, (loss, high, low) in zip(groups, found):
            rows = pl.ds(pl.multiple_of(g * z.cap, z.cap), z.cap)
            losses[g] = loss
            fs[rows, 0:z.cols] = high
            fs[rows, z.cols:2 * z.cols] = low

    for k in [0] + order:
        now = (on_x(z.nx - k), z.nx + on_y(z.ny - k))
        if k:
            g1a_copy(k, now[0]).wait_recv()
            g1b_copy(k, now[1] - z.nx).wait_recv()
        for i in now:
            start(gc_copy(i, c))
        force_of([c * hg + i for i in now])
    for k in [0] + order:
        now = (on_x(z.nx - k), z.nx + on_y(z.ny - k))
        for i in now:
            gc_copy(i, other).wait_recv()
        force_of([other * hg + i for i in now])

    def out_copies(k, source):
        return (copy("out", qs.at[k], ql.at[source], k, source, at(yy=on_y(k))),
                copy("scale", scales.at[k], landed.at[source], k, source, at(yy=on_y(k))))

    parts = z.rows // z.lanes
    square = (z.lanes, z.lanes)
    same = lax.broadcasted_iota(jnp.int32, square, 0) == lax.broadcasted_iota(jnp.int32, square, 1)

    def unsorted(k):
        rows = pl.ds(pl.multiple_of(on_y(k) * z.rows, z.rows), z.rows)
        moved = jnp.dot(back_ref[rows, :], fs[...], preferred_element_type=F32)
        return moved[:, 0:z.cols] + moved[:, z.cols:2 * z.cols]

    def send_out(step, _):
        k = lax.rem(step + z.ny // 2 - 1, z.ny - 1) + 1
        force = unsorted(k)
        top = jnp.maximum(jnp.max(jnp.abs(force), axis=1, keepdims=True), 1e-33)
        qs[k] = jnp.round(force * (32767.0 / top)).astype(jnp.int32).astype(jnp.int16)
        unit = top / 32767.0
        for part in range(parts):
            spread = jnp.where(same, unit[part * z.lanes:(part + 1) * z.lanes], 0.0)
            scales[k, part:part + 1, :] = jnp.sum(spread, axis=0, keepdims=True)
        for one in out_copies(k, y):
            one.start()
        return 0

    lax.fori_loop(0, z.ny - 1, send_out, 0)
    f_ref[:, own_cols] = unsorted(0)
    l_ref[...] = jnp.sum(jnp.sum(losses[...], axis=0), axis=1, keepdims=True) / z.samples
    drain()
    for k in order:
        source = on_y(z.ny - k)
        for one in out_copies(k, source):
            one.wait_recv()
        cols = pl.ds(pl.multiple_of(source * z.cols, z.cols), z.cols)
        for part in range(parts):
            rows = slice(part * z.lanes, (part + 1) * z.lanes)
            unit = jnp.sum(jnp.where(same, landed[source, part:part + 1, :], 0.0), axis=1, keepdims=True)
            f_ref[rows, cols] = ql[source, rows, :].astype(jnp.int32).astype(F32) * unit

    for k in range(1, z.ny):
        for one in out_copies(k, y):
            one.wait_send()


def sorted_path(z, student, teacher, bw_table, bw_index, group_ids):
    ids, count = exchanges(z)
    slots, hg = z.groups * z.cap, z.groups // 2
    quarter = z.cap // z.ny
    vmem, smem, anywhere = (pl.BlockSpec(memory_space=m) for m in (pltpu.VMEM, pltpu.SMEM, pl.ANY))
    force, loss, largest = pl.pallas_call(
        functools.partial(fused, z, ids),
        out_shape=(pltpu.VMEM((z.rows, z.tile), F32), jax.ShapeDtypeStruct((1, 1), F32),
                   jax.ShapeDtypeStruct((1, 1), jnp.int32)),
        in_specs=[anywhere, anywhere, vmem, smem, smem],
        out_specs=(vmem, vmem, vmem),
        scratch_shapes=[
            pltpu.VMEM((z.ny, z.rows, z.cols), BF16),
            pltpu.VMEM((z.ny, z.rows, z.cols), BF16),
            pltpu.VMEM((z.ny, slots, z.rows), BF16),
            pltpu.VMEM((z.samples, slots), BF16),
            pltpu.VMEM((slots, 2 * z.cols), F32),
            pltpu.VMEM((z.groups, 2 * z.cap, z.cols), BF16),
            pltpu.VMEM((z.groups, z.cap, 1), F32),
            pltpu.VMEM((z.groups, z.cap, z.cap), F32),
            pltpu.VMEM((z.groups, z.cap, z.cap), F32),
            pltpu.VMEM((hg, z.cap, z.cap), F32),
            pltpu.VMEM((hg, z.cap, z.cap), F32),
            pltpu.VMEM((z.nx, z.cap, z.cap), F32),
            pltpu.VMEM((z.nx, z.nx, quarter, z.cap), F32),
            pltpu.VMEM((z.ny, quarter, z.cap), F32),
            pltpu.VMEM((z.ny, quarter, z.cap), F32),
            pltpu.VMEM((z.cap, z.cap), F32),
            pltpu.VMEM((z.nx, quarter, z.cap), F32),
            pltpu.VMEM((z.nz, 8, z.cap), F32),
            pltpu.VMEM((z.nz, 8, z.cap), F32),
            pltpu.VMEM((z.nx, z.cap, z.cap), F32),
            pltpu.VMEM((z.ny, z.cap, z.cap), F32),
            pltpu.VMEM((2, z.cap, z.cap), F32),
            pltpu.VMEM((z.ny, quarter, z.cap), F32),
            pltpu.VMEM((z.nx, quarter, z.cap), F32),
            pltpu.VMEM((z.nz, 8, z.cap), F32),
            pltpu.VMEM((z.nz, 8, z.cap), F32),
            pltpu.VMEM((z.groups, z.blocks, 16, z.cap), BF16),
            pltpu.VMEM((1, z.samples), jnp.int32),
            pltpu.VMEM((1, z.samples), jnp.int32),
            pltpu.VMEM((z.samples, 1), jnp.int32),
            pltpu.VMEM((z.groups, 1, 1), F32),
            pltpu.VMEM((z.groups, 1, z.cap), F32),
            pltpu.VMEM((slots, 2 * z.cols), BF16),
            pltpu.VMEM((z.ny, z.rows, z.cols), jnp.int16),
            pltpu.VMEM((z.ny, z.rows, z.cols), jnp.int16),
            pltpu.VMEM((z.ny, 8, z.lanes), F32),
            pltpu.VMEM((z.ny, 8, z.lanes), F32),
            pltpu.SemaphoreType.DMA((count,)),
        ],
        compiler_params=pltpu.CompilerParams(
            collective_id=1, has_side_effects=True, vmem_limit_bytes=56 * 1024 * 1024),
        name="grouped",
    )(student, teacher, group_ids, bw_table, bw_index)
    return force, loss.reshape(()), largest.reshape(())


def gather_pair(z, block):
    y = lax.axis_index("pair")
    out = jnp.zeros((z.ny,) + block.shape, block.dtype)
    for k in range(z.ny):
        moved = lax.ppermute(block, "pair", [(i, (i + k) % z.ny) for i in range(z.ny)]) if k else block
        out = lax.dynamic_update_index_in_dim(out, moved, lax.rem(y + z.ny - k, z.ny), 0)
    return out.reshape((z.ny * block.shape[0],) + block.shape[1:])


def sum_over(array, axis, count):
    step = 1
    while step < count:
        array = array + lax.ppermute(array, axis, [(i, i ^ step) for i in range(count)])
        step *= 2
    return array


def dense_path(z, student, teacher, bw_table, bw_index, group_ids):
    students = gather_pair(z, student)
    teachers = gather_pair(z, teacher)
    both = jnp.concatenate([students, teachers], axis=0)
    wide = both.astype(F32)
    row_wide = student.astype(F32)
    norms = jnp.sum(wide * wide, axis=1)
    row_norms = jnp.sum(row_wide * row_wide, axis=1)
    gram = lax.dot_general(student, both, (((1,), (1,)), ((), ())), preferred_element_type=F32)
    part = row_norms[:, None] + norms[None, :] - 2.0 * gram
    dist = jnp.maximum(sum_over(part, "value", z.nx * z.nz * z.nc), 0.0)
    row_ids = lax.dynamic_slice_in_dim(group_ids, lax.axis_index("pair") * z.rows, z.rows)
    same = (row_ids[:, None] == group_ids[None, :]).astype(F32)
    sizes = jnp.sum(same, axis=1, keepdims=True)
    heights = bw_table[bw_index]
    weight_self, weight_cross, row_loss, pull = pair_terms(
        dist[:, :z.samples], dist[:, z.samples:], same, [heights[m] for m in range(4)], z.latent)
    loss = sum_over(jnp.broadcast_to(jnp.sum(row_loss / sizes), (8, 128)), "pair", z.ny)[0, 0] / z.samples
    pulled = row_wide * pull
    pulled = pulled + jnp.dot(weight_self, students, preferred_element_type=F32)
    pulled = pulled - jnp.dot(weight_cross, teachers, preferred_element_type=F32)
    return pulled / sizes, loss


def build(mesh, z):
    def step(student, teacher, bw_table, bw_index, group_ids):
        force, loss, largest = sorted_path(z, student, teacher, bw_table, bw_index, group_ids)
        return lax.cond(
            largest <= z.most,
            lambda *held: held[:2],
            lambda *held: dense_path(z, *held[2:]),
            force, loss, student, teacher, bw_table, bw_index, group_ids)

    return jax.shard_map(
        step, mesh=mesh,
        in_specs=(P("pair", "value"), P("pair", "value"), P(None), P(None), P(None)),
        out_specs=(P("pair", "value"), P()),
        check_vma=False)


def solution(mesh):
    return build(mesh, Sizes(ny=4, nx=4, nz=8, nc=2, samples=1536, tile=1024, latent=65536))
```

```python
import functools

import jax
import jax.numpy as jnp
from jax import lax
from jax.experimental import pallas as pl
from jax.experimental.pallas import tpu as pltpu
from jax.sharding import PartitionSpec as P

MESH = pl.DeviceIdType.MESH
F32, BF16 = jnp.float32, jnp.bfloat16


TOGETHER = 8


class Sizes:
    def __init__(self, ny, nx, nz, nc, samples, tile, latent):
        self.ny, self.nx, self.nz, self.nc = ny, nx, nz, nc
        self.samples, self.tile, self.latent = samples, tile, float(latent)
        self.rows = samples // ny
        self.cols = tile // ny
        self.groups = 2 * nc * nx
        self.half = nz // 2
        self.cap = 8 * ny * self.half
        self.blocks = self.cap // 8
        self.most = self.cap - 3
        self.lanes = min(128, self.rows)


def pair_terms(dist_self, dist_cross, mask, heights, latent):
    kern_self = jnp.zeros_like(dist_self)
    kern_cross = jnp.zeros_like(dist_cross)
    weight_self = jnp.zeros_like(dist_self)
    weight_cross = jnp.zeros_like(dist_cross)
    count = len(heights)
    for height in heights:
        width_now = height * latent
        exp_self = jnp.exp(-dist_self / width_now)
        exp_cross = jnp.exp(-dist_cross / width_now)
        kern_self = kern_self + exp_self
        kern_cross = kern_cross + exp_cross
        weight_self = weight_self + exp_self / height
        weight_cross = weight_cross + exp_cross / height
    kern_self = kern_self / count * mask
    kern_cross = kern_cross / count * mask
    weight_self = weight_self / count * mask
    weight_cross = weight_cross / count * mask
    row_loss = jnp.sum(kern_self - 2.0 * kern_cross, axis=1, keepdims=True)
    pull = jnp.sum(weight_cross, axis=1, keepdims=True) - jnp.sum(weight_self, axis=1, keepdims=True)
    return weight_self.astype(BF16), weight_cross.astype(BF16), row_loss, pull


class Pool:
    def __init__(self):
        self.total = 0

    def take(self, count):
        first = self.total
        self.total += count
        return first

    def pair(self, count):
        return self.take(count), self.take(count)


def exchanges(z):
    pool = Pool()
    sizes = {
        "in_s": z.ny, "in_t": z.ny, "core_s": z.groups // 2, "core_c": z.groups // 2, "s1a": z.nx, "s1b": z.nx, "s2a": z.ny, "s2b": z.ny, "s3": z.nz,
        "a1": z.nx, "b1": z.ny, "a2": z.ny, "b2": z.nx, "z3": z.nz,
        "gz": z.nz, "g2a": z.ny, "g2b": z.nx, "g1a": z.nx, "g1b": z.ny, "gc": z.groups // 2, "out": z.ny, "scale": z.ny, "own": 2,
    }
    return {name: pool.pair(count) for name, count in sizes.items()}, pool.total


def fused(z, ids, s_ref, t_ref, g_ref, tab_ref, idx_ref, f_ref, l_ref, most_ref,
          xin_s, xin_t, sort_ref, back_ref, xacc, xs, norms, ds_ref, dc_ref, rc_s, rc_c, r1sa, r1sb, r2sa, r2sb, sum_sa, sum_sb,
          us_ref, r3s, r1a, r1b, sums, r2a, r2b, u_ref, r3, wf, gr_ref, row_place, col_place, sizes, losses, fs, qs, ql, scales, landed, sems):
    y, v = lax.axis_index("pair"), lax.axis_index("value")
    c = lax.rem(v, z.nc)
    x = lax.rem(v // z.nc, z.nx)
    zc = v // (z.nc * z.nx)
    other = 1 - c
    hg = z.groups // 2
    quarter = z.cap // z.ny

    def at(yy=None, xx=None, zz=None, cc=None):
        yy = y if yy is None else yy
        xx = x if xx is None else xx
        zz = zc if zz is None else zz
        cc = c if cc is None else cc
        return (yy, (zz * z.nx + xx) * z.nc + cc)

    def on_y(k):
        return lax.rem(y + k, z.ny)

    def on_x(k):
        return lax.rem(x + k, z.nx)

    def on_z(k):
        return lax.rem(zc + k, z.nz)

    z_order = sorted(range(1, z.nz), key=lambda k: -min(k, z.nz - k))
    barrier = pltpu.get_barrier_semaphore()
    peers = [at(yy=on_y(k)) for k in range(1, z.ny)] + [at(xx=on_x(k)) for k in range(1, z.nx)]
    peers += [at(zz=on_z(k)) for k in range(1, z.nz)] + [at(cc=other)]
    for peer in peers:
        pl.semaphore_signal(barrier, inc=1, device_id=peer, device_id_type=MESH)
    pl.semaphore_wait(barrier, len(peers))

    def copy(name, src, dst, send, recv, device):
        first_send, first_recv = ids[name]
        return pltpu.make_async_remote_copy(
            src_ref=src, dst_ref=dst, send_sem=sems.at[first_send + send], recv_sem=sems.at[first_recv + recv],
            device_id=device, device_id_type=MESH)

    pending = []

    def drain():
        for one in pending:
            one.wait_send()

    order = sorted(range(1, z.ny), key=lambda k: min(k, z.ny - k))

    def in_copy(name, ref, land, k, source, target):
        cols = pl.ds(pl.multiple_of(target * z.cols, z.cols), z.cols)
        return copy(name, ref.at[:, cols], land.at[source], k, source, at(yy=on_y(k)))

    for k in order:
        in_copy("in_s", s_ref, xin_s, k, y, on_y(k)).start()
        pending.append(in_copy("in_t", t_ref, xin_t, k, y, on_y(k)))
    own_cols = pl.ds(pl.multiple_of(y * z.cols, z.cols), z.cols)
    own_s = pltpu.make_async_copy(s_ref.at[:, own_cols], xin_s.at[y], sems.at[ids["own"][0]])
    own_t = pltpu.make_async_copy(t_ref.at[:, own_cols], xin_t.at[y], sems.at[ids["own"][0] + 1])
    own_s.start()
    own_t.start()

    gr_ref[...] = g_ref[...].reshape(1, z.samples)
    slots = z.groups * z.cap
    eye = lax.broadcasted_iota(jnp.int32, (z.cap, z.cap), 0) == lax.broadcasted_iota(jnp.int32, (z.cap, z.cap), 1)
    above = lax.broadcasted_iota(jnp.int32, (z.cap, z.cap), 0) < lax.broadcasted_iota(jnp.int32, (z.cap, z.cap), 1)
    above = jnp.where(above, 1.0, 0.0).astype(BF16)

    def find_places(step, seen):
        first = pl.multiple_of(step * z.cap, z.cap)
        ids_row = gr_ref[:, pl.ds(first, z.cap)]
        hit = jnp.where(lax.broadcasted_iota(jnp.int32, (z.groups, z.cap), 0) == ids_row, 1.0, 0.0)
        before = seen + jnp.dot(hit.astype(BF16), above, preferred_element_type=F32)
        place = (ids_row * z.cap).astype(F32) + jnp.sum(hit * before, axis=0, keepdims=True)
        row_place[:, pl.ds(first, z.cap)] = place.astype(jnp.int32)
        turned = jnp.sum(jnp.where(eye, place, 0.0), axis=1, keepdims=True)
        col_place[pl.ds(first, z.cap), :] = turned.astype(jnp.int32)
        return seen + jnp.sum(hit, axis=1, keepdims=True)

    held = lax.fori_loop(0, z.samples // z.cap, find_places, jnp.zeros((z.groups, 1), F32))
    sizes[...] = jnp.broadcast_to(held[:, :, None], sizes.shape)
    most_ref[...] = jnp.max(held, axis=0, keepdims=True).astype(jnp.int32)

    for part in range(z.ny):
        def fill_sort(step, _):
            first = pl.multiple_of(step * z.cap, z.cap)
            slot = first + lax.broadcasted_iota(jnp.int32, (z.cap, z.rows), 0)
            place = row_place[:, part * z.rows:(part + 1) * z.rows]
            sort_ref[part, pl.ds(first, z.cap), :] = jnp.where(slot == place, 1.0, 0.0).astype(BF16)
            return 0

        lax.fori_loop(0, z.groups, fill_sort, 0)

    for k in order:
        in_copy("in_s", s_ref, xin_s, k, y, on_y(k)).wait_send()
        in_copy("in_t", t_ref, xin_t, k, y, on_y(k)).start()

    own_s.wait()
    own_t.wait()
    xacc[...] = jnp.zeros_like(xacc)
    scales[...] = jnp.zeros_like(scales)
    tall_rows = slots // 4

    def sort_from(source, values, first_col):
        def body(step, _):
            first = pl.multiple_of(step * tall_rows, tall_rows)
            place = sort_ref[source, pl.ds(first, tall_rows), :]
            xacc[pl.ds(first, tall_rows), first_col:first_col + z.cols] += jnp.dot(
                place, values[source], preferred_element_type=F32)
            return 0

        lax.fori_loop(0, 4, body, 0)

    sort_from(y, xin_s, 0)
    for k in order:
        source = on_y(z.ny - k)
        in_copy("in_s", s_ref, xin_s, k, source, on_y(k)).wait_recv()
        sort_from(source, xin_s, 0)

    def rows_of(group):
        return pl.ds(pl.multiple_of(group * z.cap, z.cap), z.cap)

    outer = (((1,), (1,)), ((), ()))

    def distances_self(groups):
        found = []
        for group in groups:
            mine = xacc[rows_of(group), 0:z.cols].astype(BF16)
            found.append((mine, lax.dot_general(mine, mine, outer, preferred_element_type=F32)))
        parts = []
        for mine, gram in found:
            diagonal = jnp.where(eye, gram, 0.0)
            norm_col = jnp.sum(diagonal, axis=1, keepdims=True)
            parts.append((norm_col, norm_col + jnp.sum(diagonal, axis=0, keepdims=True) - 2.0 * gram))
        for group, (mine, _), (norm_col, part) in zip(groups, found, parts):
            xs[group, 0:z.cap] = mine
            norms[group] = norm_col
            ds_ref[group] = part

    def distances_cross(groups):
        found = []
        for group in groups:
            theirs = xacc[rows_of(group), z.cols:2 * z.cols].astype(BF16)
            both = jnp.concatenate([xs[group, 0:z.cap], theirs], axis=0)
            found.append((theirs, lax.dot_general(both, theirs, outer, preferred_element_type=F32)))
        parts = []
        for group, (theirs, gram) in zip(groups, found):
            norm_row = jnp.sum(jnp.where(eye, gram[z.cap:2 * z.cap], 0.0), axis=0, keepdims=True)
            parts.append(norms[group] + norm_row - 2.0 * gram[0:z.cap])
        for group, (theirs, _), part in zip(groups, found, parts):
            xs[group, z.cap:2 * z.cap] = theirs
            dc_ref[group] = part

    def core_copy(name, part, land, i, group):
        return copy(name, part.at[group], land.at[i], i, i, at(cc=other))

    def quarter_of(k):
        return pl.ds(pl.multiple_of(k * quarter, quarter), quarter)

    def self_to_other(i, _):
        now = [TOGETHER * i + n for n in range(TOGETHER)]
        distances_self([other * hg + n for n in now])
        for n in now:
            core_copy("core_s", ds_ref, rc_s, n, other * hg + n).start()
        return 0

    lax.fori_loop(0, hg // TOGETHER, self_to_other, 0)

    def self_mine(i, _):
        now = [TOGETHER * i + n for n in range(TOGETHER)]
        distances_self([c * hg + n for n in now])
        for n in now:
            core_copy("core_s", ds_ref, rc_s, n, c * hg + n).wait_recv()
            ds_ref[c * hg + n] += rc_s[n]
        return 0

    lax.fori_loop(0, hg // TOGETHER, self_mine, 0)

    def s1_copies(k, source):
        second = ds_ref.at[pl.ds(c * hg + z.nx, z.nx), quarter_of(on_x(k))]
        return (copy("s1a", ds_ref.at[c * hg + on_x(k)], r1sa.at[source], k, source, at(xx=on_x(k))),
                copy("s1b", second, r1sb.at[source], k, source, at(xx=on_x(k))))

    def start(*copies):
        for one in copies:
            one.start()
            pending.append(one)

    for k in range(1, z.nx):
        start(*s1_copies(k, x))
    for i in range(hg):
        pending.append(core_copy("core_s", ds_ref, rc_s, i, other * hg + i))

    def fill_back(step, _):
        first = pl.multiple_of(step * z.cap, z.cap)
        slot = lax.broadcasted_iota(jnp.int32, (z.cap, slots), 1)
        back_ref[pl.ds(first, z.cap), :] = jnp.where(slot == col_place[pl.ds(first, z.cap), :], 1.0, 0.0).astype(BF16)
        return 0

    lax.fori_loop(0, z.samples // z.cap, fill_back, 0)

    sort_from(y, xin_t, z.cols)
    for k in order:
        source = on_y(z.ny - k)
        in_copy("in_t", t_ref, xin_t, k, source, on_y(k)).wait_recv()
        sort_from(source, xin_t, z.cols)

    def cross_to_other(i, _):
        now = [TOGETHER * i + n for n in range(TOGETHER)]
        distances_cross([other * hg + n for n in now])
        for n in now:
            core_copy("core_c", dc_ref, rc_c, n, other * hg + n).start()
        return 0

    lax.fori_loop(0, hg // TOGETHER, cross_to_other, 0)

    def a1_copy(k, source):
        return copy("a1", dc_ref.at[c * hg + on_x(k)], r1a.at[source], k, source, at(xx=on_x(k)))

    def b1_copy(k, source):
        return copy("b1", dc_ref.at[c * hg + z.nx + on_y(k)], r1b.at[source], k, source, at(yy=on_y(k)))

    def mine(k):
        now = (on_x(k), z.nx + on_y(k))
        distances_cross([c * hg + i for i in now])
        for i in now:
            core_copy("core_c", dc_ref, rc_c, i, c * hg + i).wait_recv()
            dc_ref[c * hg + i] += rc_c[i]

        if k < z.nx:
            a1_copy(k, x).start()
            b1_copy(k, y).start()

    for k in range(1, z.nx + 1):
        mine(k)
    for i in range(hg):
        pending.append(core_copy("core_c", dc_ref, rc_c, i, other * hg + i))
    for k in range(1, z.nx):
        pending.extend([a1_copy(k, x), b1_copy(k, y)])

    total_a = ds_ref[c * hg + x]
    total_b = ds_ref[pl.ds(c * hg + z.nx, z.nx), quarter_of(x), :]
    for k in range(1, z.nx):
        source = on_x(z.nx - k)
        for one in s1_copies(k, source):
            one.wait_recv()
        total_a = total_a + r1sa[source]
        total_b = total_b + r1sb[source]
    sum_sa[...] = total_a
    sum_sb[...] = total_b

    def s2_copies(k, source):
        return (copy("s2a", sum_sa.at[quarter_of(on_y(k))], r2sa.at[source], k, source, at(yy=on_y(k))),
                copy("s2b", sum_sb.at[on_y(k)], r2sb.at[source], k, source, at(yy=on_y(k))))

    for k in range(1, z.ny):
        start(*s2_copies(k, y))
    part_a = sum_sa[quarter_of(y), :]
    part_b = sum_sb[y]
    for k in range(1, z.ny):
        source = on_y(z.ny - k)
        for one in s2_copies(k, source):
            one.wait_recv()
        part_a = part_a + r2sa[source]
        part_b = part_b + r2sb[source]
    us_ref[0:z.half] = part_a.reshape(z.half, 8, z.cap)
    us_ref[z.half:2 * z.half] = part_b.reshape(z.half, 8, z.cap)

    def s3_copy(k, source):
        return copy("s3", us_ref.at[on_z(k)], r3s.at[source], k, source, at(zz=on_z(k)))

    for k in z_order:
        start(s3_copy(k, zc))

    total_a = dc_ref[c * hg + x]
    for k in range(1, z.nx):
        source = on_x(z.nx - k)
        a1_copy(k, source).wait_recv()
        total_a = total_a + r1a[source]
    sums[0] = total_a

    def a2_copy(k, source):
        return copy("a2", sums.at[0, quarter_of(on_y(k))], r2a.at[source], k, source, at(yy=on_y(k)))

    for k in range(1, z.ny):
        start(a2_copy(k, y))
    total_b = dc_ref[c * hg + z.nx + y]
    for k in range(1, z.ny):
        source = on_y(z.ny - k)
        b1_copy(k, source).wait_recv()
        total_b = total_b + r1b[source]
    sums[1] = total_b

    def b2_copy(k, source):
        return copy("b2", sums.at[1, quarter_of(on_x(k))], r2b.at[source], k, source, at(xx=on_x(k)))

    for k in range(1, z.nx):
        start(b2_copy(k, x))

    part_a = sums[0, quarter_of(y), :]
    for k in range(1, z.ny):
        source = on_y(z.ny - k)
        a2_copy(k, source).wait_recv()
        part_a = part_a + r2a[source]
    u_ref[0:z.half] = part_a.reshape(z.half, 8, z.cap)
    part_b = sums[1, quarter_of(x), :]
    for k in range(1, z.nx):
        source = on_x(z.nx - k)
        b2_copy(k, source).wait_recv()
        part_b = part_b + r2b[source]
    u_ref[z.half:2 * z.half] = part_b.reshape(z.half, 8, z.cap)

    def z3_copy(k, source):
        return copy("z3", u_ref.at[on_z(k)], r3.at[source], k, source, at(zz=on_z(k)))

    for k in z_order:
        start(z3_copy(k, zc))
    dist_self = us_ref[zc]
    for k in range(1, z.nz):
        source = on_z(z.nz - k)
        s3_copy(k, source).wait_recv()
        dist_self = dist_self + r3s[source]
    dist_cross = u_ref[zc]
    for k in range(1, z.nz):
        source = on_z(z.nz - k)
        z3_copy(k, source).wait_recv()
        dist_cross = dist_cross + r3[source]

    way = zc // z.half
    member = (1 - way) * x + way * y
    sub = (1 - way) * y + way * x
    group = c * hg + way * z.nx + member
    block = sub * z.half + lax.rem(zc, z.half)
    size = sizes[group]
    row_at = (block * 8 + lax.broadcasted_iota(jnp.int32, (8, z.cap), 0)).astype(F32)
    col_at = lax.broadcasted_iota(jnp.int32, (8, z.cap), 1).astype(F32)
    mask = jnp.where((row_at < size) & (col_at < size), 1.0, 0.0)
    heights = [tab_ref[idx_ref[m]] for m in range(4)]
    weight_self, weight_cross, row_loss, pull = pair_terms(
        jnp.maximum(dist_self, 0.0), jnp.maximum(dist_cross, 0.0), mask, heights, z.latent)
    lanes = lax.broadcasted_iota(jnp.int32, (8, z.cap), 1)

    def with_row_term(weights, term):
        first = term.astype(BF16).astype(F32)
        second = (term - first).astype(BF16).astype(F32)
        third = term - first - second
        columns = jnp.where(lanes == z.cap - 3, first, jnp.where(lanes == z.cap - 2, second, third))
        return jnp.where(lanes < z.most, weights, columns)

    wf[group, block] = jnp.concatenate(
        [with_row_term(weight_self.astype(F32), pull), with_row_term(-weight_cross.astype(F32), row_loss / size)],
        axis=0).astype(BF16)

    def gz_copy(k, source):
        way_of = source // z.half
        group_of = c * hg + way_of * z.nx + (1 - way_of) * x + way_of * y
        block_of = ((1 - way_of) * y + way_of * x) * z.half + lax.rem(source, z.half)
        place = wf.at[group_of, block_of]
        return copy("gz", place, place, k, source, at(zz=on_z(k)))

    for k in z_order:
        start(gz_copy(k, zc))
    for k in range(1, z.nz):
        gz_copy(k, on_z(z.nz - k)).wait_recv()

    def g2a_copy(k, source):
        place = wf.at[c * hg + x, pl.ds(source * z.half, z.half)]
        return copy("g2a", place, place, k, source, at(yy=on_y(k)))

    def g2b_copy(k, source):
        place = wf.at[c * hg + z.nx + y, pl.ds(source * z.half, z.half)]
        return copy("g2b", place, place, k, source, at(xx=on_x(k)))

    for k in range(1, z.nx):
        start(g2a_copy(k, y))
        start(g2b_copy(k, x))

    def g1a_copy(k, source):
        place = wf.at[c * hg + source]
        return copy("g1a", place, place, k, source, at(xx=on_x(k)))

    def g1b_copy(k, source):
        place = wf.at[c * hg + z.nx + source]
        return copy("g1b", place, place, k, source, at(yy=on_y(k)))

    for k in range(1, z.ny):
        g2a_copy(k, on_y(z.ny - k)).wait_recv()
    for k in order:
        start(g1a_copy(k, x))
    for k in range(1, z.nx):
        g2b_copy(k, on_x(z.nx - k)).wait_recv()
    for k in order:
        start(g1b_copy(k, y))

    def gc_copy(i, core):
        place = wf.at[core * hg + i]
        return copy("gc", place, place, i, i, at(cc=other))

    last = lax.broadcasted_iota(jnp.int32, (z.cap, z.cap), 1) >= z.most

    def force_of(groups):
        found = []
        for g in groups:
            held = wf[g].astype(F32).reshape(z.blocks, 2, 8, z.cap)
            to_self, to_cross = held[:, 0].reshape(z.cap, z.cap), held[:, 1].reshape(z.cap, z.cap)
            pulls = jnp.sum(jnp.where(last, to_self, 0.0), axis=1, keepdims=True)
            loss = jnp.sum(jnp.where(last, to_cross, 0.0), axis=0, keepdims=True)
            weights = jnp.concatenate([to_self, to_cross], axis=1).astype(BF16)
            values = xs[g]
            pulled = values[0:z.cap].astype(F32) * pulls + jnp.dot(weights, values, preferred_element_type=F32)
            force = pulled / sizes[g]
            high = force.astype(BF16)
            low = (force - high.astype(F32)).astype(BF16)
            found.append((loss, high, low))
        for g, (loss, high, low) in zip(groups, found):
            rows = pl.ds(pl.multiple_of(g * z.cap, z.cap), z.cap)
            losses[g] = loss
            fs[rows, 0:z.cols] = high
            fs[rows, z.cols:2 * z.cols] = low

    for k in [0] + order:
        now = (on_x(z.nx - k), z.nx + on_y(z.ny - k))
        if k:
            g1a_copy(k, now[0]).wait_recv()
            g1b_copy(k, now[1] - z.nx).wait_recv()
        for i in now:
            start(gc_copy(i, c))
        force_of([c * hg + i for i in now])
    for k in [0] + order:
        now = (on_x(z.nx - k), z.nx + on_y(z.ny - k))
        for i in now:
            gc_copy(i, other).wait_recv()
        force_of([other * hg + i for i in now])

    def out_copies(k, source):
        return (copy("out", qs.at[k], ql.at[source], k, source, at(yy=on_y(k))),
                copy("scale", scales.at[k], landed.at[source], k, source, at(yy=on_y(k))))

    parts = z.rows // z.lanes
    square = (z.lanes, z.lanes)
    same = lax.broadcasted_iota(jnp.int32, square, 0) == lax.broadcasted_iota(jnp.int32, square, 1)

    def unsorted(k):
        rows = pl.ds(pl.multiple_of(on_y(k) * z.rows, z.rows), z.rows)
        moved = jnp.dot(back_ref[rows, :], fs[...], preferred_element_type=F32)
        return moved[:, 0:z.cols] + moved[:, z.cols:2 * z.cols]

    def send_out(step, _):
        k = lax.rem(step + z.ny // 2 - 1, z.ny - 1) + 1
        force = unsorted(k)
        top = jnp.maximum(jnp.max(jnp.abs(force), axis=1, keepdims=True), 1e-33)
        qs[k] = jnp.round(force * (32767.0 / top)).astype(jnp.int32).astype(jnp.int16)
        unit = top / 32767.0
        for part in range(parts):
            spread = jnp.where(same, unit[part * z.lanes:(part + 1) * z.lanes], 0.0)
            scales[k, part:part + 1, :] = jnp.sum(spread, axis=0, keepdims=True)
        for one in out_copies(k, y):
            one.start()
        return 0

    lax.fori_loop(0, z.ny - 1, send_out, 0)
    f_ref[:, own_cols] = unsorted(0)
    l_ref[...] = jnp.sum(jnp.sum(losses[...], axis=0), axis=1, keepdims=True) / z.samples
    drain()
    for k in order:
        source = on_y(z.ny - k)
        for one in out_copies(k, source):
            one.wait_recv()
        cols = pl.ds(pl.multiple_of(source * z.cols, z.cols), z.cols)
        for part in range(parts):
            rows = slice(part * z.lanes, (part + 1) * z.lanes)
            unit = jnp.sum(jnp.where(same, landed[source, part:part + 1, :], 0.0), axis=1, keepdims=True)
            f_ref[rows, cols] = ql[source, rows, :].astype(jnp.int32).astype(F32) * unit

    for k in range(1, z.ny):
        for one in out_copies(k, y):
            one.wait_send()


def sorted_path(z, student, teacher, bw_table, bw_index, group_ids):
    ids, count = exchanges(z)
    slots, hg = z.groups * z.cap, z.groups // 2
    quarter = z.cap // z.ny
    vmem, smem, anywhere = (pl.BlockSpec(memory_space=m) for m in (pltpu.VMEM, pltpu.SMEM, pl.ANY))
    force, loss, largest = pl.pallas_call(
        functools.partial(fused, z, ids),
        out_shape=(pltpu.VMEM((z.rows, z.tile), F32), jax.ShapeDtypeStruct((1, 1), F32),
                   jax.ShapeDtypeStruct((1, 1), jnp.int32)),
        in_specs=[anywhere, anywhere, vmem, smem, smem],
        out_specs=(vmem, vmem, vmem),
        scratch_shapes=[
            pltpu.VMEM((z.ny, z.rows, z.cols), BF16),
            pltpu.VMEM((z.ny, z.rows, z.cols), BF16),
            pltpu.VMEM((z.ny, slots, z.rows), BF16),
            pltpu.VMEM((z.samples, slots), BF16),
            pltpu.VMEM((slots, 2 * z.cols), F32),
            pltpu.VMEM((z.groups, 2 * z.cap, z.cols), BF16),
            pltpu.VMEM((z.groups, z.cap, 1), F32),
            pltpu.VMEM((z.groups, z.cap, z.cap), F32),
            pltpu.VMEM((z.groups, z.cap, z.cap), F32),
            pltpu.VMEM((hg, z.cap, z.cap), F32),
            pltpu.VMEM((hg, z.cap, z.cap), F32),
            pltpu.VMEM((z.nx, z.cap, z.cap), F32),
            pltpu.VMEM((z.nx, z.nx, quarter, z.cap), F32),
            pltpu.VMEM((z.ny, quarter, z.cap), F32),
            pltpu.VMEM((z.ny, quarter, z.cap), F32),
            pltpu.VMEM((z.cap, z.cap), F32),
            pltpu.VMEM((z.nx, quarter, z.cap), F32),
            pltpu.VMEM((z.nz, 8, z.cap), F32),
            pltpu.VMEM((z.nz, 8, z.cap), F32),
            pltpu.VMEM((z.nx, z.cap, z.cap), F32),
            pltpu.VMEM((z.ny, z.cap, z.cap), F32),
            pltpu.VMEM((2, z.cap, z.cap), F32),
            pltpu.VMEM((z.ny, quarter, z.cap), F32),
            pltpu.VMEM((z.nx, quarter, z.cap), F32),
            pltpu.VMEM((z.nz, 8, z.cap), F32),
            pltpu.VMEM((z.nz, 8, z.cap), F32),
            pltpu.VMEM((z.groups, z.blocks, 16, z.cap), BF16),
            pltpu.VMEM((1, z.samples), jnp.int32),
            pltpu.VMEM((1, z.samples), jnp.int32),
            pltpu.VMEM((z.samples, 1), jnp.int32),
            pltpu.VMEM((z.groups, 1, 1), F32),
            pltpu.VMEM((z.groups, 1, z.cap), F32),
            pltpu.VMEM((slots, 2 * z.cols), BF16),
            pltpu.VMEM((z.ny, z.rows, z.cols), jnp.int16),
            pltpu.VMEM((z.ny, z.rows, z.cols), jnp.int16),
            pltpu.VMEM((z.ny, 8, z.lanes), F32),
            pltpu.VMEM((z.ny, 8, z.lanes), F32),
            pltpu.SemaphoreType.DMA((count,)),
        ],
        compiler_params=pltpu.CompilerParams(
            collective_id=1, has_side_effects=True, vmem_limit_bytes=56 * 1024 * 1024),
        name="grouped",
    )(student, teacher, group_ids, bw_table, bw_index)
    return force, loss.reshape(()), largest.reshape(())


def gather_pair(z, block):
    y = lax.axis_index("pair")
    out = jnp.zeros((z.ny,) + block.shape, block.dtype)
    for k in range(z.ny):
        moved = lax.ppermute(block, "pair", [(i, (i + k) % z.ny) for i in range(z.ny)]) if k else block
        out = lax.dynamic_update_index_in_dim(out, moved, lax.rem(y + z.ny - k, z.ny), 0)
    return out.reshape((z.ny * block.shape[0],) + block.shape[1:])


def sum_over(array, axis, count):
    step = 1
    while step < count:
        array = array + lax.ppermute(array, axis, [(i, i ^ step) for i in range(count)])
        step *= 2
    return array


def dense_path(z, student, teacher, bw_table, bw_index, group_ids):
    students = gather_pair(z, student)
    teachers = gather_pair(z, teacher)
    both = jnp.concatenate([students, teachers], axis=0)
    wide = both.astype(F32)
    row_wide = student.astype(F32)
    norms = jnp.sum(wide * wide, axis=1)
    row_norms = jnp.sum(row_wide * row_wide, axis=1)
    gram = lax.dot_general(student, both, (((1,), (1,)), ((), ())), preferred_element_type=F32)
    part = row_norms[:, None] + norms[None, :] - 2.0 * gram
    dist = jnp.maximum(sum_over(part, "value", z.nx * z.nz * z.nc), 0.0)
    row_ids = lax.dynamic_slice_in_dim(group_ids, lax.axis_index("pair") * z.rows, z.rows)
    same = (row_ids[:, None] == group_ids[None, :]).astype(F32)
    sizes = jnp.sum(same, axis=1, keepdims=True)
    heights = bw_table[bw_index]
    weight_self, weight_cross, row_loss, pull = pair_terms(
        dist[:, :z.samples], dist[:, z.samples:], same, [heights[m] for m in range(4)], z.latent)
    loss = sum_over(jnp.broadcast_to(jnp.sum(row_loss / sizes), (8, 128)), "pair", z.ny)[0, 0] / z.samples
    pulled = row_wide * pull
    pulled = pulled + jnp.dot(weight_self, students, preferred_element_type=F32)
    pulled = pulled - jnp.dot(weight_cross, teachers, preferred_element_type=F32)
    return pulled / sizes, loss


def build(mesh, z):
    def step(student, teacher, bw_table, bw_index, group_ids):
        force, loss, largest = sorted_path(z, student, teacher, bw_table, bw_index, group_ids)
        return lax.cond(
            largest <= z.most,
            lambda *held: held[:2],
            lambda *held: dense_path(z, *held[2:]),
            force, loss, student, teacher, bw_table, bw_index, group_ids)

    return jax.shard_map(
        step, mesh=mesh,
        in_specs=(P("pair", "value"), P("pair", "value"), P(None), P(None), P(None)),
        out_specs=(P("pair", "value"), P()),
        check_vma=False)


def solution(mesh):
    return build(mesh, Sizes(ny=4, nx=4, nz=8, nc=2, samples=1536, tile=1024, latent=65536))
```
